256 devices in a mesh: seq: 16 (over z, core), tp: 16 (over y, x).
Axes of the slice: x: 4, y: 4, z: 8, core: 2. Of those that a mesh axis runs over, the one named last changes fastest.
Arguments:
- tokens: bfloat16 [8192, 4096], P('seq', 'tp'), may hold values from -60 to 60
- w_qkv: bfloat16 [4096, 3, 4096], P(None, None, 'tp'), may hold values from -0.09375 to 0.09375
- w_out: bfloat16 [4096, 4096], P('tp'), may hold values from -0.09375 to 0.09375
- rand_blocks: int32 [128, 32, 3], P('seq', 'tp'), may hold values from 0 to 127, as said below
- glob_blocks: int32 [2], replicated, may hold values from 0 to 127, as said below
- window_radius: int32 [32], P('tp'), may hold values from 0 to 1, as said below
Outputs:
- mixed: bfloat16 [8192, 4096], P('seq', 'tp')
The draws below stay inside these ranges and needn't reach their ends.
Inputs may be any that keep to these rules, and one draw needn't show every extreme that they name: `rand_blocks`: split the blocks into aligned runs of 8 blocks. For one head and the query blocks of one run, the 24 entries lie at most C = ceil(8 * 3 / 16) times in any one run, and exactly C times in some run. `glob_blocks`: the 2 ids are distinct; the last block, 127, is always one of them. `window_radius`: some head has radius 1.
All inputs are finite; a program needn't handle non-finite values.
Results may differ from the reference program's by a relative error of at most 0.033.
Values may be sent and summed in bfloat16 or wider, within the bound.
No kernel may reach another device: no remote copies, remote signals or barrier semaphores. Data moves between devices by JAX's collectives and lax.ppermute only.
A program may use at most 128 MiB of HBM per device.

```python
import jax
import jax.numpy as jnp
from jax import lax

D = 4096
H = 32
DH = 128
BLK = 64
R = 3
G = 2
TOK_DEV = 512
SEQ = 8192
NB = 128


def draw_tokens(key, part):
    values = jnp.clip(jax.random.normal(key, (SEQ, D), jnp.float32), -6.0, 6.0)
    return values.astype(jnp.bfloat16)


def draw_rand_blocks(key, part):
    local = TOK_DEV // BLK
    shards = NB // local
    entries = local * R
    raw = jax.random.randint(jax.random.fold_in(key, 13), (shards, H, entries), 0, 1 << 20)
    scores = raw * entries + jnp.arange(entries, dtype=jnp.int32)[None, None, :]
    order = jnp.argsort(scores, axis=-1, stable=True).astype(jnp.int32)
    owner = order % shards
    within = jax.random.randint(jax.random.fold_in(key, 17), (shards, H, entries), 0, local)
    blocks = owner * local + within
    return blocks.reshape(shards, H, local, R).transpose(0, 2, 1, 3).reshape(NB, H, R).astype(jnp.int32)


def draw_glob_blocks(key, part):
    others = jax.random.permutation(jax.random.fold_in(key, 11), NB - 1)[:G - 1].astype(jnp.int32)
    ids = jnp.concatenate([jnp.full((1,), NB - 1, jnp.int32), others])
    return jax.random.permutation(jax.random.fold_in(key, 19), ids).astype(jnp.int32)


def draw_window_radius(key, part):
    radius = jax.random.randint(jax.random.fold_in(key, 5), (H,), 0, 2).astype(jnp.int32)
    chosen = jax.random.permutation(jax.random.fold_in(key, 7), H)[0]
    return radius.at[chosen].set(1)


def block_levels(key, shape, split, smallest, top_value):
    def one(position, shards_of):
        draws = jax.random.uniform(jax.random.fold_in(jax.random.fold_in(key, 6), position), (shards_of,), jnp.float32, smallest / len(split), top_value / len(split))
        return jnp.repeat(jnp.exp(draws), shape[position] // shards_of).reshape((-1,) + (1,) * (len(shape) - position - 1))

    loudness = one(*split[0])
    for cut in split[1:]:
        loudness = loudness * one(*cut)
    return loudness


def normal_values(stream_key, extent, width, limit, pieces=(), held_as=jnp.bfloat16):
    gain = block_levels(stream_key, extent, pieces, -0.22, 0.18) if pieces else 1.0
    values = jax.random.normal(stream_key, extent, jnp.float32) * width * gain
    return jnp.minimum(jnp.maximum(values, -limit), limit).astype(held_as)


def setup_inputs(seed: int = 0) -> dict:
    streams_of = jax.random.split(jax.random.key(seed), 7)
    return {
        "tokens": draw_tokens(jax.random.fold_in(streams_of[6], 71), 0),
        "w_qkv": normal_values(streams_of[1], (D, 3, D), D ** -0.5, 0.09375, ((2, 16),)),
        "w_out": normal_values(streams_of[2], (D, D), D ** -0.5, 0.09375, ((0, 16),)),
        "rand_blocks": draw_rand_blocks(jax.random.fold_in(streams_of[6], 71), 0),
        "glob_blocks": draw_glob_blocks(jax.random.fold_in(streams_of[6], 71), 0),
        "window_radius": draw_window_radius(jax.random.fold_in(streams_of[6], 71), 0),
    }


big_negative = -1e30


def reference(tokens, w_qkv, w_out, rand_blocks, glob_blocks, window_radius):
    projected = jnp.dot(tokens, w_qkv.reshape(D, 3 * D), preferred_element_type=jnp.float32).astype(jnp.bfloat16)
    projected = projected.reshape(SEQ, 3, H, DH)
    query_all = projected[:, 0].transpose(1, 0, 2)
    key_all = projected[:, 1].transpose(1, 0, 2)
    value_all = projected[:, 2].transpose(1, 0, 2)
    scale = 1.0 / (DH ** 0.5)

    def one_head(operands):
        query, keys, values, randoms, radius = operands
        query_blocks = query.reshape(NB, BLK, DH)
        key_blocks = keys.reshape(NB, BLK, DH)
        value_blocks = values.reshape(NB, BLK, DH)
        block_ids = jnp.arange(NB, dtype=jnp.int32)
        offsets = jnp.arange(3, dtype=jnp.int32) - 1
        window = block_ids[:, None] + offsets[None, :]
        window_ok = (window >= 0) & (window < NB) & (jnp.abs(offsets)[None, :] <= radius)
        listed = jnp.concatenate([jnp.clip(window, 0, NB - 1), randoms, jnp.broadcast_to(glob_blocks[None, :], (NB, G))], axis=1)
        valid = jnp.concatenate([window_ok, jnp.ones((NB, R + G), dtype=bool)], axis=1)
        key_list = key_blocks[listed].astype(jnp.float32)
        value_list = value_blocks[listed].astype(jnp.float32)
        scores = jnp.einsum("nqd,nlkd->nqlk", query_blocks.astype(jnp.float32), key_list) * scale
        scores = jnp.where(valid[:, None, :, None], scores, big_negative)
        row_max = jnp.max(scores, axis=(2, 3), keepdims=True)
        probs = jnp.exp(scores - row_max)
        totals = jnp.sum(probs, axis=(2, 3))
        low = probs.astype(jnp.bfloat16).astype(jnp.float32)
        result = jnp.einsum("nqlk,nlkd->nqd", low, value_list) / totals[..., None]
        glob_query = query_blocks[glob_blocks].astype(jnp.float32)
        dense = jnp.einsum("gqd,kd->gqk", glob_query, keys.astype(jnp.float32)) * scale
        dense_max = jnp.max(dense, axis=2, keepdims=True)
        dense_probs = jnp.exp(dense - dense_max)
        dense_tot = jnp.sum(dense_probs, axis=2)
        dense_low = dense_probs.astype(jnp.bfloat16).astype(jnp.float32)
        dense_out = jnp.einsum("gqk,kd->gqd", dense_low, values.astype(jnp.float32)) / dense_tot[..., None]
        result = result.at[glob_blocks].set(dense_out)
        return result.astype(jnp.bfloat16)

    heads_out = lax.map(one_head, (query_all, key_all, value_all, rand_blocks.transpose(1, 0, 2), window_radius))
    attended = heads_out.reshape(H, SEQ, DH).transpose(1, 0, 2).reshape(SEQ, D)
    return jnp.dot(attended, w_out, preferred_element_type=jnp.float32).astype(jnp.bfloat16)
```

```python
import math

import jax
import jax.numpy as jnp
from jax import lax
from jax.experimental import pallas as pl
from jax.experimental.pallas import tpu as pltpu
from jax.sharding import Mesh, PartitionSpec as P

DH = 128
BLK = 64
NZ = 8
NXY = 4
NEG = -1e30
OFFS = (0, -1, 1, 2)
CHUNKS = 2


def shift(a, axis, step):
    n = lax.axis_size(axis)
    return lax.ppermute(a, axis, [(i, (i + step) % n) for i in range(n)])


def ring4(a, axis):
    half = a.shape[0] // 2
    low = shift(a, axis, 1)
    high = shift(a, axis, -1)
    return low, high, shift(low[:half], axis, 1), shift(high[half:], axis, -1)


def plane_gather(a):
    n = a.shape[0] // 2
    f = a.shape[1]
    out = []
    for part, first, second in ((a[:n], "x", "y"), (a[n:], "y", "x")):
        stack = jnp.concatenate([part, *ring4(part, first)], axis=0)
        out.append([stack, *ring4(stack, second)])
    return [v.reshape(-1, n, f) for group in out for v in group]


def z_ring(kv):
    f1, b1 = shift(kv, "z", 1), shift(kv, "z", -1)
    f2, b2 = shift(f1, "z", 1), shift(b1, "z", -1)
    f3, b3 = shift(f2, "z", 1), shift(b2, "z", -1)
    half = kv.shape[0] // 2
    return [kv, f1, b1, f2, b2, f3, b3, shift(f3[:half], "z", 1), shift(b3[half:], "z", -1)]


def plane_copies(n, x_refs, buf, sem):
    lo, hi = pl.ds(0, n), pl.ds(n, n)
    targets = [
        buf.at[0, :, lo], buf.at[1, :, lo], buf.at[2, :, lo], buf.at[3, pl.ds(0, 2), lo], buf.at[3, pl.ds(2, 2), lo],
        buf.at[:, 0, hi], buf.at[:, 1, hi], buf.at[:, 2, hi], buf.at[pl.ds(0, 2), 3, hi], buf.at[pl.ds(2, 2), 3, hi],
    ]
    return [pltpu.make_async_copy(src, dst, sem.at[i]) for i, (src, dst) in enumerate(zip(x_refs, targets))]


def gathered_matmul(n, groups, x_refs, w_ref, buf, w_buf, x_sem, w_sem):
    copies = plane_copies(n, x_refs, buf, x_sem)
    for copy in copies:
        copy.start()
    y = lax.axis_index("y")
    x = lax.axis_index("x")
    w_copies = []
    for iy in range(NXY):
        for ix in range(NXY):
            owner = lax.rem(y + (OFFS[iy] + NXY), NXY) * NXY + lax.rem(x + (OFFS[ix] + NXY), NXY)
            row = pl.multiple_of(owner * 256, 256)
            w_copies.append(
                pltpu.make_async_copy(w_ref.at[:, pl.ds(row, 256)], w_buf.at[iy, ix], w_sem.at[iy * NXY + ix])
            )
    for copy in w_copies:
        copy.start()
    for copy in copies:
        copy.wait()
    accs = [None] * groups
    for iy in range(NXY):
        for ix in range(NXY):
            w_copies[iy * NXY + ix].wait()
            rows = buf[iy, ix]
            for g in range(groups):
                part = jnp.dot(rows, w_buf[iy, ix, g], preferred_element_type=jnp.float32)
                accs[g] = part if accs[g] is None else accs[g] + part
    return accs


def project_kernel(n, *refs):
    x_refs, w_ref = refs[:10], refs[10]
    q_ref, kv_ref, send_ref = refs[11:14]
    buf, w_buf, x_sem, w_sem = refs[14:]
    accs = gathered_matmul(n, 3, x_refs, w_ref, buf, w_buf, x_sem, w_sem)
    first = lax.axis_index("core") == 0
    for g, acc in enumerate(accs):
        low = acc.astype(jnp.bfloat16)
        h0, h1 = low[:, :DH], low[:, DH:]
        mine = jnp.where(first, h0, h1)
        other = jnp.where(first, h1, h0)
        if g == 0:
            q_ref[...] = mine
        else:
            kv_ref[:, (g - 1) * DH : g * DH] = mine
        send_ref[:, g * DH : (g + 1) * DH] = other


ANY = pl.BlockSpec(memory_space=pl.ANY)
VMEM = pl.BlockSpec(memory_space=pltpu.VMEM)
SMEM = pl.BlockSpec(memory_space=pltpu.SMEM)
PARAMS = pltpu.CompilerParams(vmem_limit_bytes=56 * 1024 * 1024)


def project(gathered, w):
    n = gathered[0].shape[1]
    bf16 = jnp.bfloat16
    return pl.pallas_call(
        lambda *refs: project_kernel(n, *refs),
        out_shape=(
            jax.ShapeDtypeStruct((2 * n, DH), bf16),
            jax.ShapeDtypeStruct((2 * n, 2 * DH), bf16),
            jax.ShapeDtypeStruct((2 * n, 3 * DH), bf16),
        ),
        in_specs=[ANY] * 11,
        out_specs=(VMEM, VMEM, VMEM),
        scratch_shapes=[
            pltpu.VMEM((4, 4, 2 * n, 256), bf16),
            pltpu.VMEM((4, 4, 3, 256, 256), bf16),
            pltpu.SemaphoreType.DMA((10,)),
            pltpu.SemaphoreType.DMA((16,)),
        ],
        compiler_params=PARAMS,
        name="project",
    )(*gathered, w)


def output_kernel(n, *refs):
    x_refs, w_ref, o_ref = refs[:10], refs[10], refs[11]
    (acc,) = gathered_matmul(n, 1, x_refs, w_ref, *refs[12:])
    o_ref[...] = acc.astype(jnp.bfloat16)


def output(gathered, w):
    n = gathered[0].shape[1]
    bf16 = jnp.bfloat16
    return pl.pallas_call(
        lambda *refs: output_kernel(n, *refs),
        out_shape=jax.ShapeDtypeStruct((2 * n, 256), bf16),
        in_specs=[ANY] * 11,
        out_specs=VMEM,
        scratch_shapes=[
            pltpu.VMEM((4, 4, 2 * n, 256), bf16),
            pltpu.VMEM((4, 4, 1, 256, 256), bf16),
            pltpu.SemaphoreType.DMA((10,)),
            pltpu.SemaphoreType.DMA((16,)),
        ],
        compiler_params=PARAMS,
        name="output",
    )(*gathered, w)


SLOTS = (0, 7, 1, 6, 2, 5, 3)


def attend_kernel(*refs):
    rand_ref, sib_ref, glob_ref, radius_ref = refs[:4]
    q_refs = refs[4 : 4 + 2 * CHUNKS]
    kv_refs = refs[4 + 2 * CHUNKS : 4 + 11 * CHUNKS]
    o_ref = refs[4 + 11 * CHUNKS]
    kv, q_buf, sem = refs[5 + 11 * CHUNKS :]
    rows = 512 // CHUNKS
    copies = []
    for i in range(2 * CHUNKS):
        side, chunk = i // CHUNKS, i % CHUNKS
        copies.append((q_refs[i].at[:, pl.ds(0, DH)], q_buf.at[side, pl.ds(chunk * rows, rows)]))
    for chunk in range(CHUNKS):
        arrays = kv_refs[9 * chunk : 9 * chunk + 9]
        for array, slot in zip(arrays, SLOTS):
            copies.append((array, kv.at[slot, chunk]))
        copies.append((arrays[7], kv.at[4, chunk, pl.ds(0, rows)]))
        copies.append((arrays[8], kv.at[4, chunk, pl.ds(rows, rows)]))
    copies = [pltpu.make_async_copy(src, dst, sem.at[i]) for i, (src, dst) in enumerate(copies)]
    for copy in copies:
        copy.start()
    for copy in copies:
        copy.wait()

    z = lax.axis_index("z")
    core = lax.axis_index("core")
    radius = radius_ref[core]
    scale = 1.0 / math.sqrt(DH)
    per_chunk = rows // BLK

    def place(block):
        slot = lax.rem(block // 16 - z + NZ, NZ)
        side = lax.rem(block // 8 + core, 2)
        within = lax.rem(block, 8)
        row = side * rows + lax.rem(within, per_chunk) * BLK
        return slot, within // per_chunk, pl.multiple_of(row, BLK)

    def take(where, col):
        slot, chunk, row = where
        return kv[slot, chunk, pl.ds(row, BLK), col * DH : (col + 1) * DH]

    column = lax.broadcasted_iota(jnp.int32, (BLK, 8 * BLK), 1) // BLK
    nt = (((1,), (1,)), ((), ()))

    def one_block(side, j):
        block = z * 16 + lax.rem(core + side, 2) * 8 + j
        table = rand_ref if side == 0 else sib_ref
        base = (j * 2 + core) * 3
        ids = [jnp.maximum(block - 1, 0), block, jnp.minimum(block + 1, 127)]
        ids += [table[base + r] for r in range(3)] + [glob_ref[g] for g in range(2)]
        places = [place(i) for i in ids]
        keys = jnp.concatenate([take(p, 0) for p in places], axis=0)
        values = jnp.concatenate([take(p, 1) for p in places], axis=0)
        query = q_buf[side, pl.ds(pl.multiple_of(j * BLK, BLK), BLK)]
        scores = lax.dot_general(query, keys, nt, preferred_element_type=jnp.float32) * scale
        low_ok = jnp.where((radius >= 1) & (block > 0), 0, 1)
        high_ok = jnp.where((radius >= 1) & (block < 127), 0, 1)
        drop = ((column == 0) & (low_ok == 1)) | ((column == 2) & (high_ok == 1))
        scores = jnp.where(drop, NEG, scores)
        top = jnp.max(scores, axis=1, keepdims=True)
        probs = jnp.exp(scores - top)
        total = jnp.sum(probs, axis=1, keepdims=True)
        acc = jnp.dot(probs.astype(jnp.bfloat16), values, preferred_element_type=jnp.float32)
        o_ref[side, pl.ds(pl.multiple_of(j * BLK, BLK), BLK)] = (acc / total).astype(jnp.bfloat16)

    for side in range(2):

        def pair(i, carry, side=side):
            for u in range(4):
                one_block(side, i * 4 + u)
            return carry

        lax.fori_loop(0, 2, pair, 0)

    glob = [glob_ref[g] for g in range(2)]
    owned = [g // 16 == z for g in glob]

    @pl.when(owned[0] | owned[1])
    def _():
        queries = []
        for g in glob:
            row = pl.multiple_of(lax.rem(g, 8) * BLK, BLK)
            queries.append(q_buf[lax.rem(g // 8 + core, 2), pl.ds(row, BLK)])
        query = jnp.concatenate(queries, axis=0)

        def step(i, carry):
            top, total, acc = carry
            part = kv[i // CHUNKS, lax.rem(i, CHUNKS)]
            scores = lax.dot_general(query, part[:, :DH], nt, preferred_element_type=jnp.float32) * scale
            new = jnp.maximum(top, jnp.max(scores, axis=1, keepdims=True))
            factor = jnp.exp(top - new)
            probs = jnp.exp(scores - new)
            total = total * factor + jnp.sum(probs, axis=1, keepdims=True)
            acc = acc * factor + jnp.dot(probs.astype(jnp.bfloat16), part[:, DH:], preferred_element_type=jnp.float32)
            return new, total, acc

        init = (
            jnp.full((2 * BLK, 1), NEG, jnp.float32),
            jnp.zeros((2 * BLK, 1), jnp.float32),
            jnp.zeros((2 * BLK, DH), jnp.float32),
        )
        _, total, acc = lax.fori_loop(0, NZ * CHUNKS, step, init)
        result = (acc / total).astype(jnp.bfloat16)
        for k, g in enumerate(glob):

            @pl.when(owned[k])
            def _(k=k, g=g):
                row = pl.multiple_of(lax.rem(g, 8) * BLK, BLK)
                o_ref[lax.rem(g // 8 + core, 2), pl.ds(row, BLK)] = result[k * BLK : (k + 1) * BLK]


def attend(rand, sib, glob, radius, queries, rings):
    rows = 512 // CHUNKS
    n_copies = 11 * CHUNKS
    return pl.pallas_call(
        attend_kernel,
        out_shape=jax.ShapeDtypeStruct((2, 512, DH), jnp.bfloat16),
        in_specs=[SMEM] * 4 + [ANY] * (11 * CHUNKS),
        out_specs=VMEM,
        scratch_shapes=[
            pltpu.VMEM((NZ, CHUNKS, 2 * rows, 2 * DH), jnp.bfloat16),
            pltpu.VMEM((2, 512, DH), jnp.bfloat16),
            pltpu.SemaphoreType.DMA((n_copies,)),
        ],
        compiler_params=PARAMS,
        name="attend",
    )(rand, sib, glob, radius, *queries, *[a for ring in rings for a in ring])


def swap(a):
    return lax.ppermute(a, "core", [(0, 1), (1, 0)])


def body(tokens, w_qkv, w_out, rand_blocks, glob_blocks, window_radius):
    core = lax.axis_index("core")
    w = w_qkv.transpose(1, 0, 2)
    rand = rand_blocks.reshape(-1)
    sib = swap(rand)
    rows = 512 // CHUNKS
    mine, theirs, rings = [], [], []
    after = None
    for chunk in range(CHUNKS):
        part = tokens[chunk * rows : (chunk + 1) * rows]
        if after is not None:
            part, _ = lax.optimization_barrier((part, after))
        gathered = plane_gather(part)
        after = gathered[1]
        q, kv, send = project(gathered, w)
        got = swap(send)
        mine.append(q)
        theirs.append(got)
        rings.append(z_ring(jnp.concatenate([kv, got[:, DH:]], axis=0)))
    ordered = jnp.where(core == 0, w_out, jnp.concatenate([w_out[DH:], w_out[:DH]], axis=0))
    ordered = ordered.reshape(256, 16, 256).transpose(1, 0, 2)
    ordered, _ = lax.optimization_barrier((ordered, after))
    w_cols = lax.all_to_all(ordered.reshape(4096, 256), ("y", "x"), 0, 0, tiled=True)
    att = attend(rand, sib, glob_blocks, window_radius, mine + theirs, rings)
    attended = jnp.concatenate([att[0], swap(att[1])], axis=1)
    return output(plane_gather(attended), w_cols[None])


def solution(mesh):
    grid = Mesh(mesh.devices.reshape(NZ, 2, NXY, NXY), ("z", "core", "y", "x"))
    seq, tp = ("z", "core"), ("y", "x")
    return jax.shard_map(
        body,
        mesh=grid,
        in_specs=(P(seq, tp), P(None, None, tp), P(tp, None), P(seq, tp, None), P(), P(tp)),
        out_specs=P(seq, tp),
        check_vma=False,
    )
```

```python
import math

import jax
import jax.numpy as jnp
from jax import lax
from jax.experimental import pallas as pl
from jax.experimental.pallas import tpu as pltpu
from jax.sharding import Mesh, PartitionSpec as P

DH = 128
BLK = 64
NZ = 8
NXY = 4
NEG = -1e30
OFFS = (0, -1, 1, 2)


def shift(a, axis, step):
    n = lax.axis_size(axis)
    return lax.ppermute(a, axis, [(i, (i + step) % n) for i in range(n)])


def ring4(a, axis):
    half = a.shape[0] // 2
    low = shift(a, axis, 1)
    high = shift(a, axis, -1)
    return low, high, shift(low[:half], axis, 1), shift(high[half:], axis, -1)


def plane_gather(a):
    n = a.shape[0] // 2
    f = a.shape[1]
    out = []
    for part, first, second in ((a[:n], "x", "y"), (a[n:], "y", "x")):
        stack = jnp.concatenate([part, *ring4(part, first)], axis=0)
        out.append([stack, *ring4(stack, second)])
    return [v.reshape(-1, n, f) for group in out for v in group]


def z_ring(kv):
    f1, b1 = shift(kv, "z", 1), shift(kv, "z", -1)
    f2, b2 = shift(f1, "z", 1), shift(b1, "z", -1)
    f3, b3 = shift(f2, "z", 1), shift(b2, "z", -1)
    half = kv.shape[0] // 2
    return [kv, f1, b1, f2, b2, f3, b3, shift(f3[:half], "z", 1), shift(b3[half:], "z", -1)]


def plane_copies(n, x_refs, buf, sem):
    lo, hi = pl.ds(0, n), pl.ds(n, n)
    targets = [
        buf.at[0, :, lo], buf.at[1, :, lo], buf.at[2, :, lo], buf.at[3, pl.ds(0, 2), lo], buf.at[3, pl.ds(2, 2), lo],
        buf.at[:, 0, hi], buf.at[:, 1, hi], buf.at[:, 2, hi], buf.at[pl.ds(0, 2), 3, hi], buf.at[pl.ds(2, 2), 3, hi],
    ]
    return [pltpu.make_async_copy(src, dst, sem.at[i]) for i, (src, dst) in enumerate(zip(x_refs, targets))]


def gathered_matmul(n, x_refs, w_ref, acc_ref, buf, w_buf, x_sem, w_sem):
    y = lax.axis_index("y")
    x = lax.axis_index("x")

    def w_copy(iy, ix):
        oy, ox = OFFS[iy] + NXY, OFFS[ix] + NXY
        owner = lax.rem(y + oy, NXY) * NXY + lax.rem(x + ox, NXY)
        row = pl.multiple_of(owner * 256, 256)
        return pltpu.make_async_copy(
            w_ref.at[:, pl.ds(row, 256)], w_buf.at[iy, :, pl.ds(ix * 256, 256)], w_sem.at[iy, ix]
        )

    copies = plane_copies(n, x_refs, buf, x_sem)
    for copy in copies:
        copy.start()
    for iy in range(NXY):
        for ix in range(NXY):
            w_copy(iy, ix).start()
    for copy in copies:
        copy.wait()
    for iy in range(NXY):
        for ix in range(NXY):
            w_copy(iy, ix).wait()

    def step(iy, carry):
        rows = jnp.concatenate([buf[iy, ix] for ix in range(NXY)], axis=1)
        for g in range(w_buf.shape[1]):
            cols = slice(g * 256, (g + 1) * 256)
            part = jnp.dot(rows, w_buf[iy, g], preferred_element_type=jnp.float32)
            acc_ref[:, cols] = jnp.where(iy == 0, part, acc_ref[:, cols] + part)
        return carry

    lax.fori_loop(0, NXY, step, 0)


def project_kernel(n, *refs):
    x_refs, w_ref = refs[:10], refs[10]
    mine_ref, send_ref, acc_ref = refs[11:14]
    gathered_matmul(n, x_refs, w_ref, acc_ref, *refs[14:])
    first = lax.axis_index("core") == 0
    for g in range(3):
        h0 = acc_ref[:, g * 256 : g * 256 + DH].astype(jnp.bfloat16)
        h1 = acc_ref[:, g * 256 + DH : (g + 1) * 256].astype(jnp.bfloat16)
        mine_ref[g] = jnp.where(first, h0, h1)
        send_ref[g] = jnp.where(first, h1, h0)


ANY = pl.BlockSpec(memory_space=pl.ANY)
VMEM = pl.BlockSpec(memory_space=pltpu.VMEM)
SMEM = pl.BlockSpec(memory_space=pltpu.SMEM)
PARAMS = pltpu.CompilerParams(vmem_limit_bytes=56 * 1024 * 1024)


def matmul_scratch(n, groups):
    bf16 = jnp.bfloat16
    return [
        pltpu.VMEM((2 * n, 256 * groups), jnp.float32),
        pltpu.VMEM((4, 4, 2 * n, 256), bf16),
        pltpu.VMEM((4, groups, 1024, 256), bf16),
        pltpu.SemaphoreType.DMA((10,)),
        pltpu.SemaphoreType.DMA((4, 4)),
    ]


def project(gathered, w):
    n = gathered[0].shape[1]
    part = jax.ShapeDtypeStruct((3, 2 * n, DH), jnp.bfloat16)
    return pl.pallas_call(
        lambda *refs: project_kernel(n, *refs),
        out_shape=(part, part),
        in_specs=[ANY] * 11,
        out_specs=(VMEM, VMEM),
        scratch_shapes=matmul_scratch(n, 3),
        compiler_params=PARAMS,
        name="project",
    )(*gathered, w)


def output_kernel(n, *refs):
    x_refs, w_ref, o_ref, acc_ref = refs[:10], refs[10], refs[11], refs[12]
    gathered_matmul(n, x_refs, w_ref, acc_ref, *refs[13:])
    o_ref[...] = acc_ref[...].astype(jnp.bfloat16)


def output(gathered, w):
    n = gathered[0].shape[1]
    return pl.pallas_call(
        lambda *refs: output_kernel(n, *refs),
        out_shape=jax.ShapeDtypeStruct((2 * n, 256), jnp.bfloat16),
        in_specs=[ANY] * 11,
        out_specs=VMEM,
        scratch_shapes=matmul_scratch(n, 1),
        compiler_params=PARAMS,
        name="output",
    )(*gathered, w)


SLOTS = (0, 7, 1, 6, 2, 5, 3)


def attend_kernel(*refs):
    rand_ref, glob_ref, radius_ref, mine_ref, theirs_ref = refs[:5]
    k_refs, v_refs = refs[5:14], refs[14:23]
    o_ref, k_buf, v_buf, q_buf, sem = refs[23:]
    copies = [(mine_ref.at[0], q_buf.at[0]), (theirs_ref.at[0], q_buf.at[1])]
    for arrays, buf in ((k_refs, k_buf), (v_refs, v_buf)):
        for array, slot in zip(arrays, SLOTS):
            copies.append((array, buf.at[slot]))
        copies.append((arrays[7], buf.at[4, pl.ds(0, 512)]))
        copies.append((arrays[8], buf.at[4, pl.ds(512, 512)]))
    copies = [pltpu.make_async_copy(src, dst, sem.at[i]) for i, (src, dst) in enumerate(copies)]
    for copy in copies:
        copy.start()
    for copy in copies:
        copy.wait()

    z = lax.axis_index("z")
    core = lax.axis_index("core")
    radius = radius_ref[core]
    scale = 1.0 / math.sqrt(DH)

    def place(block):
        slot = lax.rem(block // 16 - z + NZ, NZ)
        side = lax.rem(block // 8 + core, 2)
        return slot, pl.multiple_of(side * 512 + lax.rem(block, 8) * BLK, BLK)

    column = lax.broadcasted_iota(jnp.int32, (BLK, 8 * BLK), 1) // BLK
    nt = (((1,), (1,)), ((), ()))

    def one_block(side, j):
        block = z * 16 + lax.rem(core + side, 2) * 8 + j
        base = side * 48 + (j * 2 + core) * 3
        ids = [jnp.maximum(block - 1, 0), block, jnp.minimum(block + 1, 127)]
        ids += [rand_ref[base + r] for r in range(3)] + [glob_ref[g] for g in range(2)]
        places = [place(i) for i in ids]
        keys = jnp.concatenate([k_buf[slot, pl.ds(row, BLK)] for slot, row in places], axis=0)
        values = jnp.concatenate([v_buf[slot, pl.ds(row, BLK)] for slot, row in places], axis=0)
        mine = pl.ds(pl.multiple_of(j * BLK, BLK), BLK)
        scores = lax.dot_general(q_buf[side, mine], keys, nt, preferred_element_type=jnp.float32) * scale
        low_off = jnp.where((radius >= 1) & (block > 0), -1, 0)
        high_off = jnp.where((radius >= 1) & (block < 127), -1, 2)
        scores = jnp.where((column == low_off) | (column == high_off), NEG, scores)
        top = jnp.max(scores, axis=1, keepdims=True)
        probs = jnp.exp(scores - top)
        total = jnp.sum(probs, axis=1, keepdims=True)
        acc = jnp.dot(probs.astype(jnp.bfloat16), values, preferred_element_type=jnp.float32)
        o_ref[side, mine] = (acc / total).astype(jnp.bfloat16)

    def four_blocks(i, carry):
        for u in range(4):
            one_block(i // 2, lax.rem(i, 2) * 4 + u)
        return carry

    lax.fori_loop(0, 4, four_blocks, 0)

    glob = [glob_ref[g] for g in range(2)]
    owned = [g // 16 == z for g in glob]

    @pl.when(owned[0] | owned[1])
    def _():
        queries = []
        for g in glob:
            row = pl.multiple_of(lax.rem(g, 8) * BLK, BLK)
            queries.append(q_buf[lax.rem(g // 8 + core, 2), pl.ds(row, BLK)])
        query = jnp.concatenate(queries, axis=0)

        def step(i, carry):
            top, total, acc = carry
            scores = lax.dot_general(query, k_buf[i], nt, preferred_element_type=jnp.float32) * scale
            new = jnp.maximum(top, jnp.max(scores, axis=1, keepdims=True))
            factor = jnp.exp(top - new)
            probs = jnp.exp(scores - new)
            total = total * factor + jnp.sum(probs, axis=1, keepdims=True)
            acc = acc * factor + jnp.dot(probs.astype(jnp.bfloat16), v_buf[i], preferred_element_type=jnp.float32)
            return new, total, acc

        init = (
            jnp.full((2 * BLK, 1), NEG, jnp.float32),
            jnp.zeros((2 * BLK, 1), jnp.float32),
            jnp.zeros((2 * BLK, DH), jnp.float32),
        )
        _, total, acc = lax.fori_loop(0, NZ, step, init)
        result = (acc / total).astype(jnp.bfloat16)
        for k, g in enumerate(glob):

            @pl.when(owned[k])
            def _(k=k, g=g):
                row = pl.multiple_of(lax.rem(g, 8) * BLK, BLK)
                o_ref[lax.rem(g // 8 + core, 2), pl.ds(row, BLK)] = result[k * BLK : (k + 1) * BLK]


def attend(rand, glob, radius, mine, theirs, keys, values):
    bf16 = jnp.bfloat16
    return pl.pallas_call(
        attend_kernel,
        out_shape=jax.ShapeDtypeStruct((2, 512, DH), bf16),
        in_specs=[SMEM] * 3 + [ANY] * 20,
        out_specs=VMEM,
        scratch_shapes=[
            pltpu.VMEM((NZ, 1024, DH), bf16),
            pltpu.VMEM((NZ, 1024, DH), bf16),
            pltpu.VMEM((2, 512, DH), bf16),
            pltpu.SemaphoreType.DMA((20,)),
        ],
        compiler_params=PARAMS,
        name="attend",
    )(rand, glob, radius, mine, theirs, *keys, *values)


def swap(a):
    return lax.ppermute(a, "core", [(0, 1), (1, 0)])


def body(tokens, w_qkv, w_out, rand_blocks, glob_blocks, window_radius):
    core = lax.axis_index("core")
    rand = rand_blocks.reshape(-1)
    rand = jnp.concatenate([rand, swap(rand)])
    ordered = jnp.where(core == 0, w_out, jnp.concatenate([w_out[DH:], w_out[:DH]], axis=0))
    ordered = ordered.reshape(256, 16, 256).transpose(1, 0, 2).reshape(4096, 256)
    mine, send = project(plane_gather(tokens), w_qkv.transpose(1, 0, 2))
    theirs = swap(send)
    keys = z_ring(jnp.concatenate([mine[1], theirs[1]], axis=0))
    values = z_ring(jnp.concatenate([mine[2], theirs[2]], axis=0))
    ordered, _ = lax.optimization_barrier((ordered, theirs))
    w_cols = lax.all_to_all(ordered, ("y", "x"), 0, 0, tiled=True)
    mine, w_cols = lax.optimization_barrier((mine, w_cols))
    att = attend(rand, glob_blocks, window_radius, mine, theirs, keys, values)
    attended = jnp.concatenate([att[0], swap(att[1])], axis=1)
    return output(plane_gather(attended), w_cols[None])


def solution(mesh):
    grid = Mesh(mesh.devices.reshape(NZ, 2, NXY, NXY), ("z", "core", "y", "x"))
    seq, tp = ("z", "core"), ("y", "x")
    return jax.shard_map(
        body,
        mesh=grid,
        in_specs=(P(seq, tp), P(None, None, tp), P(tp, None), P(seq, tp, None), P(), P(tp)),
        out_specs=P(seq, tp),
        check_vma=False,
    )
```

```python
import math

import jax
import jax.numpy as jnp
from jax import lax
from jax.experimental import pallas as pl
from jax.experimental.pallas import tpu as pltpu
from jax.sharding import Mesh, PartitionSpec as P

DH = 128
BLK = 64
NZ = 8
NXY = 4
NEG = -1e30
OFFS = (0, -1, 1, 2)


def shift(a, axis, step):
    n = lax.axis_size(axis)
    return lax.ppermute(a, axis, [(i, (i + step) % n) for i in range(n)])


def around4(a, axis):
    return [shift(a, axis, 1), shift(a, axis, -1), shift(a, axis, 2)]


def plane_matmul(a, w, finish, out_shape, name, extra=()):
    n = a.shape[0] // 2
    near, far = [], []
    for part, first, second in ((a[:n], "x", "y"), (a[n:], "y", "x")):
        stack = jnp.concatenate([part, *around4(part, first)], axis=0)
        near.append(stack)
        far.append((shift(stack, second, 1), shift(stack, second, -1)))

    def blocks(v):
        return v.reshape(-1, n, 256)

    sums = partial_matmul((0,), [[blocks(v)] for v in near], w, None, name)
    far, sums, extra = lax.optimization_barrier((far, sums, extra))
    last = []
    for (low, high), second in zip(far, "yx"):
        last.append((shift(low[: 2 * n], second, 1), shift(high[2 * n :], second, -1)))
    sums = partial_matmul((1, 2), [[blocks(v) for v in f] for f in far], w, sums, name)
    out = partial_matmul((3,), [[blocks(v) for v in f] for f in last], w, sums, name, finish, out_shape)
    return out, extra


def partial_kernel(steps, counts, n, groups, has_sums, finish, *refs):
    n_x = sum(len(c) for c in counts)
    x_refs, w_ref = refs[:n_x], refs[n_x]
    sums_ref = refs[n_x + 1] if has_sums else None
    x_buf, w_buf, acc, x_sem, w_sem, s_sem = refs[-6:]
    outs = refs[n_x + 1 + has_sums : -6]
    y = lax.axis_index("y")
    x = lax.axis_index("x")
    copies = []
    i = 0
    for half in range(2):
        at = 0
        for count in counts[half]:
            copies.append(
                pltpu.make_async_copy(x_refs[i], x_buf.at[half, pl.ds(at, count)], x_sem.at[i])
            )
            at += count
            i += 1
    for k, step in enumerate(steps):
        for half in range(2):
            for j in range(NXY):
                iy, ix = (step, j) if half == 0 else (j, step)
                owner = lax.rem(y + OFFS[iy] + NXY, NXY) * NXY + lax.rem(x + OFFS[ix] + NXY, NXY)
                row = pl.multiple_of(owner * 256, 256)
                copies.append(
                    pltpu.make_async_copy(
                        w_ref.at[:, pl.ds(row, 256)],
                        w_buf.at[2 * k + half, :, pl.ds(j * 256, 256)],
                        w_sem.at[2 * k + half, j],
                    )
                )
    if has_sums:
        copies.append(pltpu.make_async_copy(sums_ref, acc, s_sem))
    for copy in copies:
        copy.start()
    for copy in copies:
        copy.wait()
    for half in range(2):
        span = slice(half * n, (half + 1) * n)
        for k in range(len(steps)):
            rows = jnp.concatenate([x_buf[half, NXY * k + j] for j in range(NXY)], axis=1)
            for g in range(groups):
                cols = slice(g * 256, (g + 1) * 256)
                part = jnp.dot(rows, w_buf[2 * k + half, g], preferred_element_type=jnp.float32)
                if has_sums or k:
                    part = acc[span, cols] + part
                acc[span, cols] = part
    if finish is None:
        copy = pltpu.make_async_copy(acc, outs[0], s_sem)
        copy.start()
        copy.wait()
    else:
        finish(acc, *outs)


ANY = pl.BlockSpec(memory_space=pl.ANY)
VMEM = pl.BlockSpec(memory_space=pltpu.VMEM)
SMEM = pl.BlockSpec(memory_space=pltpu.SMEM)
PARAMS = pltpu.CompilerParams(vmem_limit_bytes=56 * 1024 * 1024)


def partial_matmul(steps, halves, w, sums, name, finish=None, out_shape=None):
    counts = [[v.shape[0] for v in half] for half in halves]
    xs = [v for half in halves for v in half]
    n, groups = xs[0].shape[1], w.shape[0]
    total = jax.ShapeDtypeStruct((2 * n, 256 * groups), jnp.float32)
    has_sums = sums is not None
    operands = [*xs, w] + ([sums] if has_sums else [])
    bf16 = jnp.bfloat16
    return pl.pallas_call(
        lambda *refs: partial_kernel(steps, counts, n, groups, has_sums, finish, *refs),
        out_shape=total if finish is None else out_shape,
        in_specs=[ANY] * len(operands),
        out_specs=ANY if finish is None else jax.tree.map(lambda _: VMEM, out_shape),
        scratch_shapes=[
            pltpu.VMEM((2, NXY * len(steps), n, 256), bf16),
            pltpu.VMEM((2 * len(steps), groups, 1024, 256), bf16),
            pltpu.VMEM((2 * n, 256 * groups), jnp.float32),
            pltpu.SemaphoreType.DMA((len(xs),)),
            pltpu.SemaphoreType.DMA((2 * len(steps), NXY)),
            pltpu.SemaphoreType.DMA(()),
        ],
        compiler_params=PARAMS,
        name=name + str(steps[0]),
    )(*operands)


def split_heads(acc, mine_ref, send_ref):
    first = lax.axis_index("core") == 0
    for g in range(3):
        h0 = acc[:, g * 256 : g * 256 + DH].astype(jnp.bfloat16)
        h1 = acc[:, g * 256 + DH : (g + 1) * 256].astype(jnp.bfloat16)
        mine_ref[g] = jnp.where(first, h0, h1)
        send_ref[g] = jnp.where(first, h1, h0)


def round_out(acc, o_ref):
    o_ref[...] = acc[...].astype(jnp.bfloat16)


def order_kernel(w_ref, o_ref):
    first = lax.axis_index("core") == 0
    h0, h1 = w_ref[:DH], w_ref[DH:]
    o_ref[:DH] = jnp.where(first, h0, h1)
    o_ref[DH:] = jnp.where(first, h1, h0)


def order(w_out):
    return pl.pallas_call(
        order_kernel,
        out_shape=jax.ShapeDtypeStruct((4096, 256), jnp.bfloat16),
        grid=(16,),
        in_specs=[pl.BlockSpec((256, 256), lambda t: (0, t))],
        out_specs=pl.BlockSpec((256, 256), lambda t: (t, 0)),
        name="order",
    )(w_out)


def z_ring(kv):
    f1, b1 = shift(kv, "z", 1), shift(kv, "z", -1)
    f2, b2 = shift(f1, "z", 1), shift(b1, "z", -1)
    f3, b3 = shift(f2, "z", 1), shift(b2, "z", -1)
    return [kv, f1, b1, f2, b2, f3, b3, shift(f3[0], "z", 1), shift(b3[1], "z", -1)]


SLOTS = (0, 7, 1, 6, 2, 5, 3)


def attend_kernel(*refs):
    rand_ref, glob_ref, radius_ref, mine_ref, theirs_ref = refs[:5]
    kv_refs = refs[5:14]
    o_ref, kv_buf, q_buf, sem = refs[14:]
    k_buf, v_buf = kv_buf.at[0], kv_buf.at[1]
    copies = [(mine_ref.at[0], q_buf.at[0]), (theirs_ref.at[0], q_buf.at[1])]
    copies += [(array, kv_buf.at[:, slot]) for array, slot in zip(kv_refs, SLOTS)]
    copies += [(kv_refs[7], k_buf.at[4]), (kv_refs[8], v_buf.at[4])]
    copies = [pltpu.make_async_copy(src, dst, sem.at[i]) for i, (src, dst) in enumerate(copies)]
    for copy in copies:
        copy.start()
    for copy in copies:
        copy.wait()

    z = lax.axis_index("z")
    core = lax.axis_index("core")
    radius = radius_ref[core]
    scale = 1.0 / math.sqrt(DH)

    def place(block):
        slot = lax.rem(block // 16 - z + NZ, NZ)
        side = lax.rem(block // 8 + core, 2)
        return slot, pl.multiple_of(side * 512 + lax.rem(block, 8) * BLK, BLK)

    column = lax.broadcasted_iota(jnp.int32, (BLK, 8 * BLK), 1) // BLK
    nt = (((1,), (1,)), ((), ()))

    def one_block(side, j):
        block = z * 16 + lax.rem(core + side, 2) * 8 + j
        base = lax.rem(core + side, 2) * 48 + (j * 2 + core) * 3
        ids = [jnp.maximum(block - 1, 0), block, jnp.minimum(block + 1, 127)]
        ids += [rand_ref[base + r] for r in range(3)] + [glob_ref[g] for g in range(2)]
        places = [place(i) for i in ids]
        keys = jnp.concatenate([k_buf[slot, pl.ds(row, BLK)] for slot, row in places], axis=0)
        values = jnp.concatenate([v_buf[slot, pl.ds(row, BLK)] for slot, row in places], axis=0)
        mine = pl.ds(pl.multiple_of(j * BLK, BLK), BLK)
        scores = lax.dot_general(q_buf[side, mine], keys, nt, preferred_element_type=jnp.float32) * scale
        low_off = jnp.where((radius >= 1) & (block > 0), -1, 0)
        high_off = jnp.where((radius >= 1) & (block < 127), -1, 2)
        scores = jnp.where((column == low_off) | (column == high_off), NEG, scores)
        top = jnp.max(scores, axis=1, keepdims=True)
        probs = jnp.exp(scores - top)
        total = jnp.sum(probs, axis=1, keepdims=True)
        acc = jnp.dot(probs.astype(jnp.bfloat16), values, preferred_element_type=jnp.float32)
        o_ref[side, mine] = (acc / total).astype(jnp.bfloat16)

    def four_blocks(i, carry):
        for u in range(4):
            one_block(i // 2, lax.rem(i, 2) * 4 + u)
        return carry

    lax.fori_loop(0, 4, four_blocks, 0)

    glob = [glob_ref[g] for g in range(2)]
    owned = [g // 16 == z for g in glob]

    @pl.when(owned[0] | owned[1])
    def _():
        queries = []
        for g in glob:
            row = pl.multiple_of(lax.rem(g, 8) * BLK, BLK)
            queries.append(q_buf[lax.rem(g // 8 + core, 2), pl.ds(row, BLK)])
        query = jnp.concatenate(queries, axis=0)

        def step(i, carry):
            top, total, acc = carry
            scores = lax.dot_general(query, k_buf[i], nt, preferred_element_type=jnp.float32) * scale
            new = jnp.maximum(top, jnp.max(scores, axis=1, keepdims=True))
            factor = jnp.exp(top - new)
            probs = jnp.exp(scores - new)
            total = total * factor + jnp.sum(probs, axis=1, keepdims=True)
            acc = acc * factor + jnp.dot(probs.astype(jnp.bfloat16), v_buf[i], preferred_element_type=jnp.float32)
            return new, total, acc

        init = (
            jnp.full((2 * BLK, 1), NEG, jnp.float32),
            jnp.zeros((2 * BLK, 1), jnp.float32),
            jnp.zeros((2 * BLK, DH), jnp.float32),
        )
        _, total, acc = lax.fori_loop(0, NZ, step, init)
        result = (acc / total).astype(jnp.bfloat16)
        for k, g in enumerate(glob):

            @pl.when(owned[k])
            def _(k=k, g=g):
                row = pl.multiple_of(lax.rem(g, 8) * BLK, BLK)
                o_ref[lax.rem(g // 8 + core, 2), pl.ds(row, BLK)] = result[k * BLK : (k + 1) * BLK]


def attend(rand, glob, radius, mine, theirs, ring):
    bf16 = jnp.bfloat16
    return pl.pallas_call(
        attend_kernel,
        out_shape=jax.ShapeDtypeStruct((2, 512, DH), bf16),
        in_specs=[SMEM] * 3 + [ANY] * 11,
        out_specs=VMEM,
        scratch_shapes=[
            pltpu.VMEM((2, NZ, 1024, DH), bf16),
            pltpu.VMEM((2, 512, DH), bf16),
            pltpu.SemaphoreType.DMA((11,)),
        ],
        compiler_params=PARAMS,
        name="attend",
    )(rand, glob, radius, mine, theirs, *ring)


def swap(a):
    return lax.ppermute(a, "core", [(0, 1), (1, 0)])


def body(tokens, w_qkv, w_out, rand_blocks, glob_blocks, window_radius):
    bf16 = jnp.bfloat16
    rand = lax.all_gather(rand_blocks.reshape(-1), "core", axis=0, tiled=True)
    part = jax.ShapeDtypeStruct((3, 512, DH), bf16)
    (mine, send), (ordered, rand) = plane_matmul(
        tokens, w_qkv.transpose(1, 0, 2), split_heads, (part, part), "project", (order(w_out), rand)
    )
    theirs = swap(send)
    ring = z_ring(jnp.concatenate([mine[1:], theirs[1:]], axis=1))
    ordered, _ = lax.optimization_barrier((ordered, ring[1]))
    w_cols = lax.all_to_all(ordered, ("y", "x"), 0, 0, tiled=True)
    mine, w_cols = lax.optimization_barrier((mine, w_cols))
    att = attend(rand, glob_blocks, window_radius, mine, theirs, ring)
    attended = jnp.concatenate([att[0], swap(att[1])], axis=1)
    out = jax.ShapeDtypeStruct((512, 256), bf16)
    return plane_matmul(attended, w_cols[None], round_out, out, "output")[0]


def solution(mesh):
    grid = Mesh(mesh.devices.reshape(NZ, 2, NXY, NXY), ("z", "core", "y", "x"))
    seq, tp = ("z", "core"), ("y", "x")
    return jax.shard_map(
        body,
        mesh=grid,
        in_specs=(P(seq, tp), P(None, None, tp), P(tp, None), P(seq, tp, None), P(), P(tp)),
        out_specs=P(seq, tp),
        check_vma=False,
    )
```

```python
import math

import jax
import jax.numpy as jnp
from jax import lax
from jax.experimental import pallas as pl
from jax.experimental.pallas import tpu as pltpu
from jax.sharding import Mesh, PartitionSpec as P

DH = 128
BLK = 64
NZ = 8
NXY = 4
NEG = -1e30
OFFS = (0, -1, 1, 2)


def shift(a, axis, step):
    n = lax.axis_size(axis)
    return lax.ppermute(a, axis, [(i, (i + step) % n) for i in range(n)])


def around4(a, axis):
    return [shift(a, axis, 1), shift(a, axis, -1), shift(a, axis, 2)]


def plane_matmul(a, w, finish, out_shape, name, extra=()):
    n = a.shape[0] // 2
    parts = ((a[:n], "x", "y"), (a[n:], "y", "x"))
    around = lax.optimization_barrier([around4(part, first) for part, first, _ in parts])
    near, next_to, across = [], [], []
    for (part, _, second), others in zip(parts, around):
        stack = jnp.concatenate([part, *others], axis=0)
        low, high, far = around4(stack, second)
        near.append(stack)
        next_to.append((low, high))
        across.append(far)

    def blocks(v):
        return v.reshape(-1, n, 256)

    sums = partial_matmul((0,), [[blocks(v)] for v in near], w, None, name)
    next_to, sums, extra = lax.optimization_barrier((next_to, sums, extra))
    sums = partial_matmul((1, 2), [[blocks(v) for v in f] for f in next_to], w, sums, name)
    across, sums = lax.optimization_barrier((across, sums))
    out = partial_matmul((3,), [[blocks(v)] for v in across], w, sums, name, finish, out_shape)
    return out, extra


def partial_kernel(steps, counts, n, groups, has_sums, finish, *refs):
    n_x = sum(len(c) for c in counts)
    x_refs, w_ref = refs[:n_x], refs[n_x]
    sums_ref = refs[n_x + 1] if has_sums else None
    x_buf, w_buf, acc, x_sem, w_sem, s_sem = refs[-6:]
    outs = refs[n_x + 1 + has_sums : -6]
    y = lax.axis_index("y")
    x = lax.axis_index("x")
    x_copies = []
    i = 0
    for half in range(2):
        at = 0
        for count in counts[half]:
            x_copies.append(pltpu.make_async_copy(x_refs[i], x_buf.at[half, pl.ds(at, count)], x_sem.at[i]))
            at += count
            i += 1
    n_steps = len(steps)

    def w_copy(part, j, owner):
        row = pl.multiple_of(owner * 256, 256)
        return pltpu.make_async_copy(
            w_ref.at[:, pl.ds(row, 256)], w_buf.at[part, :, pl.ds(j * 256, 256)], w_sem.at[part, j]
        )

    if has_sums:
        sums_copy = pltpu.make_async_copy(sums_ref, acc, s_sem)
        sums_copy.start()
    for half in range(2):
        for k, step in enumerate(steps):
            for j in range(NXY):
                iy, ix = (step, j) if half == 0 else (j, step)
                owner = lax.rem(y + OFFS[iy] + NXY, NXY) * NXY + lax.rem(x + OFFS[ix] + NXY, NXY)
                w_copy(half * n_steps + k, j, owner).start()
        for copy, owner_half in zip(x_copies, [h for h in range(2) for _ in counts[h]]):
            if owner_half == half:
                copy.start()
    if has_sums:
        sums_copy.wait()
    for copy in x_copies:
        copy.wait()

    def multiply(part, carry):
        half, k = part // n_steps, lax.rem(part, n_steps)
        for j in range(NXY):
            w_copy(part, j, 0).wait()
        rows = jnp.concatenate([x_buf[half, NXY * k + j] for j in range(NXY)], axis=1)
        span = pl.ds(pl.multiple_of(half * n, n), n)
        for g in range(groups):
            cols = slice(g * 256, (g + 1) * 256)
            value = jnp.dot(rows, w_buf[part, g], preferred_element_type=jnp.float32)
            if has_sums:
                value = acc[span, cols] + value
            acc[span, cols] = value
        return carry

    lax.fori_loop(0, 2 * n_steps, multiply, 0)
    if finish is None:
        copy = pltpu.make_async_copy(acc, outs[0], s_sem)
        copy.start()
        copy.wait()
    else:
        finish(acc, *outs)


ANY = pl.BlockSpec(memory_space=pl.ANY)
VMEM = pl.BlockSpec(memory_space=pltpu.VMEM)
SMEM = pl.BlockSpec(memory_space=pltpu.SMEM)
PARAMS = pltpu.CompilerParams(vmem_limit_bytes=56 * 1024 * 1024)


def partial_matmul(steps, halves, w, sums, name, finish=None, out_shape=None):
    counts = [[v.shape[0] for v in half] for half in halves]
    xs = [v for half in halves for v in half]
    n, groups = xs[0].shape[1], w.shape[0]
    total = jax.ShapeDtypeStruct((2 * n, 256 * groups), jnp.float32)
    has_sums = sums is not None
    operands = [*xs, w] + ([sums] if has_sums else [])
    bf16 = jnp.bfloat16
    return pl.pallas_call(
        lambda *refs: partial_kernel(steps, counts, n, groups, has_sums, finish, *refs),
        out_shape=total if finish is None else out_shape,
        in_specs=[ANY] * len(operands),
        out_specs=ANY if finish is None else jax.tree.map(lambda _: VMEM, out_shape),
        scratch_shapes=[
            pltpu.VMEM((2, NXY * len(steps), n, 256), bf16),
            pltpu.VMEM((2 * len(steps), groups, 1024, 256), bf16),
            pltpu.VMEM((2 * n, 256 * groups), jnp.float32),
            pltpu.SemaphoreType.DMA((len(xs),)),
            pltpu.SemaphoreType.DMA((2 * len(steps), NXY)),
            pltpu.SemaphoreType.DMA(()),
        ],
        compiler_params=PARAMS,
        name=name + str(steps[0]),
    )(*operands)


def split_heads(acc, mine_ref, send_ref):
    first = lax.axis_index("core") == 0
    for g in range(3):
        h0 = acc[:, g * 256 : g * 256 + DH].astype(jnp.bfloat16)
        h1 = acc[:, g * 256 + DH : (g + 1) * 256].astype(jnp.bfloat16)
        mine_ref[g] = jnp.where(first, h0, h1)
        send_ref[g] = jnp.where(first, h1, h0)


def round_out(acc, o_ref):
    o_ref[...] = acc[...].astype(jnp.bfloat16)


def order_kernel(w_ref, o_ref, sem):
    core = lax.axis_index("core")
    copies = []
    for h in range(2):
        row = pl.multiple_of(lax.rem(core + h, 2) * DH, DH)
        for t in range(16):
            src = w_ref.at[pl.ds(row, DH), pl.ds(t * 256, 256)]
            copies.append(pltpu.make_async_copy(src, o_ref.at[t, pl.ds(h * DH, DH)], sem.at[h, t]))
    for copy in copies:
        copy.start()
    for copy in copies:
        copy.wait()


def order(w_out):
    return pl.pallas_call(
        order_kernel,
        out_shape=jax.ShapeDtypeStruct((16, 256, 256), jnp.bfloat16),
        in_specs=[ANY],
        out_specs=ANY,
        scratch_shapes=[pltpu.SemaphoreType.DMA((2, 16))],
        name="order",
    )(w_out).reshape(4096, 256)


def z_ring(a, last):
    f1, b1 = shift(a, "z", 1), shift(a, "z", -1)
    f2, b2 = shift(f1, "z", 1), shift(b1, "z", -1)
    f3, b3 = shift(f2, "z", 1), shift(b2, "z", -1)
    return [a, f1, b1, f2, b2, f3, b3, shift(f3 if last > 0 else b3, "z", last)]


SLOTS = (0, 7, 1, 6, 2, 5, 3, 4)


def attend_kernel(*refs):
    rand_ref, glob_ref, radius_ref, mine_ref, theirs_ref = refs[:5]
    k_refs, v_refs, dense_ref = refs[5:13], refs[13:21], refs[21]
    o_ref, k_buf, v_buf, q_buf, sem = refs[22:]
    copies = [(mine_ref.at[0], q_buf.at[0]), (theirs_ref.at[0], q_buf.at[1])]
    for arrays, buf in ((k_refs, k_buf), (v_refs, v_buf)):
        copies += [(array, buf.at[slot]) for array, slot in zip(arrays, SLOTS)]
    copies = [pltpu.make_async_copy(src, dst, sem.at[i]) for i, (src, dst) in enumerate(copies)]
    for copy in copies:
        copy.start()
    for copy in copies:
        copy.wait()

    z = lax.axis_index("z")
    core = lax.axis_index("core")
    radius = radius_ref[core]
    scale = 1.0 / math.sqrt(DH)

    def place(block):
        slot = lax.rem(block // 16 - z + NZ, NZ)
        side = lax.rem(block // 8 + core, 2)
        return slot, pl.multiple_of(side * 512 + lax.rem(block, 8) * BLK, BLK)

    column = lax.broadcasted_iota(jnp.int32, (BLK, 8 * BLK), 1) // BLK
    nt = (((1,), (1,)), ((), ()))

    def one_block(side, j):
        block = z * 16 + lax.rem(core + side, 2) * 8 + j
        base = lax.rem(core + side, 2) * 48 + (j * 2 + core) * 3
        ids = [jnp.maximum(block - 1, 0), block, jnp.minimum(block + 1, 127)]
        ids += [rand_ref[base + r] for r in range(3)] + [glob_ref[g] for g in range(2)]
        places = [place(i) for i in ids]
        keys = jnp.concatenate([k_buf[slot, pl.ds(row, BLK)] for slot, row in places], axis=0)
        values = jnp.concatenate([v_buf[slot, pl.ds(row, BLK)] for slot, row in places], axis=0)
        mine = pl.ds(pl.multiple_of(j * BLK, BLK), BLK)
        scores = lax.dot_general(q_buf[side, mine], keys, nt, preferred_element_type=jnp.float32) * scale
        low_off = jnp.where((radius >= 1) & (block > 0), -1, 0)
        high_off = jnp.where((radius >= 1) & (block < 127), -1, 2)
        scores = jnp.where((column == low_off) | (column == high_off), NEG, scores)
        top = jnp.max(scores, axis=1, keepdims=True)
        probs = jnp.exp(scores - top)
        total = jnp.sum(probs, axis=1, keepdims=True)
        acc = jnp.dot(probs.astype(jnp.bfloat16), values, preferred_element_type=jnp.float32)
        o_ref[side, mine] = (acc / total).astype(jnp.bfloat16)

    def four_blocks(i, carry):
        for u in range(4):
            one_block(i // 2, lax.rem(i, 2) * 4 + u)
        return carry

    lax.fori_loop(0, 4, four_blocks, 0)

    glob, owned, rows_of = owned_globals(glob_ref)

    @pl.when(owned[0] | owned[1])
    def _():
        query = jnp.concatenate([q_buf[side, pl.ds(row, BLK)] for side, row in rows_of], axis=0)
        state = (dense_ref[0], dense_ref[1], dense_ref[2])
        _, total, acc = dense_step(query, k_buf[4], v_buf[4], state)
        result = (acc / total).astype(jnp.bfloat16)
        for k, (side, row) in enumerate(rows_of):

            @pl.when(owned[k])
            def _(k=k, side=side, row=row):
                o_ref[side, pl.ds(row, BLK)] = result[k * BLK : (k + 1) * BLK]


def owned_globals(glob_ref):
    z = lax.axis_index("z")
    core = lax.axis_index("core")
    glob = [glob_ref[g] for g in range(2)]
    rows_of = [(lax.rem(g // 8 + core, 2), pl.multiple_of(lax.rem(g, 8) * BLK, BLK)) for g in glob]
    return glob, [g // 16 == z for g in glob], rows_of


def dense_step(query, keys, values, state):
    top, total, acc = state
    scores = lax.dot_general(query, keys, (((1,), (1,)), ((), ())), preferred_element_type=jnp.float32)
    scores = scores * (1.0 / math.sqrt(DH))
    new = jnp.maximum(top, jnp.max(scores, axis=1, keepdims=True))
    factor = jnp.exp(top - new)
    probs = jnp.exp(scores - new[:, :1])
    total = total * factor + jnp.sum(probs, axis=1, keepdims=True)
    acc = acc * factor + jnp.dot(probs.astype(jnp.bfloat16), values, preferred_element_type=jnp.float32)
    return new, total, acc


def dense_kernel(*refs):
    glob_ref, mine_ref, theirs_ref = refs[:3]
    k_refs, v_refs = refs[3:10], refs[10:17]
    o_ref, k_buf, v_buf, q_buf, sem = refs[17:]
    _, owned, rows_of = owned_globals(glob_ref)

    @pl.when(owned[0] | owned[1])
    def _():
        copies = [(mine_ref.at[0], q_buf.at[0]), (theirs_ref.at[0], q_buf.at[1])]
        for arrays, buf in ((k_refs, k_buf), (v_refs, v_buf)):
            copies += [(array, buf.at[i]) for i, array in enumerate(arrays)]
        copies = [pltpu.make_async_copy(src, dst, sem.at[i]) for i, (src, dst) in enumerate(copies)]
        for copy in copies:
            copy.start()
        for copy in copies:
            copy.wait()
        query = jnp.concatenate([q_buf[side, pl.ds(row, BLK)] for side, row in rows_of], axis=0)
        shape = (2 * BLK, DH)
        init = (jnp.full(shape, NEG, jnp.float32), jnp.zeros(shape, jnp.float32), jnp.zeros(shape, jnp.float32))
        state = lax.fori_loop(0, 7, lambda i, state: dense_step(query, k_buf[i], v_buf[i], state), init)
        for i, value in enumerate(state):
            o_ref[i] = value


def dense(glob, mine, theirs, keys, values):
    bf16 = jnp.bfloat16
    return pl.pallas_call(
        dense_kernel,
        out_shape=jax.ShapeDtypeStruct((3, 2 * BLK, DH), jnp.float32),
        in_specs=[SMEM] + [ANY] * 16,
        out_specs=VMEM,
        scratch_shapes=[
            pltpu.VMEM((7, 1024, DH), bf16),
            pltpu.VMEM((7, 1024, DH), bf16),
            pltpu.VMEM((2, 512, DH), bf16),
            pltpu.SemaphoreType.DMA((16,)),
        ],
        compiler_params=PARAMS,
        name="dense",
    )(glob, mine, theirs, *keys[:7], *values[:7])


def attend(rand, glob, radius, mine, theirs, keys, values, started):
    bf16 = jnp.bfloat16
    return pl.pallas_call(
        attend_kernel,
        out_shape=jax.ShapeDtypeStruct((2, 512, DH), bf16),
        in_specs=[SMEM] * 3 + [ANY] * 18 + [VMEM],
        out_specs=VMEM,
        scratch_shapes=[
            pltpu.VMEM((NZ, 1024, DH), bf16),
            pltpu.VMEM((NZ, 1024, DH), bf16),
            pltpu.VMEM((2, 512, DH), bf16),
            pltpu.SemaphoreType.DMA((18,)),
        ],
        compiler_params=PARAMS,
        name="attend",
    )(rand, glob, radius, mine, theirs, *keys, *values, started)


def swap(a):
    return lax.ppermute(a, "core", [(0, 1), (1, 0)])


def body(tokens, w_qkv, w_out, rand_blocks, glob_blocks, window_radius):
    bf16 = jnp.bfloat16
    rand = lax.all_gather(rand_blocks.reshape(-1), "core", axis=0, tiled=True)
    part = jax.ShapeDtypeStruct((3, 512, DH), bf16)
    (mine, send), (ordered, rand) = plane_matmul(
        tokens, w_qkv.transpose(1, 0, 2), split_heads, (part, part), "project", (order(w_out), rand)
    )
    theirs = swap(send)
    keys = z_ring(jnp.concatenate([mine[1], theirs[1]], axis=0), 1)
    values = z_ring(jnp.concatenate([mine[2], theirs[2]], axis=0), -1)
    ordered, _ = lax.optimization_barrier((ordered, (keys[1:3], values[1:3])))
    w_cols = lax.all_to_all(ordered, ("y", "x"), 0, 0, tiled=True)
    started = dense(glob_blocks, mine, theirs, keys, values)
    started, w_cols = lax.optimization_barrier((started, w_cols))
    att = attend(rand, glob_blocks, window_radius, mine, theirs, keys, values, started)
    attended = jnp.concatenate([att[0], swap(att[1])], axis=1)
    out = jax.ShapeDtypeStruct((512, 256), bf16)
    return plane_matmul(attended, w_cols[None], round_out, out, "output")[0]


def solution(mesh):
    grid = Mesh(mesh.devices.reshape(NZ, 2, NXY, NXY), ("z", "core", "y", "x"))
    seq, tp = ("z", "core"), ("y", "x")
    return jax.shard_map(
        body,
        mesh=grid,
        in_specs=(P(seq, tp), P(None, None, tp), P(tp, None), P(seq, tp, None), P(), P(tp)),
        out_specs=P(seq, tp),
        check_vma=False,
    )
```

```python
import math

import jax
import jax.numpy as jnp
from jax import lax
from jax.experimental import pallas as pl
from jax.experimental.pallas import tpu as pltpu
from jax.sharding import Mesh, PartitionSpec as P

DH = 128
BLK = 64
NZ = 8
NXY = 4
NEG = -1e30
OFFS = (0, -1, 1, 2)


def shift(a, axis, step):
    n = lax.axis_size(axis)
    return lax.ppermute(a, axis, [(i, (i + step) % n) for i in range(n)])


def around4(a, axis):
    return [shift(a, axis, 1), shift(a, axis, -1), shift(a, axis, 2)]


def plane_matmul(a, w, finish, out_shape, name, extra=()):
    n = a.shape[0] // 2
    parts = ((a[:n], "x", "y"), (a[n:], "y", "x"))
    around = lax.optimization_barrier([around4(part, first) for part, first, _ in parts])
    near, next_to = [], []
    for (part, _, second), others in zip(parts, around):
        stack = jnp.concatenate([part, *others], axis=0)
        near.append(stack)
        next_to.append([shift(stack, second, 1), shift(stack, second, -1)])

    def blocks(v):
        return v.reshape(-1, n, 256)

    sums = partial_matmul((0,), [[blocks(v)] for v in near], w, None, name)
    lows = [f[0] for f in next_to]
    near, lows, sums, extra = lax.optimization_barrier((near, lows, sums, extra))
    across = [shift(v, second, 2) for v, (_, _, second) in zip(near, parts)]
    sums = partial_matmul((1, 2), [[blocks(v), blocks(f[1])] for v, f in zip(lows, next_to)], w, sums, name)
    out = partial_matmul((3,), [[blocks(v)] for v in across], w, sums, name, finish, out_shape)
    return out, extra


def partial_kernel(steps, counts, n, groups, has_sums, finish, *refs):
    n_x = sum(len(c) for c in counts)
    x_refs, w_ref = refs[:n_x], refs[n_x]
    sums_ref = refs[n_x + 1] if has_sums else None
    x_buf, w_buf, acc, x_sem, w_sem, s_sem = refs[-6:]
    outs = refs[n_x + 1 + has_sums : -6]
    y = lax.axis_index("y")
    x = lax.axis_index("x")
    x_copies = []
    i = 0
    for half in range(2):
        at = 0
        for count in counts[half]:
            x_copies.append(pltpu.make_async_copy(x_refs[i], x_buf.at[half, pl.ds(at, count)], x_sem.at[i]))
            at += count
            i += 1
    n_steps = len(steps)

    def w_copy(part, j, owner):
        row = pl.multiple_of(owner * 256, 256)
        return pltpu.make_async_copy(
            w_ref.at[:, pl.ds(row, 256)], w_buf.at[part, :, pl.ds(j * 256, 256)], w_sem.at[part, j]
        )

    if has_sums:
        sums_copy = pltpu.make_async_copy(sums_ref, acc, s_sem)
        sums_copy.start()
    for half in range(2):
        for k, step in enumerate(steps):
            for j in range(NXY):
                iy, ix = (step, j) if half == 0 else (j, step)
                owner = lax.rem(y + OFFS[iy] + NXY, NXY) * NXY + lax.rem(x + OFFS[ix] + NXY, NXY)
                w_copy(half * n_steps + k, j, owner).start()
        for copy, owner_half in zip(x_copies, [h for h in range(2) for _ in counts[h]]):
            if owner_half == half:
                copy.start()
    if has_sums:
        sums_copy.wait()
    for copy in x_copies:
        copy.wait()

    def multiply(part, carry):
        half, k = part // n_steps, lax.rem(part, n_steps)
        for j in range(NXY):
            w_copy(part, j, 0).wait()
        rows = jnp.concatenate([x_buf[half, NXY * k + j] for j in range(NXY)], axis=1)
        span = pl.ds(pl.multiple_of(half * n, n), n)
        for g in range(groups):
            cols = slice(g * 256, (g + 1) * 256)
            value = jnp.dot(rows, w_buf[part, g], preferred_element_type=jnp.float32)
            if has_sums:
                value = acc[span, cols] + value
            acc[span, cols] = value
        return carry

    lax.fori_loop(0, 2 * n_steps, multiply, 0)
    if finish is None:
        copy = pltpu.make_async_copy(acc, outs[0], s_sem)
        copy.start()
        copy.wait()
    else:
        finish(acc, *outs)


ANY = pl.BlockSpec(memory_space=pl.ANY)
VMEM = pl.BlockSpec(memory_space=pltpu.VMEM)
SMEM = pl.BlockSpec(memory_space=pltpu.SMEM)
PARAMS = pltpu.CompilerParams(vmem_limit_bytes=56 * 1024 * 1024)


def partial_matmul(steps, halves, w, sums, name, finish=None, out_shape=None):
    counts = [[v.shape[0] for v in half] for half in halves]
    xs = [v for half in halves for v in half]
    n, groups = xs[0].shape[1], w.shape[0]
    total = jax.ShapeDtypeStruct((2 * n, 256 * groups), jnp.float32)
    has_sums = sums is not None
    operands = [*xs, w] + ([sums] if has_sums else [])
    bf16 = jnp.bfloat16
    return pl.pallas_call(
        lambda *refs: partial_kernel(steps, counts, n, groups, has_sums, finish, *refs),
        out_shape=total if finish is None else out_shape,
        in_specs=[ANY] * len(operands),
        out_specs=ANY if finish is None else jax.tree.map(lambda _: VMEM, out_shape),
        scratch_shapes=[
            pltpu.VMEM((2, NXY * len(steps), n, 256), bf16),
            pltpu.VMEM((2 * len(steps), groups, 1024, 256), bf16),
            pltpu.VMEM((2 * n, 256 * groups), jnp.float32),
            pltpu.SemaphoreType.DMA((len(xs),)),
            pltpu.SemaphoreType.DMA((2 * len(steps), NXY)),
            pltpu.SemaphoreType.DMA(()),
        ],
        compiler_params=PARAMS,
        name=name + str(steps[0]),
    )(*operands)


def split_heads(acc, mine_ref, send_ref):
    first = lax.axis_index("core") == 0
    for g in range(3):
        h0 = acc[:, g * 256 : g * 256 + DH].astype(jnp.bfloat16)
        h1 = acc[:, g * 256 + DH : (g + 1) * 256].astype(jnp.bfloat16)
        mine_ref[g] = jnp.where(first, h0, h1)
        send_ref[g] = jnp.where(first, h1, h0)


def round_out(acc, o_ref):
    o_ref[...] = acc[...].astype(jnp.bfloat16)


def order_kernel(w_ref, o_ref, sem):
    core = lax.axis_index("core")
    copies = []
    for h in range(2):
        row = pl.multiple_of(lax.rem(core + h, 2) * DH, DH)
        for t in range(16):
            src = w_ref.at[pl.ds(row, DH), pl.ds(t * 256, 256)]
            copies.append(pltpu.make_async_copy(src, o_ref.at[t, pl.ds(h * DH, DH)], sem.at[h, t]))
    for copy in copies:
        copy.start()
    for copy in copies:
        copy.wait()


def order(w_out):
    return pl.pallas_call(
        order_kernel,
        out_shape=jax.ShapeDtypeStruct((16, 256, 256), jnp.bfloat16),
        in_specs=[VMEM],
        out_specs=ANY,
        scratch_shapes=[pltpu.SemaphoreType.DMA((2, 16))],
        compiler_params=PARAMS,
        name="order",
    )(w_out).reshape(4096, 256)


def z_ring(a):
    f1, b1 = shift(a, "z", 1), shift(a, "z", -1)
    f2, b2 = shift(f1, "z", 1), shift(b1, "z", -1)
    return [a, f1, b1, f2, b2, shift(f2, "z", 1), shift(b2, "z", -1)]


SLOTS = (0, 7, 1, 6, 2, 5, 3, 4)


def attend_kernel(*refs):
    rand_ref, glob_ref, radius_ref, mine_ref, theirs_ref = refs[:5]
    k_refs, v_refs, dense_ref = refs[5:13], refs[13:21], refs[21]
    o_ref, k_buf, v_buf, q_buf, sem = refs[22:]
    copies = [(mine_ref.at[0], q_buf.at[0]), (theirs_ref.at[0], q_buf.at[1])]
    for arrays, buf in ((k_refs, k_buf), (v_refs, v_buf)):
        copies += [(array, buf.at[slot]) for array, slot in zip(arrays, SLOTS)]
    copies = [pltpu.make_async_copy(src, dst, sem.at[i]) for i, (src, dst) in enumerate(copies)]
    for copy in copies:
        copy.start()
    for copy in copies:
        copy.wait()

    z = lax.axis_index("z")
    core = lax.axis_index("core")
    radius = radius_ref[core]
    scale = 1.0 / math.sqrt(DH)

    def place(block):
        slot = lax.rem(block // 16 - z + NZ, NZ)
        side = lax.rem(block // 8 + core, 2)
        return slot, pl.multiple_of(side * 512 + lax.rem(block, 8) * BLK, BLK)

    column = lax.broadcasted_iota(jnp.int32, (BLK, 8 * BLK), 1) // BLK
    nt = (((1,), (1,)), ((), ()))

    def one_block(side, j):
        block = z * 16 + lax.rem(core + side, 2) * 8 + j
        base = lax.rem(core + side, 2) * 48 + (j * 2 + core) * 3
        ids = [jnp.maximum(block - 1, 0), block, jnp.minimum(block + 1, 127)]
        ids += [rand_ref[base + r] for r in range(3)] + [glob_ref[g] for g in range(2)]
        places = [place(i) for i in ids]
        keys = jnp.concatenate([k_buf[slot, pl.ds(row, BLK)] for slot, row in places], axis=0)
        values = jnp.concatenate([v_buf[slot, pl.ds(row, BLK)] for slot, row in places], axis=0)
        mine = pl.ds(pl.multiple_of(j * BLK, BLK), BLK)
        scores = lax.dot_general(q_buf[side, mine], keys, nt, preferred_element_type=jnp.float32) * scale
        low_off = jnp.where((radius >= 1) & (block > 0), -1, 0)
        high_off = jnp.where((radius >= 1) & (block < 127), -1, 2)
        scores = jnp.where((column == low_off) | (column == high_off), NEG, scores)
        top = jnp.max(scores, axis=1, keepdims=True)
        probs = jnp.exp(scores - top)
        total = jnp.sum(probs, axis=1, keepdims=True)
        acc = jnp.dot(probs.astype(jnp.bfloat16), values, preferred_element_type=jnp.float32)
        o_ref[side, mine] = (acc / total).astype(jnp.bfloat16)

    def four_blocks(i, carry):
        for u in range(4):
            one_block(i // 2, lax.rem(i, 2) * 4 + u)
        return carry

    lax.fori_loop(0, 4, four_blocks, 0)

    glob, owned, rows_of = owned_globals(glob_ref)

    @pl.when(owned[0] | owned[1])
    def _():
        query = jnp.concatenate([q_buf[side, pl.ds(row, BLK)] for side, row in rows_of], axis=0)
        state = (dense_ref[0], dense_ref[1], dense_ref[2])
        _, total, acc = lax.fori_loop(3, 6, lambda i, state: dense_step(query, k_buf[i], v_buf[i], state), state)
        result = (acc / total).astype(jnp.bfloat16)
        for k, (side, row) in enumerate(rows_of):

            @pl.when(owned[k])
            def _(k=k, side=side, row=row):
                o_ref[side, pl.ds(row, BLK)] = result[k * BLK : (k + 1) * BLK]


def owned_globals(glob_ref):
    z = lax.axis_index("z")
    core = lax.axis_index("core")
    glob = [glob_ref[g] for g in range(2)]
    rows_of = [(lax.rem(g // 8 + core, 2), pl.multiple_of(lax.rem(g, 8) * BLK, BLK)) for g in glob]
    return glob, [g // 16 == z for g in glob], rows_of


def dense_step(query, keys, values, state):
    top, total, acc = state
    scores = lax.dot_general(query, keys, (((1,), (1,)), ((), ())), preferred_element_type=jnp.float32)
    scores = scores * (1.0 / math.sqrt(DH))
    new = jnp.maximum(top, jnp.max(scores, axis=1, keepdims=True))
    factor = jnp.exp(top - new)
    probs = jnp.exp(scores - new[:, :1])
    total = total * factor + jnp.sum(probs, axis=1, keepdims=True)
    acc = acc * factor + jnp.dot(probs.astype(jnp.bfloat16), values, preferred_element_type=jnp.float32)
    return new, total, acc


def dense_kernel(*refs):
    glob_ref, mine_ref, theirs_ref = refs[:3]
    k_refs, v_refs = refs[3:8], refs[8:13]
    o_ref, k_buf, v_buf, q_buf, sem = refs[13:]
    _, owned, rows_of = owned_globals(glob_ref)

    @pl.when(owned[0] | owned[1])
    def _():
        copies = [(mine_ref.at[0], q_buf.at[0]), (theirs_ref.at[0], q_buf.at[1])]
        for arrays, buf in ((k_refs, k_buf), (v_refs, v_buf)):
            copies += [(array, buf.at[i]) for i, array in enumerate(arrays)]
        copies = [pltpu.make_async_copy(src, dst, sem.at[i]) for i, (src, dst) in enumerate(copies)]
        for copy in copies:
            copy.start()
        for copy in copies:
            copy.wait()
        query = jnp.concatenate([q_buf[side, pl.ds(row, BLK)] for side, row in rows_of], axis=0)
        shape = (2 * BLK, DH)
        init = (jnp.full(shape, NEG, jnp.float32), jnp.zeros(shape, jnp.float32), jnp.zeros(shape, jnp.float32))
        state = lax.fori_loop(0, 5, lambda i, state: dense_step(query, k_buf[i], v_buf[i], state), init)
        for i, value in enumerate(state):
            o_ref[i] = value


def dense(glob, mine, theirs, keys, values):
    bf16 = jnp.bfloat16
    return pl.pallas_call(
        dense_kernel,
        out_shape=jax.ShapeDtypeStruct((3, 2 * BLK, DH), jnp.float32),
        in_specs=[SMEM] + [ANY] * 12,
        out_specs=VMEM,
        scratch_shapes=[
            pltpu.VMEM((5, 1024, DH), bf16),
            pltpu.VMEM((5, 1024, DH), bf16),
            pltpu.VMEM((2, 512, DH), bf16),
            pltpu.SemaphoreType.DMA((12,)),
        ],
        compiler_params=PARAMS,
        name="dense",
    )(glob, mine, theirs, *keys[:5], *values[:5])


def attend(rand, glob, radius, mine, theirs, keys, values, started):
    bf16 = jnp.bfloat16
    return pl.pallas_call(
        attend_kernel,
        out_shape=jax.ShapeDtypeStruct((2, 512, DH), bf16),
        in_specs=[SMEM] * 3 + [ANY] * 18 + [VMEM],
        out_specs=VMEM,
        scratch_shapes=[
            pltpu.VMEM((NZ, 1024, DH), bf16),
            pltpu.VMEM((NZ, 1024, DH), bf16),
            pltpu.VMEM((2, 512, DH), bf16),
            pltpu.SemaphoreType.DMA((18,)),
        ],
        compiler_params=PARAMS,
        name="attend",
    )(rand, glob, radius, mine, theirs, *keys, *values, started)


def swap(a):
    return lax.ppermute(a, "core", [(0, 1), (1, 0)])


def body(tokens, w_qkv, w_out, rand_blocks, glob_blocks, window_radius):
    bf16 = jnp.bfloat16
    part = jax.ShapeDtypeStruct((3, 512, DH), bf16)
    (mine, send), ordered = plane_matmul(
        tokens, w_qkv.transpose(1, 0, 2), split_heads, (part, part), "project", order(w_out)
    )
    theirs = swap(send)
    keys = z_ring(jnp.concatenate([mine[1], theirs[1]], axis=0))
    values = z_ring(jnp.concatenate([mine[2], theirs[2]], axis=0))
    ordered, _ = lax.optimization_barrier((ordered, send))
    rand, _ = lax.optimization_barrier((rand_blocks.reshape(-1), keys[1:3]))
    rand = lax.all_gather(rand, "core", axis=0, tiled=True)
    w_cols = lax.all_to_all(ordered, ("y", "x"), 0, 0, tiled=True)
    started = dense(glob_blocks, mine, theirs, keys, values)
    keys[5], values[6], started, rand = lax.optimization_barrier((keys[5], values[6], started, rand))
    keys.append(shift(keys[5], "z", 1))
    values.append(shift(values[6], "z", -1))
    att = attend(rand, glob_blocks, window_radius, mine, theirs, keys, values, started)
    att, w_cols = lax.optimization_barrier((att, w_cols))
    attended = jnp.concatenate([att[0], swap(att[1])], axis=1)
    out = jax.ShapeDtypeStruct((512, 256), bf16)
    return plane_matmul(attended, w_cols[None], round_out, out, "output")[0]


def solution(mesh):
    grid = Mesh(mesh.devices.reshape(NZ, 2, NXY, NXY), ("z", "core", "y", "x"))
    seq, tp = ("z", "core"), ("y", "x")
    return jax.shard_map(
        body,
        mesh=grid,
        in_specs=(P(seq, tp), P(None, None, tp), P(tp, None), P(seq, tp, None), P(), P(tp)),
        out_specs=P(seq, tp),
        check_vma=False,
    )
```

```python
import math

import jax
import jax.numpy as jnp
from jax import lax
from jax.experimental import pallas as pl
from jax.experimental.pallas import tpu as pltpu
from jax.sharding import Mesh, PartitionSpec as P

DH = 128
BLK = 64
NZ = 8
NXY = 4
NEG = -1e30
OFFS = (0, -1, 1, 2)


def shift(a, axis, step):
    n = lax.axis_size(axis)
    return lax.ppermute(a, axis, [(i, (i + step) % n) for i in range(n)])


def around4(a, axis):
    return [shift(a, axis, 1), shift(a, axis, -1), shift(a, axis, 2)]


def plane_matmul(a, w, finish, out_shape, name, more=(), extra=()):
    n = a.shape[0] // 2
    others = around4(a[n:], "y")
    by_x = lax.all_gather(a[:n], "x", axis=0, tiled=True)
    by_x, others = lax.optimization_barrier((by_x, others))
    near = [by_x, jnp.concatenate([a[n:], *others], axis=0)]
    far = [(shift(stack, second, 1), shift(stack, second, -1)) for stack, second in zip(near, "yx")]

    def blocks(v):
        return v.reshape(-1, n, 256)

    sums = partial_matmul((0,), [[blocks(v)] for v in near], w, None, name)
    far, sums, extra = lax.optimization_barrier((far, sums, extra))
    last = []
    for (low, high), second in zip(far, "yx"):
        last.append((shift(low[: 2 * n], second, 1), shift(high[2 * n :], second, -1)))
    sums = partial_matmul((1, 2), [[blocks(v) for v in f] for f in far], w, sums, name)
    out = partial_matmul((3,), [[blocks(v) for v in f] for f in last], w, sums, name, finish, out_shape, more)
    return out, extra


def partial_kernel(steps, counts, n, groups, has_sums, n_more, finish, *refs):
    n_x = sum(len(c) for c in counts)
    x_refs, w_ref = refs[:n_x], refs[n_x]
    sums_ref = refs[n_x + 1] if has_sums else None
    x_buf, w_buf, acc, x_sem, w_sem, s_sem = refs[-6:]
    more = refs[n_x + 1 + has_sums : n_x + 1 + has_sums + n_more]
    outs = refs[n_x + 1 + has_sums + n_more : -6]
    y = lax.axis_index("y")
    x = lax.axis_index("x")
    x_copies = []
    i = 0
    for half in range(2):
        at = 0
        for count in counts[half]:
            x_copies.append(pltpu.make_async_copy(x_refs[i], x_buf.at[half, pl.ds(at, count)], x_sem.at[i]))
            at += count
            i += 1
    n_steps = len(steps)

    def w_copy(part, j, owner):
        row = pl.multiple_of(owner * 256, 256)
        return pltpu.make_async_copy(
            w_ref.at[:, pl.ds(row, 256)], w_buf.at[part, :, pl.ds(j * 256, 256)], w_sem.at[part, j]
        )

    if has_sums:
        sums_copy = pltpu.make_async_copy(sums_ref, acc, s_sem)
        sums_copy.start()
    for half in range(2):
        for k, step in enumerate(steps):
            for j in range(NXY):
                if half == 0:
                    owner = lax.rem(y + OFFS[step] + NXY, NXY) * NXY + j
                else:
                    owner = lax.rem(y + OFFS[j] + NXY, NXY) * NXY + lax.rem(x + OFFS[step] + NXY, NXY)
                w_copy(half * n_steps + k, j, owner).start()
        for copy, owner_half in zip(x_copies, [h for h in range(2) for _ in counts[h]]):
            if owner_half == half:
                copy.start()
    if has_sums:
        sums_copy.wait()
    for copy in x_copies:
        copy.wait()

    def multiply(i, carry):
        part, g = i // groups, lax.rem(i, groups)
        half, k = part // n_steps, lax.rem(part, n_steps)

        @pl.when(g == 0)
        def _():
            for j in range(NXY):
                w_copy(part, j, 0).wait()

        rows = jnp.concatenate([x_buf[half, NXY * k + j] for j in range(NXY)], axis=1)
        span = pl.ds(pl.multiple_of(half * n, n), n)
        value = jnp.dot(rows, w_buf[part, g], preferred_element_type=jnp.float32)
        if has_sums:
            value = acc[g, span] + value
        acc[g, span] = value
        return carry

    lax.fori_loop(0, 2 * n_steps * groups, multiply, 0)
    if finish is None:
        copy = pltpu.make_async_copy(acc, outs[0], s_sem)
        copy.start()
        copy.wait()
    else:
        finish(acc, *more, *outs)


HBM = pl.BlockSpec(memory_space=pltpu.HBM)
VMEM = pl.BlockSpec(memory_space=pltpu.VMEM)
SMEM = pl.BlockSpec(memory_space=pltpu.SMEM)
PARAMS = pltpu.CompilerParams(vmem_limit_bytes=56 * 1024 * 1024)


def partial_matmul(steps, halves, w, sums, name, finish=None, out_shape=None, more=()):
    counts = [[v.shape[0] for v in half] for half in halves]
    xs = [v for half in halves for v in half]
    n, groups = xs[0].shape[1], w.shape[0]
    total = jax.ShapeDtypeStruct((groups, 2 * n, 256), jnp.float32)
    has_sums = sums is not None
    operands = [*xs, w] + ([sums] if has_sums else [])
    bf16 = jnp.bfloat16
    return pl.pallas_call(
        lambda *refs: partial_kernel(steps, counts, n, groups, has_sums, len(more), finish, *refs),
        out_shape=total if finish is None else out_shape,
        in_specs=[HBM] * len(operands) + [VMEM] * len(more),
        out_specs=HBM if finish is None else jax.tree.map(lambda _: VMEM, out_shape),
        scratch_shapes=[
            pltpu.VMEM((2, NXY * len(steps), n, 256), bf16),
            pltpu.VMEM((2 * len(steps), groups, 1024, 256), bf16),
            pltpu.VMEM((groups, 2 * n, 256), jnp.float32),
            pltpu.SemaphoreType.DMA((len(xs),)),
            pltpu.SemaphoreType.DMA((2 * len(steps), NXY)),
            pltpu.SemaphoreType.DMA(()),
        ],
        compiler_params=PARAMS,
        name=name + str(steps[0]),
    )(*operands, *more)


def split_heads(acc, ids_ref, mine_ref, send_ref):
    first = lax.axis_index("core") == 0
    for g in range(3):
        h0 = acc[g, :, :DH].astype(jnp.bfloat16)
        h1 = acc[g, :, DH:].astype(jnp.bfloat16)
        mine_ref[g] = jnp.where(first, h0, h1)
        send_ref[g * 512 : (g + 1) * 512] = jnp.where(first, h1, h0)
    send_ref[3 * 512 :] = ids_ref[...]


def round_out(acc, o_ref):
    o_ref[...] = acc[0].astype(jnp.bfloat16)


def order_kernel(w_ref, o_ref, sem):
    core = lax.axis_index("core")
    copies = []
    for h in range(2):
        row = pl.multiple_of(lax.rem(core + h, 2) * DH, DH)
        for t in range(16):
            src = w_ref.at[pl.ds(row, DH), pl.ds(t * 256, 256)]
            copies.append(pltpu.make_async_copy(src, o_ref.at[t, pl.ds(h * DH, DH)], sem.at[h, t]))
    for copy in copies:
        copy.start()
    for copy in copies:
        copy.wait()


def order(w_out):
    return pl.pallas_call(
        order_kernel,
        out_shape=jax.ShapeDtypeStruct((16, 256, 256), jnp.bfloat16),
        in_specs=[VMEM],
        out_specs=HBM,
        scratch_shapes=[pltpu.SemaphoreType.DMA((2, 16))],
        compiler_params=PARAMS,
        name="order",
    )(w_out).reshape(4096, 256)


def z_ring(a):
    f1, b1 = shift(a, "z", 1), shift(a, "z", -1)
    f2, b2 = shift(f1, "z", 1), shift(b1, "z", -1)
    return [a, f1, b1, f2, b2, shift(f2, "z", 1), shift(b2, "z", -1)]


SLOTS = (0, 7, 1, 6, 2, 5, 3, 4)


def attend_kernel(*refs):
    rand_ref, glob_ref, radius_ref, mine_ref, theirs_ref = refs[:5]
    k_refs, v_refs, dense_ref = refs[5:13], refs[13:21], refs[21]
    o_ref, k_buf, v_buf, q_buf, sem = refs[22:]
    copies = [(mine_ref.at[0], q_buf.at[0]), (theirs_ref.at[pl.ds(0, 512)], q_buf.at[1])]
    for arrays, buf in ((k_refs, k_buf), (v_refs, v_buf)):
        copies += [(array, buf.at[slot]) for array, slot in zip(arrays, SLOTS)]
    copies = [pltpu.make_async_copy(src, dst, sem.at[i]) for i, (src, dst) in enumerate(copies)]
    for copy in copies:
        copy.start()
    for copy in copies:
        copy.wait()

    z = lax.axis_index("z")
    core = lax.axis_index("core")
    radius = radius_ref[core]
    scale = 1.0 / math.sqrt(DH)

    def place(block):
        slot = lax.rem(block // 16 - z + NZ, NZ)
        side = lax.rem(block // 8 + core, 2)
        return slot, pl.multiple_of(side * 512 + lax.rem(block, 8) * BLK, BLK)

    column = lax.broadcasted_iota(jnp.int32, (BLK, 8 * BLK), 1) // BLK
    nt = (((1,), (1,)), ((), ()))

    def one_block(side, j):
        block = z * 16 + lax.rem(core + side, 2) * 8 + j
        base = side * 48 + (j * 2 + core) * 3
        ids = [jnp.maximum(block - 1, 0), block, jnp.minimum(block + 1, 127)]
        ids += [rand_ref[base + r] for r in range(3)] + [glob_ref[g] for g in range(2)]
        places = [place(i) for i in ids]
        keys = jnp.concatenate([k_buf[slot, pl.ds(row, BLK)] for slot, row in places], axis=0)
        values = jnp.concatenate([v_buf[slot, pl.ds(row, BLK)] for slot, row in places], axis=0)
        mine = pl.ds(pl.multiple_of(j * BLK, BLK), BLK)
        scores = lax.dot_general(q_buf[side, mine], keys, nt, preferred_element_type=jnp.float32) * scale
        low_off = jnp.where((radius >= 1) & (block > 0), -1, 0)
        high_off = jnp.where((radius >= 1) & (block < 127), -1, 2)
        scores = jnp.where((column == low_off) | (column == high_off), NEG, scores)
        top = jnp.max(scores, axis=1, keepdims=True)
        probs = jnp.exp(scores - top)
        total = jnp.sum(probs, axis=1, keepdims=True)
        acc = jnp.dot(probs.astype(jnp.bfloat16), values, preferred_element_type=jnp.float32)
        o_ref[side, mine] = (acc / total).astype(jnp.bfloat16)

    def four_blocks(i, carry):
        for u in range(4):
            one_block(i // 2, lax.rem(i, 2) * 4 + u)
        return carry

    lax.fori_loop(0, 4, four_blocks, 0)

    glob, owned, rows_of = owned_globals(glob_ref)

    @pl.when(owned[0] | owned[1])
    def _():
        query = jnp.concatenate([q_buf[side, pl.ds(row, BLK)] for side, row in rows_of], axis=0)
        state = (dense_ref[0], dense_ref[1], dense_ref[2])
        _, total, acc = lax.fori_loop(3, 6, lambda i, state: dense_step(query, k_buf[i], v_buf[i], state), state)
        result = (acc / total).astype(jnp.bfloat16)
        for k, (side, row) in enumerate(rows_of):

            @pl.when(owned[k])
            def _(k=k, side=side, row=row):
                o_ref[side, pl.ds(row, BLK)] = result[k * BLK : (k + 1) * BLK]


def owned_globals(glob_ref):
    z = lax.axis_index("z")
    core = lax.axis_index("core")
    glob = [glob_ref[g] for g in range(2)]
    rows_of = [(lax.rem(g // 8 + core, 2), pl.multiple_of(lax.rem(g, 8) * BLK, BLK)) for g in glob]
    return glob, [g // 16 == z for g in glob], rows_of


def dense_step(query, keys, values, state):
    top, total, acc = state
    scores = lax.dot_general(query, keys, (((1,), (1,)), ((), ())), preferred_element_type=jnp.float32)
    scores = scores * (1.0 / math.sqrt(DH))
    new = jnp.maximum(top, jnp.max(scores, axis=1, keepdims=True))
    factor = jnp.exp(top - new)
    probs = jnp.exp(scores - new[:, :1])
    total = total * factor + jnp.sum(probs, axis=1, keepdims=True)
    acc = acc * factor + jnp.dot(probs.astype(jnp.bfloat16), values, preferred_element_type=jnp.float32)
    return new, total, acc


def dense_kernel(*refs):
    glob_ref, mine_ref, theirs_ref = refs[:3]
    k_refs, v_refs = refs[3:8], refs[8:13]
    o_ref, k_buf, v_buf, q_buf, sem = refs[13:]
    _, owned, rows_of = owned_globals(glob_ref)

    @pl.when(owned[0] | owned[1])
    def _():
        copies = [(mine_ref.at[0], q_buf.at[0]), (theirs_ref.at[pl.ds(0, 512)], q_buf.at[1])]
        for arrays, buf in ((k_refs, k_buf), (v_refs, v_buf)):
            copies += [(array, buf.at[i]) for i, array in enumerate(arrays)]
        copies = [pltpu.make_async_copy(src, dst, sem.at[i]) for i, (src, dst) in enumerate(copies)]
        for copy in copies:
            copy.start()
        for copy in copies:
            copy.wait()
        query = jnp.concatenate([q_buf[side, pl.ds(row, BLK)] for side, row in rows_of], axis=0)
        shape = (2 * BLK, DH)
        init = (jnp.full(shape, NEG, jnp.float32), jnp.zeros(shape, jnp.float32), jnp.zeros(shape, jnp.float32))
        state = lax.fori_loop(0, 5, lambda i, state: dense_step(query, k_buf[i], v_buf[i], state), init)
        for i, value in enumerate(state):
            o_ref[i] = value


def dense(glob, mine, theirs, keys, values):
    bf16 = jnp.bfloat16
    return pl.pallas_call(
        dense_kernel,
        out_shape=jax.ShapeDtypeStruct((3, 2 * BLK, DH), jnp.float32),
        in_specs=[SMEM] + [HBM] * 12,
        out_specs=VMEM,
        scratch_shapes=[
            pltpu.VMEM((5, 1024, DH), bf16),
            pltpu.VMEM((5, 1024, DH), bf16),
            pltpu.VMEM((2, 512, DH), bf16),
            pltpu.SemaphoreType.DMA((12,)),
        ],
        compiler_params=PARAMS,
        name="dense",
    )(glob, mine, theirs, *keys[:5], *values[:5])


def attend(rand, glob, radius, mine, theirs, keys, values, started):
    bf16 = jnp.bfloat16
    return pl.pallas_call(
        attend_kernel,
        out_shape=jax.ShapeDtypeStruct((2, 512, DH), bf16),
        in_specs=[SMEM] * 3 + [HBM] * 18 + [VMEM],
        out_specs=VMEM,
        scratch_shapes=[
            pltpu.VMEM((NZ, 1024, DH), bf16),
            pltpu.VMEM((NZ, 1024, DH), bf16),
            pltpu.VMEM((2, 512, DH), bf16),
            pltpu.SemaphoreType.DMA((18,)),
        ],
        compiler_params=PARAMS,
        name="attend",
    )(rand, glob, radius, mine, theirs, *keys, *values, started)


def swap(a):
    return lax.ppermute(a, "core", [(0, 1), (1, 0)])


def body(tokens, w_qkv, w_out, rand_blocks, glob_blocks, window_radius):
    bf16 = jnp.bfloat16
    rand = rand_blocks.reshape(-1)
    ids = jnp.pad(rand.astype(bf16)[None], ((0, 15), (0, DH - 48)))
    shapes = (jax.ShapeDtypeStruct((3, 512, DH), bf16), jax.ShapeDtypeStruct((3 * 512 + 16, DH), bf16))
    (mine, send), ordered = plane_matmul(
        tokens, w_qkv.transpose(1, 0, 2), split_heads, shapes, "project", (ids,), order(w_out)
    )
    theirs = swap(send)
    keys = z_ring(jnp.concatenate([mine[1], theirs[512:1024]], axis=0))
    values = z_ring(jnp.concatenate([mine[2], theirs[1024:1536]], axis=0))
    ordered, _ = lax.optimization_barrier((ordered, send))
    ids, _ = lax.optimization_barrier((theirs[1536:], keys[1:3]))
    rand = jnp.concatenate([rand, ids[0, :48].astype(jnp.int32)])
    w_cols = lax.all_to_all(ordered, ("y", "x"), 0, 0, tiled=True)
    started = dense(glob_blocks, mine, theirs, keys, values)
    keys[5], values[6], started, rand = lax.optimization_barrier((keys[5], values[6], started, rand))
    keys.append(shift(keys[5], "z", 1))
    values.append(shift(values[6], "z", -1))
    att = attend(rand, glob_blocks, window_radius, mine, theirs, keys, values, started)
    att, w_cols = lax.optimization_barrier((att, w_cols))
    attended = jnp.concatenate([att[0], swap(att[1])], axis=1)
    out = jax.ShapeDtypeStruct((512, 256), bf16)
    return plane_matmul(attended, w_cols[None], round_out, out, "output")[0]


def solution(mesh):
    grid = Mesh(mesh.devices.reshape(NZ, 2, NXY, NXY), ("z", "core", "y", "x"))
    seq, tp = ("z", "core"), ("y", "x")
    return jax.shard_map(
        body,
        mesh=grid,
        in_specs=(P(seq, tp), P(None, None, tp), P(tp, None), P(seq, tp, None), P(), P(tp)),
        out_specs=P(seq, tp),
        check_vma=False,
    )
```

```python
import math

import jax
import jax.numpy as jnp
from jax import lax
from jax.experimental import pallas as pl
from jax.experimental.pallas import tpu as pltpu
from jax.sharding import Mesh, PartitionSpec as P

DH = 128
BLK = 64
NZ = 8
NXY = 4
NEG = -1e30
OFFS = (0, -1, 1, 2)


def shift(a, axis, step):
    n = lax.axis_size(axis)
    return lax.ppermute(a, axis, [(i, (i + step) % n) for i in range(n)])


def around4(a, axis):
    return [shift(a, axis, 1), shift(a, axis, -1), shift(a, axis, 2)]


def plane_matmul(a, w, finish, out_shape, name, more=(), extra=()):
    n = a.shape[0] // 2
    others = around4(a[n:], "y")
    by_x = lax.all_gather(a[:n], "x", axis=0, tiled=True)
    by_x, others = lax.optimization_barrier((by_x, others))
    near = [by_x, jnp.concatenate([a[n:], *others], axis=0)]
    far = [(shift(stack, second, 1), shift(stack, second, -1)) for stack, second in zip(near, "yx")]

    def blocks(v):
        return v.reshape(-1, n, 256)

    sums = partial_matmul((0,), [[blocks(v)] for v in near], w, None, name)
    far, sums, extra = lax.optimization_barrier((far, sums, extra))
    last = []
    for (low, high), second in zip(far, "yx"):
        last.append((shift(low[: 2 * n], second, 1), shift(high[2 * n :], second, -1)))
    sums = partial_matmul((1, 2), [[blocks(v) for v in f] for f in far], w, sums, name)
    out = partial_matmul((3,), [[blocks(v) for v in f] for f in last], w, sums, name, finish, out_shape, more)
    return out, extra


def partial_kernel(steps, counts, n, groups, has_sums, n_more, finish, *refs):
    n_x = sum(len(c) for c in counts)
    x_refs, w_ref = refs[:n_x], refs[n_x]
    sums_ref = refs[n_x + 1] if has_sums else None
    x_buf, w_buf, acc, x_sem, w_sem, s_sem = refs[-6:]
    more = refs[n_x + 1 + has_sums : n_x + 1 + has_sums + n_more]
    outs = refs[n_x + 1 + has_sums + n_more : -6]
    y = lax.axis_index("y")
    x = lax.axis_index("x")
    x_copies = []
    i = 0
    for half in range(2):
        at = 0
        for count in counts[half]:
            x_copies.append(pltpu.make_async_copy(x_refs[i], x_buf.at[half, pl.ds(at, count)], x_sem.at[i]))
            at += count
            i += 1
    n_steps = len(steps)

    def w_copy(part, j, owner):
        row = pl.multiple_of(owner * 256, 256)
        return pltpu.make_async_copy(
            w_ref.at[:, pl.ds(row, 256)], w_buf.at[part, :, pl.ds(j * 256, 256)], w_sem.at[part, j]
        )

    if has_sums:
        sums_copy = pltpu.make_async_copy(sums_ref, acc, s_sem)
        sums_copy.start()
    for half in range(2):
        for k, step in enumerate(steps):
            for j in range(NXY):
                if half == 0:
                    owner = lax.rem(y + OFFS[step] + NXY, NXY) * NXY + j
                else:
                    owner = lax.rem(y + OFFS[j] + NXY, NXY) * NXY + lax.rem(x + OFFS[step] + NXY, NXY)
                w_copy(half * n_steps + k, j, owner).start()
        for copy, owner_half in zip(x_copies, [h for h in range(2) for _ in counts[h]]):
            if owner_half == half:
                copy.start()
    if has_sums:
        sums_copy.wait()
    for copy in x_copies:
        copy.wait()

    def multiply(part, carry):
        half, k = part // n_steps, lax.rem(part, n_steps)
        for j in range(NXY):
            w_copy(part, j, 0).wait()
        rows = jnp.concatenate([x_buf[half, NXY * k + j] for j in range(NXY)], axis=1)
        span = pl.ds(pl.multiple_of(half * n, n), n)
        for g in range(groups):
            value = jnp.dot(rows, w_buf[part, g], preferred_element_type=jnp.float32)
            if has_sums:
                value = acc[g, span] + value
            acc[g, span] = value
        return carry

    lax.fori_loop(0, 2 * n_steps, multiply, 0)
    if finish is None:
        copy = pltpu.make_async_copy(acc, outs[0], s_sem)
        copy.start()
        copy.wait()
    else:
        finish(acc, *more, *outs)


HBM = pl.BlockSpec(memory_space=pltpu.HBM)
VMEM = pl.BlockSpec(memory_space=pltpu.VMEM)
SMEM = pl.BlockSpec(memory_space=pltpu.SMEM)
PARAMS = pltpu.CompilerParams(vmem_limit_bytes=56 * 1024 * 1024)


def partial_matmul(steps, halves, w, sums, name, finish=None, out_shape=None, more=()):
    counts = [[v.shape[0] for v in half] for half in halves]
    xs = [v for half in halves for v in half]
    n, groups = xs[0].shape[1], w.shape[0]
    total = jax.ShapeDtypeStruct((groups, 2 * n, 256), jnp.float32)
    has_sums = sums is not None
    operands = [*xs, w] + ([sums] if has_sums else [])
    bf16 = jnp.bfloat16
    return pl.pallas_call(
        lambda *refs: partial_kernel(steps, counts, n, groups, has_sums, len(more), finish, *refs),
        out_shape=total if finish is None else out_shape,
        in_specs=[HBM] * len(operands) + [VMEM] * len(more),
        out_specs=HBM if finish is None else jax.tree.map(lambda _: VMEM, out_shape),
        scratch_shapes=[
            pltpu.VMEM((2, NXY * len(steps), n, 256), bf16),
            pltpu.VMEM((2 * len(steps), groups, 1024, 256), bf16),
            pltpu.VMEM((groups, 2 * n, 256), jnp.float32),
            pltpu.SemaphoreType.DMA((len(xs),)),
            pltpu.SemaphoreType.DMA((2 * len(steps), NXY)),
            pltpu.SemaphoreType.DMA(()),
        ],
        compiler_params=PARAMS,
        name=name + str(steps[0]),
    )(*operands, *more)


def split_heads(acc, ids_ref, q_ref, kv_ref, send_q_ref, send_kv_ref):
    first = lax.axis_index("core") == 0
    for g in range(3):
        h0 = acc[g, :, :DH].astype(jnp.bfloat16)
        h1 = acc[g, :, DH:].astype(jnp.bfloat16)
        mine = jnp.where(first, h0, h1)
        other = jnp.where(first, h1, h0)
        if g == 0:
            q_ref[...] = mine
            send_q_ref[:512] = other
        else:
            kv_ref[g - 1] = mine
            send_kv_ref[g - 1] = other
    send_q_ref[512:] = ids_ref[...]


def round_out(acc, o_ref):
    o_ref[...] = acc[0].astype(jnp.bfloat16)


def order_kernel(w_ref, o_ref, sem):
    core = lax.axis_index("core")
    copies = []
    for h in range(2):
        row = pl.multiple_of(lax.rem(core + h, 2) * DH, DH)
        for t in range(16):
            src = w_ref.at[pl.ds(row, DH), pl.ds(t * 256, 256)]
            copies.append(pltpu.make_async_copy(src, o_ref.at[t, pl.ds(h * DH, DH)], sem.at[h, t]))
    for copy in copies:
        copy.start()
    for copy in copies:
        copy.wait()


def order(w_out):
    return pl.pallas_call(
        order_kernel,
        out_shape=jax.ShapeDtypeStruct((16, 256, 256), jnp.bfloat16),
        in_specs=[VMEM],
        out_specs=HBM,
        scratch_shapes=[pltpu.SemaphoreType.DMA((2, 16))],
        compiler_params=PARAMS,
        name="order",
    )(w_out).reshape(4096, 256)


def z_ring(a):
    f1, b1 = shift(a, "z", 1), shift(a, "z", -1)
    f2, b2 = shift(f1, "z", 1), shift(b1, "z", -1)
    return [a, f1, b1, f2, b2, shift(f2, "z", 1), shift(b2, "z", -1)]


SLOTS = (0, 7, 1, 6, 2, 5, 3, 4)


def attend_kernel(*refs):
    rand_ref, glob_ref, radius_ref, mine_ref, theirs_ref = refs[:5]
    rings, dense_ref = (refs[5:13], refs[13:21]), refs[21]
    o_refs = refs[22:24]
    kv_buf, q_buf, sem = refs[24:]
    copies = [(mine_ref, q_buf.at[0]), (theirs_ref.at[pl.ds(0, 512)], q_buf.at[1])]
    for side, arrays in enumerate(rings):
        copies += [(array, kv_buf.at[slot, side]) for array, slot in zip(arrays, SLOTS)]
    copies = [pltpu.make_async_copy(src, dst, sem.at[i]) for i, (src, dst) in enumerate(copies)]
    for copy in copies:
        copy.start()
    for copy in copies:
        copy.wait()

    z = lax.axis_index("z")
    core = lax.axis_index("core")
    radius = radius_ref[core]
    scale = 1.0 / math.sqrt(DH)

    def place(block):
        slot = lax.rem(block // 16 - z + NZ, NZ)
        side = lax.rem(block // 8 + core, 2)
        return slot, side, pl.multiple_of(lax.rem(block, 8) * BLK, BLK)

    column = lax.broadcasted_iota(jnp.int32, (BLK, 8 * BLK), 1) // BLK
    nt = (((1,), (1,)), ((), ()))

    def one_block(side, j):
        block = z * 16 + lax.rem(core + side, 2) * 8 + j
        base = side * 48 + (j * 2 + core) * 3
        ids = [jnp.maximum(block - 1, 0), block, jnp.minimum(block + 1, 127)]
        ids += [rand_ref[base + r] for r in range(3)] + [glob_ref[g] for g in range(2)]
        places = [place(i) for i in ids]
        keys = jnp.concatenate([kv_buf[slot, owner, 0, pl.ds(row, BLK)] for slot, owner, row in places], axis=0)
        values = jnp.concatenate([kv_buf[slot, owner, 1, pl.ds(row, BLK)] for slot, owner, row in places], axis=0)
        mine = pl.ds(pl.multiple_of(j * BLK, BLK), BLK)
        scores = lax.dot_general(q_buf[side, mine], keys, nt, preferred_element_type=jnp.float32) * scale
        low_off = jnp.where((radius >= 1) & (block > 0), -1, 0)
        high_off = jnp.where((radius >= 1) & (block < 127), -1, 2)
        scores = jnp.where((column == low_off) | (column == high_off), NEG, scores)
        top = jnp.max(scores, axis=1, keepdims=True)
        probs = jnp.exp(scores - top)
        total = jnp.sum(probs, axis=1, keepdims=True)
        acc = jnp.dot(probs.astype(jnp.bfloat16), values, preferred_element_type=jnp.float32)
        o_refs[side][mine] = (acc / total).astype(jnp.bfloat16)

    for side in range(2):

        def four_blocks(i, carry, side=side):
            for u in range(4):
                one_block(side, i * 4 + u)
            return carry

        lax.fori_loop(0, 2, four_blocks, 0)

    glob, owned, rows_of = owned_globals(glob_ref)

    @pl.when(owned[0] | owned[1])
    def _():
        query = jnp.concatenate([q_buf[side, pl.ds(row, BLK)] for side, row in rows_of], axis=0)
        state = (dense_ref[0], dense_ref[1], dense_ref[2])
        _, total, acc = lax.fori_loop(3, 6, lambda i, state: dense_step(query, kv_buf.at[i], state), state)
        result = (acc / total).astype(jnp.bfloat16)
        for k, (side, row) in enumerate(rows_of):

            for which in range(2):

                @pl.when(owned[k] & (side == which))
                def _(k=k, which=which, row=row):
                    o_refs[which][pl.ds(row, BLK)] = result[k * BLK : (k + 1) * BLK]


def owned_globals(glob_ref):
    z = lax.axis_index("z")
    core = lax.axis_index("core")
    glob = [glob_ref[g] for g in range(2)]
    rows_of = [(lax.rem(g // 8 + core, 2), pl.multiple_of(lax.rem(g, 8) * BLK, BLK)) for g in glob]
    return glob, [g // 16 == z for g in glob], rows_of


def dense_step(query, kv_ref, state):
    top, total, acc = state
    keys = jnp.concatenate([kv_ref[0, 0], kv_ref[1, 0]], axis=0)
    values = jnp.concatenate([kv_ref[0, 1], kv_ref[1, 1]], axis=0)
    scores = lax.dot_general(query, keys, (((1,), (1,)), ((), ())), preferred_element_type=jnp.float32)
    scores = scores * (1.0 / math.sqrt(DH))
    new = jnp.maximum(top, jnp.max(scores, axis=1, keepdims=True))
    factor = jnp.exp(top - new)
    probs = jnp.exp(scores - new[:, :1])
    total = total * factor + jnp.sum(probs, axis=1, keepdims=True)
    acc = acc * factor + jnp.dot(probs.astype(jnp.bfloat16), values, preferred_element_type=jnp.float32)
    return new, total, acc


def dense_kernel(*refs):
    glob_ref, mine_ref, theirs_ref = refs[:3]
    rings = refs[3:8], refs[8:13]
    o_ref, kv_buf, q_buf, sem = refs[13:]
    _, owned, rows_of = owned_globals(glob_ref)

    @pl.when(owned[0] | owned[1])
    def _():
        copies = [(mine_ref, q_buf.at[0]), (theirs_ref.at[pl.ds(0, 512)], q_buf.at[1])]
        for side, arrays in enumerate(rings):
            copies += [(array, kv_buf.at[i, side]) for i, array in enumerate(arrays)]
        copies = [pltpu.make_async_copy(src, dst, sem.at[i]) for i, (src, dst) in enumerate(copies)]
        for copy in copies:
            copy.start()
        for copy in copies:
            copy.wait()
        query = jnp.concatenate([q_buf[side, pl.ds(row, BLK)] for side, row in rows_of], axis=0)
        shape = (2 * BLK, DH)
        init = (jnp.full(shape, NEG, jnp.float32), jnp.zeros(shape, jnp.float32), jnp.zeros(shape, jnp.float32))
        state = lax.fori_loop(0, 5, lambda i, state: dense_step(query, kv_buf.at[i], state), init)
        for i, value in enumerate(state):
            o_ref[i] = value


def dense(glob, mine, theirs, own, other):
    bf16 = jnp.bfloat16
    return pl.pallas_call(
        dense_kernel,
        out_shape=jax.ShapeDtypeStruct((3, 2 * BLK, DH), jnp.float32),
        in_specs=[SMEM] + [HBM] * 12,
        out_specs=VMEM,
        scratch_shapes=[
            pltpu.VMEM((5, 2, 2, 512, DH), bf16),
            pltpu.VMEM((2, 512, DH), bf16),
            pltpu.SemaphoreType.DMA((12,)),
        ],
        compiler_params=PARAMS,
        name="dense",
    )(glob, mine, theirs, *own[:5], *other[:5])


def attend(rand, glob, radius, mine, theirs, own, other, started):
    bf16 = jnp.bfloat16
    return pl.pallas_call(
        attend_kernel,
        out_shape=(jax.ShapeDtypeStruct((512, DH), bf16),) * 2,
        in_specs=[SMEM] * 3 + [HBM] * 18 + [VMEM],
        out_specs=(VMEM, VMEM),
        scratch_shapes=[
            pltpu.VMEM((NZ, 2, 2, 512, DH), bf16),
            pltpu.VMEM((2, 512, DH), bf16),
            pltpu.SemaphoreType.DMA((18,)),
        ],
        compiler_params=PARAMS,
        name="attend",
    )(rand, glob, radius, mine, theirs, *own, *other, started)


def swap(a):
    return lax.ppermute(a, "core", [(0, 1), (1, 0)])


def body(tokens, w_qkv, w_out, rand_blocks, glob_blocks, window_radius):
    bf16 = jnp.bfloat16
    rand = rand_blocks.reshape(-1)
    ids = jnp.pad(rand.astype(bf16)[None], ((0, 15), (0, DH - 48)))
    heads = jax.ShapeDtypeStruct((2, 512, DH), bf16)
    shapes = (jax.ShapeDtypeStruct((512, DH), bf16), heads, jax.ShapeDtypeStruct((528, DH), bf16), heads)
    (mine, own, send_q, send_kv), ordered = plane_matmul(
        tokens, w_qkv.transpose(1, 0, 2), split_heads, shapes, "project", (ids,), order(w_out)
    )
    own = z_ring(own)
    other = swap(send_kv)
    ordered, _ = lax.optimization_barrier((ordered, other))
    w_cols = lax.all_to_all(ordered, ("y", "x"), 0, 0, tiled=True)
    other = z_ring(other)
    theirs = swap(send_q)
    ids, _ = lax.optimization_barrier((theirs[512:], own[1:3]))
    rand = jnp.concatenate([rand, ids[0, :48].astype(jnp.int32)])
    started = dense(glob_blocks, mine, theirs, own, other)
    own[5], other[6], started, rand = lax.optimization_barrier((own[5], other[6], started, rand))
    own.append(shift(own[5], "z", 1))
    other.append(shift(other[6], "z", -1))
    att = attend(rand, glob_blocks, window_radius, mine, theirs, own, other, started)
    attended = jnp.concatenate([att[0], swap(att[1])], axis=1)
    out = jax.ShapeDtypeStruct((512, 256), bf16)
    return plane_matmul(attended, w_cols[None], round_out, out, "output", (), w_cols)[0]


def solution(mesh):
    grid = Mesh(mesh.devices.reshape(NZ, 2, NXY, NXY), ("z", "core", "y", "x"))
    seq, tp = ("z", "core"), ("y", "x")
    return jax.shard_map(
        body,
        mesh=grid,
        in_specs=(P(seq, tp), P(None, None, tp), P(tp, None), P(seq, tp, None), P(), P(tp)),
        out_specs=P(seq, tp),
        check_vma=False,
    )
```

```python
import math

import jax
import jax.numpy as jnp
from jax import lax
from jax.experimental import pallas as pl
from jax.experimental.pallas import tpu as pltpu
from jax.sharding import Mesh, PartitionSpec as P

DH = 128
BLK = 64
NZ = 8
NXY = 4
NEG = -1e30
OFFS = (0, -1, 1, 2)


def shift(a, axis, step):
    n = lax.axis_size(axis)
    return lax.ppermute(a, axis, [(i, (i + step) % n) for i in range(n)])


def around4(a, axis):
    return [shift(a, axis, 1), shift(a, axis, -1), shift(a, axis, 2)]


def plane_matmul(a, w, finish, out_shape, name, more=(), extra=()):
    n = a.shape[0] // 2
    others = around4(a[n:], "y")
    by_x = lax.all_to_all(jnp.concatenate([a[:n]] * NXY, axis=0), "x", 0, 0, tiled=True)
    by_x, others = lax.optimization_barrier((by_x, others))
    near = [by_x, jnp.concatenate([a[n:], *others], axis=0)]
    far = [(shift(stack, second, 1), shift(stack, second, -1)) for stack, second in zip(near, "yx")]

    def blocks(v):
        return v.reshape(-1, n, 256)

    sums = partial_matmul((0,), [[blocks(v)] for v in near], w, None, name)
    far, sums, extra = lax.optimization_barrier((far, sums, extra))
    last = []
    for (low, high), second in zip(far, "yx"):
        last.append((shift(low[: 2 * n], second, 1), shift(high[2 * n :], second, -1)))
    sums = partial_matmul((1, 2), [[blocks(v) for v in f] for f in far], w, sums, name)
    out = partial_matmul((3,), [[blocks(v) for v in f] for f in last], w, sums, name, finish, out_shape, more)
    return out, extra


def partial_kernel(steps, counts, n, groups, has_sums, n_more, finish, *refs):
    n_x = sum(len(c) for c in counts)
    x_refs, w_ref = refs[:n_x], refs[n_x]
    sums_ref = refs[n_x + 1] if has_sums else None
    x_buf, w_buf, acc, x_sem, w_sem, s_sem = refs[-6:]
    more = refs[n_x + 1 + has_sums : n_x + 1 + has_sums + n_more]
    outs = refs[n_x + 1 + has_sums + n_more : -6]
    y = lax.axis_index("y")
    x = lax.axis_index("x")
    x_copies = []
    i = 0
    for half in range(2):
        at = 0
        for count in counts[half]:
            x_copies.append(pltpu.make_async_copy(x_refs[i], x_buf.at[half, pl.ds(at, count)], x_sem.at[i]))
            at += count
            i += 1
    n_steps = len(steps)

    def w_copy(part, j, owner):
        row = pl.multiple_of(owner * 256, 256)
        return pltpu.make_async_copy(
            w_ref.at[:, pl.ds(row, 256)], w_buf.at[part, :, pl.ds(j * 256, 256)], w_sem.at[part, j]
        )

    for copy in x_copies:
        copy.start()
    if has_sums:
        sums_copy = pltpu.make_async_copy(sums_ref, acc, s_sem)
    for half in range(2):
        for k, step in enumerate(steps):
            for j in range(NXY):
                if half == 0:
                    owner = lax.rem(y + OFFS[step] + NXY, NXY) * NXY + j
                else:
                    owner = lax.rem(y + OFFS[j] + NXY, NXY) * NXY + lax.rem(x + OFFS[step] + NXY, NXY)
                w_copy(half * n_steps + k, j, owner).start()
        if has_sums and half == 0:
            sums_copy.start()
    for copy in x_copies:
        copy.wait()

    def multiply(part, carry):
        half, k = part // n_steps, lax.rem(part, n_steps)
        for j in range(NXY):
            w_copy(part, j, 0).wait()
        rows = jnp.concatenate([x_buf[half, NXY * k + j] for j in range(NXY)], axis=1)
        span = pl.ds(pl.multiple_of(half * n, n), n)
        if has_sums:

            @pl.when(part == 0)
            def _():
                sums_copy.wait()

        for g in range(groups):
            value = jnp.dot(rows, w_buf[part, g], preferred_element_type=jnp.float32)
            if has_sums:
                value = acc[g, span] + value
            acc[g, span] = value
        return carry

    lax.fori_loop(0, 2 * n_steps, multiply, 0)
    if finish is None:
        copy = pltpu.make_async_copy(acc, outs[0], s_sem)
        copy.start()
        copy.wait()
    else:
        finish(acc, *more, *outs)


HBM = pl.BlockSpec(memory_space=pltpu.HBM)
VMEM = pl.BlockSpec(memory_space=pltpu.VMEM)
SMEM = pl.BlockSpec(memory_space=pltpu.SMEM)
PARAMS = pltpu.CompilerParams(vmem_limit_bytes=56 * 1024 * 1024)


def partial_matmul(steps, halves, w, sums, name, finish=None, out_shape=None, more=()):
    counts = [[v.shape[0] for v in half] for half in halves]
    xs = [v for half in halves for v in half]
    n, groups = xs[0].shape[1], w.shape[0]
    total = jax.ShapeDtypeStruct((groups, 2 * n, 256), jnp.float32)
    has_sums = sums is not None
    operands = [*xs, w] + ([sums] if has_sums else [])
    bf16 = jnp.bfloat16
    return pl.pallas_call(
        lambda *refs: partial_kernel(steps, counts, n, groups, has_sums, len(more), finish, *refs),
        out_shape=total if finish is None else out_shape,
        in_specs=[HBM] * len(operands) + [VMEM] * len(more),
        out_specs=HBM if finish is None else jax.tree.map(lambda _: VMEM, out_shape),
        scratch_shapes=[
            pltpu.VMEM((2, NXY * len(steps), n, 256), bf16),
            pltpu.VMEM((2 * len(steps), groups, 1024, 256), bf16),
            pltpu.VMEM((groups, 2 * n, 256), jnp.float32),
            pltpu.SemaphoreType.DMA((len(xs),)),
            pltpu.SemaphoreType.DMA((2 * len(steps), NXY)),
            pltpu.SemaphoreType.DMA(()),
        ],
        compiler_params=PARAMS,
        name=name + str(steps[0]),
    )(*operands, *more)


def split_heads(acc, ids_ref, q_ref, kv_ref, send_q_ref, send_kv_ref):
    first = lax.axis_index("core") == 0
    for g in range(3):
        h0 = acc[g, :, :DH].astype(jnp.bfloat16)
        h1 = acc[g, :, DH:].astype(jnp.bfloat16)
        mine = jnp.where(first, h0, h1)
        other = jnp.where(first, h1, h0)
        if g == 0:
            q_ref[...] = mine
            send_q_ref[:512] = other
        else:
            kv_ref[g - 1] = mine
            send_kv_ref[g - 1] = other
    send_q_ref[512:] = ids_ref[...]


def round_out(acc, o_ref):
    o_ref[...] = acc[0].astype(jnp.bfloat16)


def order_kernel(w_ref, o_ref, sem):
    core = lax.axis_index("core")
    copies = []
    for h in range(2):
        row = pl.multiple_of(lax.rem(core + h, 2) * DH, DH)
        for t in range(16):
            src = w_ref.at[pl.ds(row, DH), pl.ds(t * 256, 256)]
            copies.append(pltpu.make_async_copy(src, o_ref.at[t, pl.ds(h * DH, DH)], sem.at[h, t]))
    for copy in copies:
        copy.start()
    for copy in copies:
        copy.wait()


def order(w_out):
    return pl.pallas_call(
        order_kernel,
        out_shape=jax.ShapeDtypeStruct((16, 256, 256), jnp.bfloat16),
        in_specs=[VMEM],
        out_specs=HBM,
        scratch_shapes=[pltpu.SemaphoreType.DMA((2, 16))],
        compiler_params=PARAMS,
        name="order",
    )(w_out).reshape(4096, 256)


def z_ring(a):
    f1, b1 = shift(a, "z", 1), shift(a, "z", -1)
    f2, b2 = shift(f1, "z", 1), shift(b1, "z", -1)
    return [a, f1, b1, f2, b2, shift(f2, "z", 1), shift(b2, "z", -1)]


SLOTS = (0, 7, 1, 6, 2, 5, 3, 4)


def attend_kernel(*refs):
    rand_ref, glob_ref, radius_ref, mine_ref, theirs_ref = refs[:5]
    rings, dense_ref = (refs[5:13], refs[13:21]), refs[21]
    o_refs = refs[22:24]
    kv_buf, q_buf, sem = refs[24:]
    copies = [(mine_ref, q_buf.at[0]), (theirs_ref.at[pl.ds(0, 512)], q_buf.at[1])]
    for side, arrays in enumerate(rings):
        copies += [(array, kv_buf.at[slot, side]) for array, slot in zip(arrays, SLOTS)]
    copies = [pltpu.make_async_copy(src, dst, sem.at[i]) for i, (src, dst) in enumerate(copies)]
    for copy in copies:
        copy.start()
    for copy in copies:
        copy.wait()

    z = lax.axis_index("z")
    core = lax.axis_index("core")
    radius = radius_ref[core]
    scale = 1.0 / math.sqrt(DH)

    def place(block):
        slot = lax.rem(block // 16 - z + NZ, NZ)
        side = lax.rem(block // 8 + core, 2)
        return slot, side, pl.multiple_of(lax.rem(block, 8) * BLK, BLK)

    column = lax.broadcasted_iota(jnp.int32, (BLK, 8 * BLK), 1) // BLK
    nt = (((1,), (1,)), ((), ()))

    def one_block(side, j):
        block = z * 16 + lax.rem(core + side, 2) * 8 + j
        base = side * 48 + (j * 2 + core) * 3
        ids = [jnp.maximum(block - 1, 0), block, jnp.minimum(block + 1, 127)]
        ids += [rand_ref[base + r] for r in range(3)] + [glob_ref[g] for g in range(2)]
        places = [place(i) for i in ids]
        keys = jnp.concatenate([kv_buf[slot, owner, 0, pl.ds(row, BLK)] for slot, owner, row in places], axis=0)
        values = jnp.concatenate([kv_buf[slot, owner, 1, pl.ds(row, BLK)] for slot, owner, row in places], axis=0)
        mine = pl.ds(pl.multiple_of(j * BLK, BLK), BLK)
        scores = lax.dot_general(q_buf[side, mine], keys, nt, preferred_element_type=jnp.float32) * scale
        low_off = jnp.where((radius >= 1) & (block > 0), -1, 0)
        high_off = jnp.where((radius >= 1) & (block < 127), -1, 2)
        scores = jnp.where((column == low_off) | (column == high_off), NEG, scores)
        top = jnp.max(scores, axis=1, keepdims=True)
        probs = jnp.exp(scores - top)
        total = jnp.sum(probs, axis=1, keepdims=True)
        acc = jnp.dot(probs.astype(jnp.bfloat16), values, preferred_element_type=jnp.float32)
        o_refs[side][mine] = (acc / total).astype(jnp.bfloat16)

    for side in range(2):

        def four_blocks(i, carry, side=side):
            for u in range(4):
                one_block(side, i * 4 + u)
            return carry

        lax.fori_loop(0, 2, four_blocks, 0)

    glob, owned, rows_of = owned_globals(glob_ref)

    @pl.when(owned[0] | owned[1])
    def _():
        query = jnp.concatenate([q_buf[side, pl.ds(row, BLK)] for side, row in rows_of], axis=0)
        state = (dense_ref[0], dense_ref[1], dense_ref[2])
        _, total, acc = lax.fori_loop(3, 6, lambda i, state: dense_step(query, kv_buf.at[i], state), state)
        result = (acc / total).astype(jnp.bfloat16)
        for k, (side, row) in enumerate(rows_of):

            for which in range(2):

                @pl.when(owned[k] & (side == which))
                def _(k=k, which=which, row=row):
                    o_refs[which][pl.ds(row, BLK)] = result[k * BLK : (k + 1) * BLK]


def owned_globals(glob_ref):
    z = lax.axis_index("z")
    core = lax.axis_index("core")
    glob = [glob_ref[g] for g in range(2)]
    rows_of = [(lax.rem(g // 8 + core, 2), pl.multiple_of(lax.rem(g, 8) * BLK, BLK)) for g in glob]
    return glob, [g // 16 == z for g in glob], rows_of


def dense_step(query, kv_ref, state):
    top, total, acc = state
    keys = jnp.concatenate([kv_ref[0, 0], kv_ref[1, 0]], axis=0)
    values = jnp.concatenate([kv_ref[0, 1], kv_ref[1, 1]], axis=0)
    scores = lax.dot_general(query, keys, (((1,), (1,)), ((), ())), preferred_element_type=jnp.float32)
    scores = scores * (1.0 / math.sqrt(DH))
    new = jnp.maximum(top, jnp.max(scores, axis=1, keepdims=True))
    factor = jnp.exp(top - new)
    probs = jnp.exp(scores - new[:, :1])
    total = total * factor + jnp.sum(probs, axis=1, keepdims=True)
    acc = acc * factor + jnp.dot(probs.astype(jnp.bfloat16), values, preferred_element_type=jnp.float32)
    return new, total, acc


def dense_kernel(*refs):
    glob_ref, mine_ref, theirs_ref = refs[:3]
    rings = refs[3:8], refs[8:13]
    o_ref, kv_buf, q_buf, sem = refs[13:]
    _, owned, rows_of = owned_globals(glob_ref)

    @pl.when(owned[0] | owned[1])
    def _():
        copies = [(mine_ref, q_buf.at[0]), (theirs_ref.at[pl.ds(0, 512)], q_buf.at[1])]
        for side, arrays in enumerate(rings):
            copies += [(array, kv_buf.at[i, side]) for i, array in enumerate(arrays)]
        copies = [pltpu.make_async_copy(src, dst, sem.at[i]) for i, (src, dst) in enumerate(copies)]
        for copy in copies:
            copy.start()
        for copy in copies:
            copy.wait()
        query = jnp.concatenate([q_buf[side, pl.ds(row, BLK)] for side, row in rows_of], axis=0)
        shape = (2 * BLK, DH)
        init = (jnp.full(shape, NEG, jnp.float32), jnp.zeros(shape, jnp.float32), jnp.zeros(shape, jnp.float32))
        state = lax.fori_loop(0, 5, lambda i, state: dense_step(query, kv_buf.at[i], state), init)
        for i, value in enumerate(state):
            o_ref[i] = value


def dense(glob, mine, theirs, own, other):
    bf16 = jnp.bfloat16
    return pl.pallas_call(
        dense_kernel,
        out_shape=jax.ShapeDtypeStruct((3, 2 * BLK, DH), jnp.float32),
        in_specs=[SMEM] + [HBM] * 12,
        out_specs=VMEM,
        scratch_shapes=[
            pltpu.VMEM((5, 2, 2, 512, DH), bf16),
            pltpu.VMEM((2, 512, DH), bf16),
            pltpu.SemaphoreType.DMA((12,)),
        ],
        compiler_params=PARAMS,
        name="dense",
    )(glob, mine, theirs, *own[:5], *other[:5])


def attend(rand, glob, radius, mine, theirs, own, other, started):
    bf16 = jnp.bfloat16
    return pl.pallas_call(
        attend_kernel,
        out_shape=(jax.ShapeDtypeStruct((512, DH), bf16),) * 2,
        in_specs=[SMEM] * 3 + [HBM] * 18 + [VMEM],
        out_specs=(VMEM, VMEM),
        scratch_shapes=[
            pltpu.VMEM((NZ, 2, 2, 512, DH), bf16),
            pltpu.VMEM((2, 512, DH), bf16),
            pltpu.SemaphoreType.DMA((18,)),
        ],
        compiler_params=PARAMS,
        cost_estimate=pl.CostEstimate(flops=14000000000, transcendentals=0, bytes_accessed=28000000),
        name="attend",
    )(rand, glob, radius, mine, theirs, *own, *other, started)


def swap(a):
    return lax.ppermute(a, "core", [(0, 1), (1, 0)])


def body(tokens, w_qkv, w_out, rand_blocks, glob_blocks, window_radius):
    bf16 = jnp.bfloat16
    rand = rand_blocks.reshape(-1)
    ids = jnp.pad(rand.astype(bf16)[None], ((0, 15), (0, DH - 48)))
    heads = jax.ShapeDtypeStruct((2, 512, DH), bf16)
    shapes = (jax.ShapeDtypeStruct((512, DH), bf16), heads, jax.ShapeDtypeStruct((528, DH), bf16), heads)
    (mine, own, send_q, send_kv), ordered = plane_matmul(
        tokens, w_qkv.transpose(1, 0, 2), split_heads, shapes, "project", (ids,), order(w_out)
    )
    own = z_ring(own)
    other = swap(send_kv)
    ordered, _ = lax.optimization_barrier((ordered, other))
    w_cols = lax.all_to_all(ordered, ("y", "x"), 0, 0, tiled=True)
    other = z_ring(other)
    theirs = swap(send_q)
    ids, _ = lax.optimization_barrier((theirs[512:], own[1:3]))
    rand = jnp.concatenate([rand, ids[0, :48].astype(jnp.int32)])
    started = dense(glob_blocks, mine, theirs, own, other)
    own[5], other[6], started, rand = lax.optimization_barrier((own[5], other[6], started, rand))
    own.append(shift(own[5], "z", 1))
    other.append(shift(other[6], "z", -1))
    att = attend(rand, glob_blocks, window_radius, mine, theirs, own, other, started)
    att, w_cols = lax.optimization_barrier((att, w_cols))
    attended = jnp.concatenate([att[0], swap(att[1])], axis=1)
    out = jax.ShapeDtypeStruct((512, 256), bf16)
    return plane_matmul(attended, w_cols[None], round_out, out, "output")[0]


def solution(mesh):
    grid = Mesh(mesh.devices.reshape(NZ, 2, NXY, NXY), ("z", "core", "y", "x"))
    seq, tp = ("z", "core"), ("y", "x")
    return jax.shard_map(
        body,
        mesh=grid,
        in_specs=(P(seq, tp), P(None, None, tp), P(tp, None), P(seq, tp, None), P(), P(tp)),
        out_specs=P(seq, tp),
        check_vma=False,
    )
```

```python
import math

import jax
import jax.numpy as jnp
from jax import lax
from jax.experimental import pallas as pl
from jax.experimental.pallas import tpu as pltpu
from jax.sharding import Mesh, PartitionSpec as P

DH = 128
BLK = 64
NZ = 8
NXY = 4
NEG = -1e30
OFFS = (0, -1, 1, 2)


def shift(a, axis, step):
    n = lax.axis_size(axis)
    return lax.ppermute(a, axis, [(i, (i + step) % n) for i in range(n)])


def around4(a, axis):
    return [shift(a, axis, 1), shift(a, axis, -1), shift(a, axis, 2)]


def plane_matmul(a, w, finish, out_shape, name, more=(), extra=(), halves=True):
    n = a.shape[0] // 2
    others = around4(a[n:], "y")
    by_x = lax.all_to_all(jnp.concatenate([a[:n]] * NXY, axis=0), "x", 0, 0, tiled=True)
    by_x, others = lax.optimization_barrier((by_x, others))
    near = [by_x, jnp.concatenate([a[n:], *others], axis=0)]
    far = [(shift(stack, second, 1), shift(stack, second, -1)) for stack, second in zip(near, "yx")]

    def blocks(v):
        return v.reshape(-1, n, 256)

    sums = partial_matmul((0,), [[blocks(v)] for v in near], w, None, name)
    far, sums, extra = lax.optimization_barrier((far, sums, extra))
    last = []
    for (low, high), second in zip(far, "yx"):
        if halves:
            last.append((shift(low[: 2 * n], second, 1), shift(high[2 * n :], second, -1)))
        else:
            last.append((shift(low, second, 1),))
    sums = partial_matmul((1, 2), [[blocks(v) for v in f] for f in far], w, sums, name)
    out = partial_matmul((3,), [[blocks(v) for v in f] for f in last], w, sums, name, finish, out_shape, more)
    return out, extra


def partial_kernel(steps, counts, n, groups, has_sums, n_more, finish, *refs):
    n_x = sum(len(c) for c in counts)
    x_refs, w_ref = refs[:n_x], refs[n_x]
    sums_ref = refs[n_x + 1] if has_sums else None
    x_buf, w_buf, acc, x_sem, w_sem, s_sem = refs[-6:]
    more = refs[n_x + 1 + has_sums : n_x + 1 + has_sums + n_more]
    outs = refs[n_x + 1 + has_sums + n_more : -6]
    y = lax.axis_index("y")
    x = lax.axis_index("x")
    x_copies = []
    i = 0
    for half in range(2):
        at = 0
        for count in counts[half]:
            x_copies.append(pltpu.make_async_copy(x_refs[i], x_buf.at[half, pl.ds(at, count)], x_sem.at[i]))
            at += count
            i += 1
    n_steps = len(steps)

    def w_copy(part, j, owner):
        row = pl.multiple_of(owner * 256, 256)
        return pltpu.make_async_copy(
            w_ref.at[:, pl.ds(row, 256)], w_buf.at[part, :, pl.ds(j * 256, 256)], w_sem.at[part, j]
        )

    for copy in x_copies:
        copy.start()
    if has_sums:
        sums_copy = pltpu.make_async_copy(sums_ref, acc, s_sem)
    for half in range(2):
        for k, step in enumerate(steps):
            for j in range(NXY):
                if half == 0:
                    owner = lax.rem(y + OFFS[step] + NXY, NXY) * NXY + j
                else:
                    owner = lax.rem(y + OFFS[j] + NXY, NXY) * NXY + lax.rem(x + OFFS[step] + NXY, NXY)
                w_copy(half * n_steps + k, j, owner).start()
        if has_sums and half == 0:
            sums_copy.start()
    for copy in x_copies:
        copy.wait()

    def multiply(part, carry):
        half, k = part // n_steps, lax.rem(part, n_steps)
        for j in range(NXY):
            w_copy(part, j, 0).wait()
        rows = jnp.concatenate([x_buf[half, NXY * k + j] for j in range(NXY)], axis=1)
        span = pl.ds(pl.multiple_of(half * n, n), n)
        if has_sums:

            @pl.when(part == 0)
            def _():
                sums_copy.wait()

        for g in range(groups):
            value = jnp.dot(rows, w_buf[part, g], preferred_element_type=jnp.float32)
            if has_sums:
                value = acc[g, span] + value
            acc[g, span] = value
        return carry

    lax.fori_loop(0, 2 * n_steps, multiply, 0)
    if finish is None:
        copy = pltpu.make_async_copy(acc, outs[0], s_sem)
        copy.start()
        copy.wait()
    else:
        finish(acc, *more, *outs)


HBM = pl.BlockSpec(memory_space=pltpu.HBM)
VMEM = pl.BlockSpec(memory_space=pltpu.VMEM)
SMEM = pl.BlockSpec(memory_space=pltpu.SMEM)
PARAMS = pltpu.CompilerParams(vmem_limit_bytes=56 * 1024 * 1024)


def partial_matmul(steps, halves, w, sums, name, finish=None, out_shape=None, more=()):
    counts = [[v.shape[0] for v in half] for half in halves]
    xs = [v for half in halves for v in half]
    n, groups = xs[0].shape[1], w.shape[0]
    total = jax.ShapeDtypeStruct((groups, 2 * n, 256), jnp.float32)
    has_sums = sums is not None
    operands = [*xs, w] + ([sums] if has_sums else [])
    bf16 = jnp.bfloat16
    return pl.pallas_call(
        lambda *refs: partial_kernel(steps, counts, n, groups, has_sums, len(more), finish, *refs),
        out_shape=total if finish is None else out_shape,
        in_specs=[HBM] * len(operands) + [VMEM] * len(more),
        out_specs=HBM if finish is None else jax.tree.map(lambda _: VMEM, out_shape),
        scratch_shapes=[
            pltpu.VMEM((2, NXY * len(steps), n, 256), bf16),
            pltpu.VMEM((2 * len(steps), groups, 1024, 256), bf16),
            pltpu.VMEM((groups, 2 * n, 256), jnp.float32),
            pltpu.SemaphoreType.DMA((len(xs),)),
            pltpu.SemaphoreType.DMA((2 * len(steps), NXY)),
            pltpu.SemaphoreType.DMA(()),
        ],
        compiler_params=PARAMS,
        name=name + str(steps[0]),
    )(*operands, *more)


def split_heads(acc, ids_ref, q_ref, kv_ref, send_q_ref, send_kv_ref):
    first = lax.axis_index("core") == 0
    for g in range(3):
        h0 = acc[g, :, :DH].astype(jnp.bfloat16)
        h1 = acc[g, :, DH:].astype(jnp.bfloat16)
        mine = jnp.where(first, h0, h1)
        other = jnp.where(first, h1, h0)
        if g == 0:
            q_ref[...] = mine
            send_q_ref[:512] = other
        else:
            kv_ref[g - 1] = mine
            send_kv_ref[g - 1] = other
    send_q_ref[512:] = ids_ref[...]


def round_out(acc, o_ref):
    o_ref[...] = acc[0].astype(jnp.bfloat16)


def order_kernel(w_ref, o_ref, sem):
    core = lax.axis_index("core")
    copies = []
    for h in range(2):
        row = pl.multiple_of(lax.rem(core + h, 2) * DH, DH)
        for t in range(16):
            src = w_ref.at[pl.ds(row, DH), pl.ds(t * 256, 256)]
            copies.append(pltpu.make_async_copy(src, o_ref.at[t, pl.ds(h * DH, DH)], sem.at[h, t]))
    for copy in copies:
        copy.start()
    for copy in copies:
        copy.wait()


def order(w_out):
    return pl.pallas_call(
        order_kernel,
        out_shape=jax.ShapeDtypeStruct((16, 256, 256), jnp.bfloat16),
        in_specs=[VMEM],
        out_specs=HBM,
        scratch_shapes=[pltpu.SemaphoreType.DMA((2, 16))],
        compiler_params=PARAMS,
        name="order",
    )(w_out).reshape(4096, 256)


def z_ring(a):
    f1, b1 = shift(a, "z", 1), shift(a, "z", -1)
    f2, b2 = shift(f1, "z", 1), shift(b1, "z", -1)
    return [a, f1, b1, f2, b2, shift(f2, "z", 1), shift(b2, "z", -1)]


SLOTS = (0, 7, 1, 6, 2, 5, 3, 4)


def attend_kernel(*refs):
    rand_ref, glob_ref, radius_ref, mine_ref, theirs_ref = refs[:5]
    rings, dense_ref = (refs[5:13], refs[13:21]), refs[21]
    o_refs = refs[22:24]
    kv_buf, q_buf, o_buf, sem = refs[24:]
    copies = [(mine_ref, q_buf.at[0]), (theirs_ref.at[pl.ds(0, 512)], q_buf.at[1])]
    for side, arrays in enumerate(rings):
        copies += [(array, kv_buf.at[slot, side]) for array, slot in zip(arrays, SLOTS)]
    copies = [pltpu.make_async_copy(src, dst, sem.at[i]) for i, (src, dst) in enumerate(copies)]
    for copy in copies:
        copy.start()
    for copy in copies:
        copy.wait()

    z = lax.axis_index("z")
    core = lax.axis_index("core")
    radius = radius_ref[core]
    scale = 1.0 / math.sqrt(DH)

    def place(block):
        slot = lax.rem(block // 16 - z + NZ, NZ)
        side = lax.rem(block // 8 + core, 2)
        return slot, side, pl.multiple_of(lax.rem(block, 8) * BLK, BLK)

    column = lax.broadcasted_iota(jnp.int32, (BLK, 8 * BLK), 1) // BLK
    nt = (((1,), (1,)), ((), ()))

    def one_block(side, j):
        block = z * 16 + lax.rem(core + side, 2) * 8 + j
        base = side * 48 + (j * 2 + core) * 3
        ids = [jnp.maximum(block - 1, 0), block, jnp.minimum(block + 1, 127)]
        ids += [rand_ref[base + r] for r in range(3)] + [glob_ref[g] for g in range(2)]
        places = [place(i) for i in ids]
        keys = jnp.concatenate([kv_buf[slot, owner, 0, pl.ds(row, BLK)] for slot, owner, row in places], axis=0)
        values = jnp.concatenate([kv_buf[slot, owner, 1, pl.ds(row, BLK)] for slot, owner, row in places], axis=0)
        mine = pl.ds(j * BLK, BLK)
        scores = lax.dot_general(q_buf[side, mine], keys, nt, preferred_element_type=jnp.float32) * scale
        low_off = jnp.where((radius >= 1) & (block > 0), -1, 0)
        high_off = jnp.where((radius >= 1) & (block < 127), -1, 2)
        scores = jnp.where((column == low_off) | (column == high_off), NEG, scores)
        top = jnp.max(scores, axis=1, keepdims=True)
        probs = jnp.exp(scores - top)
        total = jnp.sum(probs, axis=1, keepdims=True)
        acc = jnp.dot(probs.astype(jnp.bfloat16), values, preferred_element_type=jnp.float32)
        o_buf[side, mine] = (acc / total).astype(jnp.bfloat16)

    def eight_blocks(side, carry):
        for j in range(8):
            one_block(side, j)
        return carry

    lax.fori_loop(0, 2, eight_blocks, 0)

    glob, owned, rows_of = owned_globals(glob_ref)

    @pl.when(owned[0] | owned[1])
    def _():
        query = jnp.concatenate([q_buf[side, pl.ds(row, BLK)] for side, row in rows_of], axis=0)
        state = (dense_ref[0], dense_ref[1], dense_ref[2])
        _, total, acc = lax.fori_loop(3, 6, lambda i, state: dense_step(query, kv_buf.at[i], state), state)
        result = (acc / total).astype(jnp.bfloat16)
        for k, (side, row) in enumerate(rows_of):

            @pl.when(owned[k])
            def _(k=k, side=side, row=row):
                o_buf[side, pl.ds(row, BLK)] = result[k * BLK : (k + 1) * BLK]

    for side in range(2):
        o_refs[side][...] = o_buf[side]


def owned_globals(glob_ref):
    z = lax.axis_index("z")
    core = lax.axis_index("core")
    glob = [glob_ref[g] for g in range(2)]
    rows_of = [(lax.rem(g // 8 + core, 2), pl.multiple_of(lax.rem(g, 8) * BLK, BLK)) for g in glob]
    return glob, [g // 16 == z for g in glob], rows_of


def dense_step(query, kv_ref, state):
    top, total, acc = state
    keys = jnp.concatenate([kv_ref[0, 0], kv_ref[1, 0]], axis=0)
    values = jnp.concatenate([kv_ref[0, 1], kv_ref[1, 1]], axis=0)
    scores = lax.dot_general(query, keys, (((1,), (1,)), ((), ())), preferred_element_type=jnp.float32)
    scores = scores * (1.0 / math.sqrt(DH))
    new = jnp.maximum(top, jnp.max(scores, axis=1, keepdims=True))
    factor = jnp.exp(top - new)
    probs = jnp.exp(scores - new[:, :1])
    total = total * factor + jnp.sum(probs, axis=1, keepdims=True)
    acc = acc * factor + jnp.dot(probs.astype(jnp.bfloat16), values, preferred_element_type=jnp.float32)
    return new, total, acc


def dense_kernel(*refs):
    glob_ref, mine_ref, theirs_ref = refs[:3]
    rings = refs[3:8], refs[8:13]
    o_ref, kv_buf, q_buf, sem = refs[13:]
    _, owned, rows_of = owned_globals(glob_ref)

    @pl.when(owned[0] | owned[1])
    def _():
        copies = [(mine_ref, q_buf.at[0]), (theirs_ref.at[pl.ds(0, 512)], q_buf.at[1])]
        for side, arrays in enumerate(rings):
            copies += [(array, kv_buf.at[i, side]) for i, array in enumerate(arrays)]
        copies = [pltpu.make_async_copy(src, dst, sem.at[i]) for i, (src, dst) in enumerate(copies)]
        for copy in copies:
            copy.start()
        for copy in copies:
            copy.wait()
        query = jnp.concatenate([q_buf[side, pl.ds(row, BLK)] for side, row in rows_of], axis=0)
        shape = (2 * BLK, DH)
        init = (jnp.full(shape, NEG, jnp.float32), jnp.zeros(shape, jnp.float32), jnp.zeros(shape, jnp.float32))
        state = lax.fori_loop(0, 5, lambda i, state: dense_step(query, kv_buf.at[i], state), init)
        for i, value in enumerate(state):
            o_ref[i] = value


def dense(glob, mine, theirs, own, other):
    bf16 = jnp.bfloat16
    return pl.pallas_call(
        dense_kernel,
        out_shape=jax.ShapeDtypeStruct((3, 2 * BLK, DH), jnp.float32),
        in_specs=[SMEM] + [HBM] * 12,
        out_specs=VMEM,
        scratch_shapes=[
            pltpu.VMEM((5, 2, 2, 512, DH), bf16),
            pltpu.VMEM((2, 512, DH), bf16),
            pltpu.SemaphoreType.DMA((12,)),
        ],
        compiler_params=PARAMS,
        name="dense",
    )(glob, mine, theirs, *own[:5], *other[:5])


def attend(rand, glob, radius, mine, theirs, own, other, started):
    bf16 = jnp.bfloat16
    return pl.pallas_call(
        attend_kernel,
        out_shape=(jax.ShapeDtypeStruct((512, DH), bf16),) * 2,
        in_specs=[SMEM] * 3 + [HBM] * 18 + [VMEM],
        out_specs=(VMEM, VMEM),
        scratch_shapes=[
            pltpu.VMEM((NZ, 2, 2, 512, DH), bf16),
            pltpu.VMEM((2, 512, DH), bf16),
            pltpu.VMEM((2, 512, DH), bf16),
            pltpu.SemaphoreType.DMA((18,)),
        ],
        compiler_params=PARAMS,
        cost_estimate=pl.CostEstimate(flops=14000000000, transcendentals=0, bytes_accessed=28000000),
        name="attend",
    )(rand, glob, radius, mine, theirs, *own, *other, started)


def swap(a):
    return lax.ppermute(a, "core", [(0, 1), (1, 0)])


def body(tokens, w_qkv, w_out, rand_blocks, glob_blocks, window_radius):
    bf16 = jnp.bfloat16
    rand = rand_blocks.reshape(-1)
    ids = jnp.pad(rand.astype(bf16)[None], ((0, 15), (0, DH - 48)))
    heads = jax.ShapeDtypeStruct((2, 512, DH), bf16)
    shapes = (jax.ShapeDtypeStruct((512, DH), bf16), heads, jax.ShapeDtypeStruct((528, DH), bf16), heads)
    (mine, own, send_q, send_kv), ordered = plane_matmul(
        tokens, w_qkv.transpose(1, 0, 2), split_heads, shapes, "project", (ids,), order(w_out), False
    )
    own = z_ring(own)
    other = swap(send_kv)
    ordered, _ = lax.optimization_barrier((ordered, other))
    w_cols = lax.all_to_all(ordered, ("y", "x"), 0, 0, tiled=True)
    other = z_ring(other)
    theirs = swap(send_q)
    ids, _ = lax.optimization_barrier((theirs[512:], own[1:3]))
    rand = jnp.concatenate([rand, ids[0, :48].astype(jnp.int32)])
    started = dense(glob_blocks, mine, theirs, own, other)
    own[5], other[6], started, rand = lax.optimization_barrier((own[5], other[6], started, rand))
    own.append(shift(own[5], "z", 1))
    other.append(shift(other[6], "z", -1))
    att = attend(rand, glob_blocks, window_radius, mine, theirs, own, other, started)
    att, w_cols = lax.optimization_barrier((att, w_cols))
    attended = jnp.concatenate([att[0], swap(att[1])], axis=1)
    out = jax.ShapeDtypeStruct((512, 256), bf16)
    return plane_matmul(attended, w_cols[None], round_out, out, "output")[0]


def solution(mesh):
    grid = Mesh(mesh.devices.reshape(NZ, 2, NXY, NXY), ("z", "core", "y", "x"))
    seq, tp = ("z", "core"), ("y", "x")
    return jax.shard_map(
        body,
        mesh=grid,
        in_specs=(P(seq, tp), P(None, None, tp), P(tp, None), P(seq, tp, None), P(), P(tp)),
        out_specs=P(seq, tp),
        check_vma=False,
    )
```

```python
import math

import jax
import jax.numpy as jnp
from jax import lax
from jax.experimental import pallas as pl
from jax.experimental.pallas import tpu as pltpu
from jax.sharding import Mesh, PartitionSpec as P

DH = 128
BLK = 64
NZ = 8
NXY = 4
NEG = -1e30
OFFS = (0, -1, 1, 2)


def shift(a, axis, step):
    n = lax.axis_size(axis)
    return lax.ppermute(a, axis, [(i, (i + step) % n) for i in range(n)])


def around4(a, axis):
    return [shift(a, axis, 1), shift(a, axis, -1), shift(a, axis, 2)]


def plane_matmul(a, w, finish, out_shape, name, more=(), extra=(), halves=True):
    n = a.shape[0] // 2
    others = around4(a[n:], "y")
    by_x = lax.all_to_all(jnp.concatenate([a[:n]] * NXY, axis=0), "x", 0, 0, tiled=True)
    by_x, others = lax.optimization_barrier((by_x, others))
    near = [by_x, jnp.concatenate([a[n:], *others], axis=0)]
    far = [(shift(stack, second, 1), shift(stack, second, -1)) for stack, second in zip(near, "yx")]

    def blocks(v):
        return v.reshape(-1, n, 256)

    sums = partial_matmul((0,), [[blocks(v)] for v in near], w, None, name)
    far, sums, extra = lax.optimization_barrier((far, sums, extra))
    last = []
    for (low, high), second in zip(far, "yx"):
        if halves:
            last.append((shift(low[: 2 * n], second, 1), shift(high[2 * n :], second, -1)))
        else:
            last.append((shift(low, second, 1),))
    sums = partial_matmul((1, 2), [[blocks(v) for v in f] for f in far], w, sums, name)
    out = partial_matmul((3,), [[blocks(v) for v in f] for f in last], w, sums, name, finish, out_shape, more)
    return out, extra


def partial_kernel(steps, counts, n, groups, has_sums, n_more, finish, *refs):
    n_x = sum(len(c) for c in counts)
    x_refs, w_ref = refs[:n_x], refs[n_x]
    sums_ref = refs[n_x + 1] if has_sums else None
    acc, s_sem = refs[-2:]
    more = refs[n_x + 1 + has_sums : n_x + 1 + has_sums + n_more]
    outs = refs[n_x + 1 + has_sums + n_more : -2]
    y = lax.axis_index("y")
    x = lax.axis_index("x")
    n_steps = len(steps)
    arrays = [[], []]
    i = 0
    for half in range(2):
        for count in counts[half]:
            arrays[half] += [(x_refs[i], j) for j in range(count)]
            i += 1
    if has_sums:
        sums_copy = pltpu.make_async_copy(sums_ref, acc, s_sem)
        sums_copy.start()
    for half in range(2):
        for k, step in enumerate(steps):
            blocks = arrays[half][NXY * k : NXY * (k + 1)]
            rows = jnp.concatenate([ref[j] for ref, j in blocks], axis=1)
            starts = []
            for j in range(NXY):
                if half == 0:
                    owner = lax.rem(y + OFFS[step] + NXY, NXY) * NXY + j
                else:
                    owner = lax.rem(y + OFFS[j] + NXY, NXY) * NXY + lax.rem(x + OFFS[step] + NXY, NXY)
                starts.append(pl.multiple_of(owner * 256, 256))
            if has_sums and half == 0 and k == 0:
                sums_copy.wait()
            span = slice(half * n, (half + 1) * n)

            def column(g, carry, rows=rows, starts=starts, span=span, first=k == 0 and not has_sums):
                weights = jnp.concatenate([w_ref[g, pl.ds(start, 256)] for start in starts], axis=0)
                value = jnp.dot(rows, weights, preferred_element_type=jnp.float32)
                acc[g, span] = value if first else acc[g, span] + value
                return carry

            lax.fori_loop(0, groups, column, 0)
    if finish is None:
        copy = pltpu.make_async_copy(acc, outs[0], s_sem)
        copy.start()
        copy.wait()
    else:
        finish(acc, *more, *outs)


HBM = pl.BlockSpec(memory_space=pltpu.HBM)
VMEM = pl.BlockSpec(memory_space=pltpu.VMEM)
SMEM = pl.BlockSpec(memory_space=pltpu.SMEM)
PARAMS = pltpu.CompilerParams(vmem_limit_bytes=24 * 1024 * 1024)


def in_vmem(a):
    return pltpu.with_memory_space_constraint(a, pltpu.VMEM)


def partial_matmul(steps, halves, w, sums, name, finish=None, out_shape=None, more=()):
    counts = [[v.shape[0] for v in half] for half in halves]
    xs = [v for half in halves for v in half]
    n, groups = xs[0].shape[1], w.shape[0]
    total = jax.ShapeDtypeStruct((groups, 2 * n, 256), jnp.float32)
    has_sums = sums is not None
    operands = [in_vmem(v) for v in [*xs, w]] + ([sums] if has_sums else [])
    return pl.pallas_call(
        lambda *refs: partial_kernel(steps, counts, n, groups, has_sums, len(more), finish, *refs),
        out_shape=total if finish is None else out_shape,
        in_specs=[VMEM] * (len(xs) + 1) + [HBM] * has_sums + [VMEM] * len(more),
        out_specs=HBM if finish is None else jax.tree.map(lambda _: VMEM, out_shape),
        scratch_shapes=[
            pltpu.VMEM((groups, 2 * n, 256), jnp.float32),
            pltpu.SemaphoreType.DMA(()),
        ],
        compiler_params=PARAMS,
        name=name + str(steps[0]),
    )(*operands, *more)


def split_heads(acc, ids_ref, q_ref, kv_ref, send_q_ref, send_kv_ref):
    first = lax.axis_index("core") == 0
    for g in range(3):
        h0 = acc[g, :, :DH].astype(jnp.bfloat16)
        h1 = acc[g, :, DH:].astype(jnp.bfloat16)
        mine = jnp.where(first, h0, h1)
        other = jnp.where(first, h1, h0)
        if g == 0:
            q_ref[...] = mine
            send_q_ref[:512] = other
        else:
            kv_ref[g - 1] = mine
            send_kv_ref[g - 1] = other
    send_q_ref[512:] = ids_ref[...]


def round_out(acc, o_ref):
    o_ref[...] = acc[0].astype(jnp.bfloat16)


def order_kernel(w_ref, o_ref, sem):
    core = lax.axis_index("core")
    copies = []
    for h in range(2):
        row = pl.multiple_of(lax.rem(core + h, 2) * DH, DH)
        for t in range(16):
            src = w_ref.at[pl.ds(row, DH), pl.ds(t * 256, 256)]
            copies.append(pltpu.make_async_copy(src, o_ref.at[t, pl.ds(h * DH, DH)], sem.at[h, t]))
    for copy in copies:
        copy.start()
    for copy in copies:
        copy.wait()


def order(w_out):
    return pl.pallas_call(
        order_kernel,
        out_shape=jax.ShapeDtypeStruct((16, 256, 256), jnp.bfloat16),
        in_specs=[VMEM],
        out_specs=HBM,
        scratch_shapes=[pltpu.SemaphoreType.DMA((2, 16))],
        compiler_params=PARAMS,
        name="order",
    )(w_out).reshape(4096, 256)


def z_ring(a):
    f1, b1 = shift(a, "z", 1), shift(a, "z", -1)
    f2, b2 = shift(f1, "z", 1), shift(b1, "z", -1)
    return [a, f1, b1, f2, b2, shift(f2, "z", 1), shift(b2, "z", -1)]


SLOTS = (0, 7, 1, 6, 2, 5, 3, 4)


def attend_kernel(*refs):
    rand_ref, glob_ref, radius_ref, mine_ref, theirs_ref = refs[:5]
    rings, dense_ref = (refs[5:13], refs[13:21]), refs[21]
    o_refs = refs[22:24]
    kv_buf, q_buf, o_buf, sem = refs[24:]
    copies = [(mine_ref, q_buf.at[0]), (theirs_ref.at[pl.ds(0, 512)], q_buf.at[1])]
    for side, arrays in enumerate(rings):
        copies += [(array, kv_buf.at[slot, side]) for array, slot in zip(arrays, SLOTS)]
    copies = [pltpu.make_async_copy(src, dst, sem.at[i]) for i, (src, dst) in enumerate(copies)]
    for copy in copies:
        copy.start()
    for copy in copies:
        copy.wait()

    z = lax.axis_index("z")
    core = lax.axis_index("core")
    radius = radius_ref[core]
    scale = 1.0 / math.sqrt(DH)

    def place(block):
        slot = lax.rem(block // 16 - z + NZ, NZ)
        side = lax.rem(block // 8 + core, 2)
        return slot, side, pl.multiple_of(lax.rem(block, 8) * BLK, BLK)

    column = lax.broadcasted_iota(jnp.int32, (BLK, 8 * BLK), 1) // BLK
    nt = (((1,), (1,)), ((), ()))

    def one_block(side, j):
        block = z * 16 + lax.rem(core + side, 2) * 8 + j
        base = side * 48 + (j * 2 + core) * 3
        ids = [jnp.maximum(block - 1, 0), block, jnp.minimum(block + 1, 127)]
        ids += [rand_ref[base + r] for r in range(3)] + [glob_ref[g] for g in range(2)]
        places = [place(i) for i in ids]
        keys = jnp.concatenate([kv_buf[slot, owner, 0, pl.ds(row, BLK)] for slot, owner, row in places], axis=0)
        values = jnp.concatenate([kv_buf[slot, owner, 1, pl.ds(row, BLK)] for slot, owner, row in places], axis=0)
        mine = pl.ds(j * BLK, BLK)
        scores = lax.dot_general(q_buf[side, mine], keys, nt, preferred_element_type=jnp.float32) * scale
        low_off = jnp.where((radius >= 1) & (block > 0), -1, 0)
        high_off = jnp.where((radius >= 1) & (block < 127), -1, 2)
        scores = jnp.where((column == low_off) | (column == high_off), NEG, scores)
        top = jnp.max(scores, axis=1, keepdims=True)
        probs = jnp.exp(scores - top)
        total = jnp.sum(probs, axis=1, keepdims=True)
        acc = jnp.dot(probs.astype(jnp.bfloat16), values, preferred_element_type=jnp.float32)
        o_buf[side, mine] = (acc / total).astype(jnp.bfloat16)

    def eight_blocks(side, carry):
        for j in range(8):
            one_block(side, j)
        return carry

    lax.fori_loop(0, 2, eight_blocks, 0)

    glob, owned, rows_of = owned_globals(glob_ref)

    @pl.when(owned[0] | owned[1])
    def _():
        query = jnp.concatenate([q_buf[side, pl.ds(row, BLK)] for side, row in rows_of], axis=0)
        state = (dense_ref[0], dense_ref[1], dense_ref[2])
        _, total, acc = lax.fori_loop(3, 6, lambda i, state: dense_step(query, kv_buf.at[i], state), state)
        result = (acc / total).astype(jnp.bfloat16)
        for k, (side, row) in enumerate(rows_of):

            @pl.when(owned[k])
            def _(k=k, side=side, row=row):
                o_buf[side, pl.ds(row, BLK)] = result[k * BLK : (k + 1) * BLK]

    for side in range(2):
        o_refs[side][...] = o_buf[side]


def owned_globals(glob_ref):
    z = lax.axis_index("z")
    core = lax.axis_index("core")
    glob = [glob_ref[g] for g in range(2)]
    rows_of = [(lax.rem(g // 8 + core, 2), pl.multiple_of(lax.rem(g, 8) * BLK, BLK)) for g in glob]
    return glob, [g // 16 == z for g in glob], rows_of


def dense_step(query, kv_ref, state):
    top, total, acc = state
    keys = jnp.concatenate([kv_ref[0, 0], kv_ref[1, 0]], axis=0)
    values = jnp.concatenate([kv_ref[0, 1], kv_ref[1, 1]], axis=0)
    scores = lax.dot_general(query, keys, (((1,), (1,)), ((), ())), preferred_element_type=jnp.float32)
    scores = scores * (1.0 / math.sqrt(DH))
    new = jnp.maximum(top, jnp.max(scores, axis=1, keepdims=True))
    factor = jnp.exp(top - new)
    probs = jnp.exp(scores - new[:, :1])
    total = total * factor + jnp.sum(probs, axis=1, keepdims=True)
    acc = acc * factor + jnp.dot(probs.astype(jnp.bfloat16), values, preferred_element_type=jnp.float32)
    return new, total, acc


def dense_kernel(*refs):
    glob_ref, mine_ref, theirs_ref = refs[:3]
    rings = refs[3:8], refs[8:13]
    o_ref, kv_buf, q_buf, sem = refs[13:]
    _, owned, rows_of = owned_globals(glob_ref)

    @pl.when(owned[0] | owned[1])
    def _():
        copies = [(mine_ref, q_buf.at[0]), (theirs_ref.at[pl.ds(0, 512)], q_buf.at[1])]
        for side, arrays in enumerate(rings):
            copies += [(array, kv_buf.at[i, side]) for i, array in enumerate(arrays)]
        copies = [pltpu.make_async_copy(src, dst, sem.at[i]) for i, (src, dst) in enumerate(copies)]
        for copy in copies:
            copy.start()
        for copy in copies:
            copy.wait()
        query = jnp.concatenate([q_buf[side, pl.ds(row, BLK)] for side, row in rows_of], axis=0)
        shape = (2 * BLK, DH)
        init = (jnp.full(shape, NEG, jnp.float32), jnp.zeros(shape, jnp.float32), jnp.zeros(shape, jnp.float32))
        state = lax.fori_loop(0, 5, lambda i, state: dense_step(query, kv_buf.at[i], state), init)
        for i, value in enumerate(state):
            o_ref[i] = value


def dense(glob, mine, theirs, own, other):
    bf16 = jnp.bfloat16
    return pl.pallas_call(
        dense_kernel,
        out_shape=jax.ShapeDtypeStruct((3, 2 * BLK, DH), jnp.float32),
        in_specs=[SMEM] + [VMEM] * 12,
        out_specs=VMEM,
        scratch_shapes=[
            pltpu.VMEM((5, 2, 2, 512, DH), bf16),
            pltpu.VMEM((2, 512, DH), bf16),
            pltpu.SemaphoreType.DMA((12,)),
        ],
        compiler_params=PARAMS,
        name="dense",
    )(glob, *map(in_vmem, [mine, theirs, *own[:5], *other[:5]]))


def attend(rand, glob, radius, mine, theirs, own, other, started):
    bf16 = jnp.bfloat16
    return pl.pallas_call(
        attend_kernel,
        out_shape=(jax.ShapeDtypeStruct((512, DH), bf16),) * 2,
        in_specs=[SMEM] * 3 + [VMEM] * 19,
        out_specs=(VMEM, VMEM),
        scratch_shapes=[
            pltpu.VMEM((NZ, 2, 2, 512, DH), bf16),
            pltpu.VMEM((2, 512, DH), bf16),
            pltpu.VMEM((2, 512, DH), bf16),
            pltpu.SemaphoreType.DMA((18,)),
        ],
        compiler_params=PARAMS,
        cost_estimate=pl.CostEstimate(flops=14000000000, transcendentals=0, bytes_accessed=28000000),
        name="attend",
    )(rand, glob, radius, in_vmem(mine), in_vmem(theirs), *map(in_vmem, [*own, *other]), started)


def swap(a):
    return lax.ppermute(a, "core", [(0, 1), (1, 0)])


def body(tokens, w_qkv, w_out, rand_blocks, glob_blocks, window_radius):
    bf16 = jnp.bfloat16
    rand = rand_blocks.reshape(-1)
    ids = jnp.pad(rand.astype(bf16)[None], ((0, 15), (0, DH - 48)))
    heads = jax.ShapeDtypeStruct((2, 512, DH), bf16)
    shapes = (jax.ShapeDtypeStruct((512, DH), bf16), heads, jax.ShapeDtypeStruct((528, DH), bf16), heads)
    (mine, own, send_q, send_kv), ordered = plane_matmul(
        tokens, w_qkv.transpose(1, 0, 2), split_heads, shapes, "project", (ids,), order(w_out), False
    )
    own = z_ring(own)
    other = swap(send_kv)
    ordered, _ = lax.optimization_barrier((ordered, other))
    w_cols = lax.all_to_all(ordered, ("y", "x"), 0, 0, tiled=True)
    other = z_ring(other)
    theirs = swap(send_q)
    ids, _ = lax.optimization_barrier((theirs[512:], own[1:3]))
    rand = jnp.concatenate([rand, ids[0, :48].astype(jnp.int32)])
    started = dense(glob_blocks, mine, theirs, own, other)
    own[5], other[6], started, rand = lax.optimization_barrier((own[5], other[6], started, rand))
    own.append(shift(own[5], "z", 1))
    other.append(shift(other[6], "z", -1))
    att = attend(rand, glob_blocks, window_radius, mine, theirs, own, other, started)
    att, w_cols = lax.optimization_barrier((att, w_cols))
    attended = jnp.concatenate([att[0], swap(att[1])], axis=1)
    out = jax.ShapeDtypeStruct((512, 256), bf16)
    return plane_matmul(attended, w_cols[None], round_out, out, "output")[0]


def solution(mesh):
    grid = Mesh(mesh.devices.reshape(NZ, 2, NXY, NXY), ("z", "core", "y", "x"))
    seq, tp = ("z", "core"), ("y", "x")
    return jax.shard_map(
        body,
        mesh=grid,
        in_specs=(P(seq, tp), P(None, None, tp), P(tp, None), P(seq, tp, None), P(), P(tp)),
        out_specs=P(seq, tp),
        check_vma=False,
    )
```

```python
import math

import jax
import jax.numpy as jnp
from jax import lax
from jax.experimental import pallas as pl
from jax.experimental.pallas import tpu as pltpu
from jax.sharding import Mesh, PartitionSpec as P

DH = 128
BLK = 64
NZ = 8
NXY = 4
NEG = -1e30
OFFS = (0, -1, 1, 2)


def shift(a, axis, step):
    n = lax.axis_size(axis)
    return lax.ppermute(a, axis, [(i, (i + step) % n) for i in range(n)])


def around4(a, axis):
    return [shift(a, axis, 1), shift(a, axis, -1), shift(a, axis, 2)]


def plane_matmul(a, w, finish, out_shape, name, more=(), extra=(), halves=True):
    n = a.shape[0] // 2
    w = in_vmem(w)
    others = around4(a[n:], "y")
    by_x = lax.all_to_all(jnp.concatenate([a[:n]] * NXY, axis=0), "x", 0, 0, tiled=True)
    by_x, others = lax.optimization_barrier((by_x, others))
    near = [by_x, jnp.concatenate([a[n:], *others], axis=0)]
    far = [(shift(stack, second, 1), shift(stack, second, -1)) for stack, second in zip(near, "yx")]

    def blocks(v):
        return v.reshape(-1, n, 256)

    sums = partial_matmul((0,), [[blocks(v)] for v in near], w, None, name)
    far, sums, extra = lax.optimization_barrier((far, sums, extra))
    last = []
    for (low, high), second in zip(far, "yx"):
        if halves:
            last.append((shift(low[: 2 * n], second, 1), shift(high[2 * n :], second, -1)))
        else:
            last.append((shift(low, second, 1),))
    sums = partial_matmul((1, 2), [[blocks(v) for v in f] for f in far], w, sums, name)
    out = partial_matmul((3,), [[blocks(v) for v in f] for f in last], w, sums, name, finish, out_shape, more)
    return out, extra


def partial_kernel(steps, counts, n, groups, has_sums, n_more, finish, *refs):
    n_x = sum(len(c) for c in counts)
    x_refs, w_ref = refs[:n_x], refs[n_x]
    sums_ref = refs[n_x + 1] if has_sums else None
    acc = refs[-1]
    more = refs[n_x + 1 + has_sums : n_x + 1 + has_sums + n_more]
    outs = refs[n_x + 1 + has_sums + n_more : -1]
    y = lax.axis_index("y")
    x = lax.axis_index("x")
    n_steps = len(steps)
    arrays = [[], []]
    i = 0
    for half in range(2):
        for count in counts[half]:
            arrays[half] += [(x_refs[i], j) for j in range(count)]
            i += 1
    acc = acc if finish is not None else outs[0]
    for half in range(2):
        for k, step in enumerate(steps):
            blocks = arrays[half][NXY * k : NXY * (k + 1)]
            rows = jnp.concatenate([ref[j] for ref, j in blocks], axis=1)
            starts = []
            for j in range(NXY):
                if half == 0:
                    owner = lax.rem(y + OFFS[step] + NXY, NXY) * NXY + j
                else:
                    owner = lax.rem(y + OFFS[j] + NXY, NXY) * NXY + lax.rem(x + OFFS[step] + NXY, NXY)
                starts.append(pl.multiple_of(owner * 256, 256))
            span = slice(half * n, (half + 1) * n)

            def column(g, carry, rows=rows, starts=starts, span=span, first=k == 0):
                weights = jnp.concatenate([w_ref[g, pl.ds(start, 256)] for start in starts], axis=0)
                value = jnp.dot(rows, weights, preferred_element_type=jnp.float32)
                if not first:
                    value = acc[g, span] + value
                elif has_sums:
                    value = sums_ref[g, span] + value
                acc[g, span] = value
                return carry

            lax.fori_loop(0, groups, column, 0)
    if finish is not None:
        finish(acc, *more, *outs)


HBM = pl.BlockSpec(memory_space=pltpu.HBM)
VMEM = pl.BlockSpec(memory_space=pltpu.VMEM)
SMEM = pl.BlockSpec(memory_space=pltpu.SMEM)
PARAMS = pltpu.CompilerParams(vmem_limit_bytes=8 * 1024 * 1024)


def in_vmem(a):
    return pltpu.with_memory_space_constraint(a, pltpu.VMEM)


def partial_matmul(steps, halves, w, sums, name, finish=None, out_shape=None, more=()):
    counts = [[v.shape[0] for v in half] for half in halves]
    xs = [v for half in halves for v in half]
    n, groups = xs[0].shape[1], w.shape[0]
    total = jax.ShapeDtypeStruct((groups, 2 * n, 256), jnp.float32)
    has_sums = sums is not None
    operands = [*(xs if finish is None else map(in_vmem, xs)), w] + ([in_vmem(sums)] if has_sums else [])
    return pl.pallas_call(
        lambda *refs: partial_kernel(steps, counts, n, groups, has_sums, len(more), finish, *refs),
        out_shape=total if finish is None else out_shape,
        in_specs=[VMEM] * (len(operands) + len(more)),
        out_specs=VMEM if finish is None else jax.tree.map(lambda _: VMEM, out_shape),
        scratch_shapes=[
            pltpu.VMEM((groups, 2 * n, 256), jnp.float32),
        ],
        compiler_params=PARAMS,
        name=name + str(steps[0]),
    )(*operands, *more)


def split_heads(acc, ids_ref, q_ref, kv_ref, send_q_ref, send_kv_ref):
    first = lax.axis_index("core") == 0
    for g in range(3):
        h0 = acc[g, :, :DH].astype(jnp.bfloat16)
        h1 = acc[g, :, DH:].astype(jnp.bfloat16)
        mine = jnp.where(first, h0, h1)
        other = jnp.where(first, h1, h0)
        if g == 0:
            q_ref[...] = mine
            send_q_ref[:512] = other
        else:
            kv_ref[g - 1] = mine
            send_kv_ref[g - 1] = other
    send_q_ref[512:] = ids_ref[...]


def round_out(acc, o_ref):
    o_ref[...] = acc[0].astype(jnp.bfloat16)


def order_kernel(w_ref, o_ref, sem):
    core = lax.axis_index("core")
    copies = []
    for h in range(2):
        row = pl.multiple_of(lax.rem(core + h, 2) * DH, DH)
        for t in range(16):
            src = w_ref.at[pl.ds(row, DH), pl.ds(t * 256, 256)]
            copies.append(pltpu.make_async_copy(src, o_ref.at[t, pl.ds(h * DH, DH)], sem.at[h, t]))
    for copy in copies:
        copy.start()
    for copy in copies:
        copy.wait()


def order(w_out):
    return pl.pallas_call(
        order_kernel,
        out_shape=jax.ShapeDtypeStruct((16, 256, 256), jnp.bfloat16),
        in_specs=[VMEM],
        out_specs=HBM,
        scratch_shapes=[pltpu.SemaphoreType.DMA((2, 16))],
        compiler_params=PARAMS,
        name="order",
    )(w_out).reshape(4096, 256)


def z_ring(a):
    f1, b1 = shift(a, "z", 1), shift(a, "z", -1)
    f2, b2 = shift(f1, "z", 1), shift(b1, "z", -1)
    return [a, f1, b1, f2, b2, shift(f2, "z", 1), shift(b2, "z", -1)]


SLOTS = (0, 7, 1, 6, 2, 5, 3, 4)


def attend_kernel(*refs):
    rand_ref, glob_ref, radius_ref, mine_ref, theirs_ref = refs[:5]
    rings, dense_ref = (refs[5:13], refs[13:21]), refs[21]
    o_refs = refs[22:24]
    kv_buf, q_buf, o_buf, sem = refs[24:]
    copies = [(mine_ref, q_buf.at[0]), (theirs_ref.at[pl.ds(0, 512)], q_buf.at[1])]
    for side, arrays in enumerate(rings):
        copies += [(array, kv_buf.at[slot, side]) for array, slot in zip(arrays, SLOTS)]
    copies = [pltpu.make_async_copy(src, dst, sem.at[i]) for i, (src, dst) in enumerate(copies)]
    for copy in copies:
        copy.start()
    for copy in copies:
        copy.wait()

    z = lax.axis_index("z")
    core = lax.axis_index("core")
    radius = radius_ref[core]
    scale = 1.0 / math.sqrt(DH)

    def place(block):
        slot = lax.rem(block // 16 - z + NZ, NZ)
        side = lax.rem(block // 8 + core, 2)
        return slot, side, pl.multiple_of(lax.rem(block, 8) * BLK, BLK)

    column = lax.broadcasted_iota(jnp.int32, (BLK, 8 * BLK), 1) // BLK
    nt = (((1,), (1,)), ((), ()))

    def one_block(side, j):
        block = z * 16 + lax.rem(core + side, 2) * 8 + j
        base = side * 48 + (j * 2 + core) * 3
        ids = [jnp.maximum(block - 1, 0), block, jnp.minimum(block + 1, 127)]
        ids += [rand_ref[base + r] for r in range(3)] + [glob_ref[g] for g in range(2)]
        places = [place(i) for i in ids]
        keys = jnp.concatenate([kv_buf[slot, owner, 0, pl.ds(row, BLK)] for slot, owner, row in places], axis=0)
        values = jnp.concatenate([kv_buf[slot, owner, 1, pl.ds(row, BLK)] for slot, owner, row in places], axis=0)
        mine = pl.ds(j * BLK, BLK)
        scores = lax.dot_general(q_buf[side, mine], keys, nt, preferred_element_type=jnp.float32) * scale
        low_off = jnp.where((radius >= 1) & (block > 0), -1, 0)
        high_off = jnp.where((radius >= 1) & (block < 127), -1, 2)
        scores = jnp.where((column == low_off) | (column == high_off), NEG, scores)
        top = jnp.max(scores, axis=1, keepdims=True)
        probs = jnp.exp(scores - top)
        total = jnp.sum(probs, axis=1, keepdims=True)
        acc = jnp.dot(probs.astype(jnp.bfloat16), values, preferred_element_type=jnp.float32)
        o_buf[side, mine] = (acc / total).astype(jnp.bfloat16)

    def eight_blocks(side, carry):
        for j in range(8):
            one_block(side, j)
        return carry

    lax.fori_loop(0, 2, eight_blocks, 0)

    glob, owned, rows_of = owned_globals(glob_ref)

    @pl.when(owned[0] | owned[1])
    def _():
        query = jnp.concatenate([q_buf[side, pl.ds(row, BLK)] for side, row in rows_of], axis=0)
        state = (dense_ref[0], dense_ref[1], dense_ref[2])
        _, total, acc = dense_step(query, kv_buf.at[4], state)
        result = (acc / total).astype(jnp.bfloat16)
        for k, (side, row) in enumerate(rows_of):

            @pl.when(owned[k])
            def _(k=k, side=side, row=row):
                o_buf[side, pl.ds(row, BLK)] = result[k * BLK : (k + 1) * BLK]

    copies = [pltpu.make_async_copy(o_buf.at[side], o_refs[side], sem.at[side]) for side in range(2)]
    for copy in copies:
        copy.start()
    for copy in copies:
        copy.wait()


def owned_globals(glob_ref):
    z = lax.axis_index("z")
    core = lax.axis_index("core")
    glob = [glob_ref[g] for g in range(2)]
    rows_of = [(lax.rem(g // 8 + core, 2), pl.multiple_of(lax.rem(g, 8) * BLK, BLK)) for g in glob]
    return glob, [g // 16 == z for g in glob], rows_of


def dense_step(query, kv_ref, state):
    top, total, acc = state
    keys = jnp.concatenate([kv_ref[0, 0], kv_ref[1, 0]], axis=0)
    values = jnp.concatenate([kv_ref[0, 1], kv_ref[1, 1]], axis=0)
    scores = lax.dot_general(query, keys, (((1,), (1,)), ((), ())), preferred_element_type=jnp.float32)
    scores = scores * (1.0 / math.sqrt(DH))
    new = jnp.maximum(top, jnp.max(scores, axis=1, keepdims=True))
    factor = jnp.exp(top - new)
    probs = jnp.exp(scores - new[:, :1])
    total = total * factor + jnp.sum(probs, axis=1, keepdims=True)
    acc = acc * factor + jnp.dot(probs.astype(jnp.bfloat16), values, preferred_element_type=jnp.float32)
    return new, total, acc


def dense_kernel(n, has_state, *refs):
    glob_ref, mine_ref, theirs_ref = refs[:3]
    rings = refs[3 : 3 + n], refs[3 + n : 3 + 2 * n]
    state_ref = refs[3 + 2 * n]
    o_ref, kv_buf, q_buf, sem = refs[-4:]
    _, owned, rows_of = owned_globals(glob_ref)

    @pl.when(owned[0] | owned[1])
    def _():
        copies = [(mine_ref, q_buf.at[0]), (theirs_ref.at[pl.ds(0, 512)], q_buf.at[1])]
        for side, arrays in enumerate(rings):
            copies += [(array, kv_buf.at[i, side]) for i, array in enumerate(arrays)]
        copies = [pltpu.make_async_copy(src, dst, sem.at[i]) for i, (src, dst) in enumerate(copies)]
        for copy in copies:
            copy.start()
        for copy in copies:
            copy.wait()
        query = jnp.concatenate([q_buf[side, pl.ds(row, BLK)] for side, row in rows_of], axis=0)
        if has_state:
            init = (state_ref[0], state_ref[1], state_ref[2])
        else:
            zeros = jnp.zeros((2 * BLK, DH), jnp.float32)
            init = (zeros + NEG, zeros, zeros)
        state = lax.fori_loop(0, n, lambda i, state: dense_step(query, kv_buf.at[i], state), init)
        for i, value in enumerate(state):
            o_ref[i] = value


def dense(glob, mine, theirs, own, other, state=None):
    bf16 = jnp.bfloat16
    n = len(own)
    has_state = state is not None
    return pl.pallas_call(
        lambda *refs: dense_kernel(n, has_state, *refs),
        out_shape=jax.ShapeDtypeStruct((3, 2 * BLK, DH), jnp.float32),
        in_specs=[SMEM] + [HBM] * 2 + [VMEM] * (2 * n + has_state),
        out_specs=VMEM,
        scratch_shapes=[
            pltpu.VMEM((n, 2, 2, 512, DH), bf16),
            pltpu.VMEM((2, 512, DH), bf16),
            pltpu.SemaphoreType.DMA((2 + 2 * n,)),
        ],
        compiler_params=PARAMS,
        name="dense",
    )(glob, mine, theirs, *map(in_vmem, [*own, *other]), *([state] if has_state else []))


def attend(rand, glob, radius, mine, theirs, own, other, started):
    bf16 = jnp.bfloat16
    return pl.pallas_call(
        attend_kernel,
        out_shape=(jax.ShapeDtypeStruct((512, DH), bf16),) * 2,
        in_specs=[SMEM] * 3 + [HBM] * 2 + [VMEM] * 17,
        out_specs=(HBM, HBM),
        scratch_shapes=[
            pltpu.VMEM((NZ, 2, 2, 512, DH), bf16),
            pltpu.VMEM((2, 512, DH), bf16),
            pltpu.VMEM((2, 512, DH), bf16),
            pltpu.SemaphoreType.DMA((18,)),
        ],
        compiler_params=PARAMS,
        cost_estimate=pl.CostEstimate(flops=14000000000, transcendentals=0, bytes_accessed=28000000),
        name="attend",
    )(rand, glob, radius, mine, theirs, *map(in_vmem, [*own, *other]), started)


def swap(a):
    return lax.ppermute(a, "core", [(0, 1), (1, 0)])


def body(tokens, w_qkv, w_out, rand_blocks, glob_blocks, window_radius):
    bf16 = jnp.bfloat16
    rand = rand_blocks.reshape(-1)
    ids = jnp.pad(rand.astype(bf16)[None], ((0, 15), (0, DH - 48)))
    heads = jax.ShapeDtypeStruct((2, 512, DH), bf16)
    shapes = (jax.ShapeDtypeStruct((512, DH), bf16), heads, jax.ShapeDtypeStruct((528, DH), bf16), heads)
    (mine, own, send_q, send_kv), (ordered, rand) = plane_matmul(
        tokens, w_qkv.transpose(1, 0, 2), split_heads, shapes, "project", (ids,), (order(w_out), rand), False
    )
    own = z_ring(own)
    other = swap(send_kv)
    ordered, _ = lax.optimization_barrier((ordered, other))
    w_cols = lax.all_to_all(ordered, ("y", "x"), 0, 0, tiled=True)
    other = z_ring(other)
    theirs = swap(send_q)
    ids, _ = lax.optimization_barrier((theirs[512:], own[1:3]))
    rand = jnp.concatenate([rand, ids[0, :48].astype(jnp.int32)])
    started = dense(glob_blocks, mine, theirs, own[:5], other[:5])
    own[5], other[6], started, rand = lax.optimization_barrier((own[5], other[6], started, rand))
    started = dense(glob_blocks, mine, theirs, own[5:], other[5:], started)
    own.append(shift(own[5], "z", 1))
    other.append(shift(other[6], "z", -1))
    att = attend(rand, glob_blocks, window_radius, mine, theirs, own, other, started)
    att, w_cols = lax.optimization_barrier((att, w_cols))
    attended = jnp.concatenate([att[0], swap(att[1])], axis=1)
    out = jax.ShapeDtypeStruct((512, 256), bf16)
    return plane_matmul(attended, w_cols[None], round_out, out, "output")[0]


def solution(mesh):
    grid = Mesh(mesh.devices.reshape(NZ, 2, NXY, NXY), ("z", "core", "y", "x"))
    seq, tp = ("z", "core"), ("y", "x")
    return jax.shard_map(
        body,
        mesh=grid,
        in_specs=(P(seq, tp), P(None, None, tp), P(tp, None), P(seq, tp, None), P(), P(tp)),
        out_specs=P(seq, tp),
        check_vma=False,
    )
```

```python
import math

import jax
import jax.numpy as jnp
from jax import lax
from jax.experimental import pallas as pl
from jax.experimental.pallas import tpu as pltpu
from jax.sharding import Mesh, PartitionSpec as P

DH = 128
BLK = 64
NZ = 8
NXY = 4
NEG = -1e30
OFFS = (0, -1, 1, 2)


def shift(a, axis, step):
    n = lax.axis_size(axis)
    return lax.ppermute(a, axis, [(i, (i + step) % n) for i in range(n)])


def around4(a, axis):
    return [shift(a, axis, 1), shift(a, axis, -1), shift(a, axis, 2)]


def plane_matmul(a, w, finish, out_shape, name, more=(), extra=(), halves=True):
    n = a.shape[0] // 2
    w = in_vmem(w)
    others = around4(a[n:], "y")
    by_x = lax.all_to_all(jnp.concatenate([a[:n]] * NXY, axis=0), "x", 0, 0, tiled=True)
    by_x, others = lax.optimization_barrier((by_x, others))
    near = [by_x, jnp.concatenate([a[n:], *others], axis=0)]
    far = [(shift(stack, second, 1), shift(stack, second, -1)) for stack, second in zip(near, "yx")]

    def blocks(v):
        return v.reshape(-1, n, 256)

    sums = partial_matmul((0,), [[blocks(v)] for v in near], w, None, name)
    lows, highs = zip(*far)
    lows, sums, extra = lax.optimization_barrier((lows, sums, extra))
    last = []
    for low, high, second in zip(lows, highs, "yx"):
        if halves:
            last.append((shift(low[: 2 * n], second, 1), shift(high[2 * n :], second, -1)))
        else:
            last.append((shift(low, second, 1),))
    far = list(zip(lows, highs))
    sums = partial_matmul((1, 2), [[blocks(v) for v in f] for f in far], w, sums, name)
    out = partial_matmul((3,), [[blocks(v) for v in f] for f in last], w, sums, name, finish, out_shape, more)
    return out, extra


def partial_kernel(steps, counts, n, groups, has_sums, n_more, finish, *refs):
    n_x = sum(len(c) for c in counts)
    x_refs, w_ref = refs[:n_x], refs[n_x]
    sums_ref = refs[n_x + 1] if has_sums else None
    acc = refs[-1]
    more = refs[n_x + 1 + has_sums : n_x + 1 + has_sums + n_more]
    outs = refs[n_x + 1 + has_sums + n_more : -1]
    y = lax.axis_index("y")
    x = lax.axis_index("x")
    n_steps = len(steps)
    arrays = [[], []]
    i = 0
    for half in range(2):
        for count in counts[half]:
            arrays[half] += [(x_refs[i], j) for j in range(count)]
            i += 1
    acc = acc if finish is not None else outs[0]
    for half in range(2):
        for k, step in enumerate(steps):
            blocks = arrays[half][NXY * k : NXY * (k + 1)]
            rows = jnp.concatenate([ref[j] for ref, j in blocks], axis=1)
            starts = []
            for j in range(NXY):
                if half == 0:
                    owner = lax.rem(y + OFFS[step] + NXY, NXY) * NXY + j
                else:
                    owner = lax.rem(y + OFFS[j] + NXY, NXY) * NXY + lax.rem(x + OFFS[step] + NXY, NXY)
                starts.append(pl.multiple_of(owner * 256, 256))
            span = slice(half * n, (half + 1) * n)

            def column(g, carry, rows=rows, starts=starts, span=span, first=k == 0):
                weights = jnp.concatenate([w_ref[g, pl.ds(start, 256)] for start in starts], axis=0)
                value = jnp.dot(rows, weights, preferred_element_type=jnp.float32)
                if not first:
                    value = acc[g, span] + value
                elif has_sums:
                    value = sums_ref[g, span] + value
                acc[g, span] = value
                return carry

            lax.fori_loop(0, groups, column, 0)
    if finish is not None:
        finish(acc, *more, *outs)


HBM = pl.BlockSpec(memory_space=pltpu.HBM)
VMEM = pl.BlockSpec(memory_space=pltpu.VMEM)
SMEM = pl.BlockSpec(memory_space=pltpu.SMEM)
PARAMS = pltpu.CompilerParams(vmem_limit_bytes=8 * 1024 * 1024)


def in_vmem(a):
    return pltpu.with_memory_space_constraint(a, pltpu.VMEM)


def partial_matmul(steps, halves, w, sums, name, finish=None, out_shape=None, more=()):
    counts = [[v.shape[0] for v in half] for half in halves]
    xs = [v for half in halves for v in half]
    n, groups = xs[0].shape[1], w.shape[0]
    total = jax.ShapeDtypeStruct((groups, 2 * n, 256), jnp.float32)
    has_sums = sums is not None
    operands = [*(xs if finish is None else map(in_vmem, xs)), w] + ([in_vmem(sums)] if has_sums else [])
    return pl.pallas_call(
        lambda *refs: partial_kernel(steps, counts, n, groups, has_sums, len(more), finish, *refs),
        out_shape=total if finish is None else out_shape,
        in_specs=[VMEM] * (len(operands) + len(more)),
        out_specs=VMEM if finish is None else jax.tree.map(lambda _: VMEM, out_shape),
        scratch_shapes=[
            pltpu.VMEM((groups, 2 * n, 256), jnp.float32),
        ],
        compiler_params=PARAMS,
        name=name + str(steps[0]),
    )(*operands, *more)


def split_heads(acc, ids_ref, q_ref, kv_ref, send_q_ref, send_kv_ref):
    first = lax.axis_index("core") == 0
    for g in range(3):
        h0 = acc[g, :, :DH].astype(jnp.bfloat16)
        h1 = acc[g, :, DH:].astype(jnp.bfloat16)
        mine = jnp.where(first, h0, h1)
        other = jnp.where(first, h1, h0)
        if g == 0:
            q_ref[...] = mine
            send_q_ref[:512] = other
        else:
            kv_ref[g - 1] = mine
            send_kv_ref[g - 1] = other
    send_q_ref[512:] = ids_ref[...]


def round_out(acc, o_ref):
    o_ref[...] = acc[0].astype(jnp.bfloat16)


def order_kernel(w_ref, o_ref, sem):
    core = lax.axis_index("core")
    copies = []
    for h in range(2):
        row = pl.multiple_of(lax.rem(core + h, 2) * DH, DH)
        for t in range(16):
            src = w_ref.at[pl.ds(row, DH), pl.ds(t * 256, 256)]
            copies.append(pltpu.make_async_copy(src, o_ref.at[t, pl.ds(h * DH, DH)], sem.at[h, t]))
    for copy in copies:
        copy.start()
    for copy in copies:
        copy.wait()


def order(w_out):
    return pl.pallas_call(
        order_kernel,
        out_shape=jax.ShapeDtypeStruct((16, 256, 256), jnp.bfloat16),
        in_specs=[VMEM],
        out_specs=HBM,
        scratch_shapes=[pltpu.SemaphoreType.DMA((2, 16))],
        compiler_params=PARAMS,
        name="order",
    )(w_out).reshape(4096, 256)


def z_ring(a):
    f1, b1 = shift(a, "z", 1), shift(a, "z", -1)
    f2, b2 = shift(f1, "z", 1), shift(b1, "z", -1)
    return [a, f1, b1, f2, b2, shift(f2, "z", 1), shift(b2, "z", -1)]


SLOTS = (0, 7, 1, 6, 2, 5, 3, 4)


def attend_kernel(*refs):
    rand_ref, glob_ref, radius_ref, mine_ref, theirs_ref = refs[:5]
    rings, dense_ref = (refs[5:13], refs[13:21]), refs[21]
    o_refs = refs[22:24]
    kv_buf, q_buf, o_buf, sem = refs[24:]
    copies = [(mine_ref, q_buf.at[0]), (theirs_ref.at[pl.ds(0, 512)], q_buf.at[1])]
    for side, arrays in enumerate(rings):
        copies += [(array, kv_buf.at[slot, side]) for array, slot in zip(arrays, SLOTS)]
    copies = [pltpu.make_async_copy(src, dst, sem.at[i]) for i, (src, dst) in enumerate(copies)]
    for copy in copies:
        copy.start()
    for copy in copies:
        copy.wait()

    z = lax.axis_index("z")
    core = lax.axis_index("core")
    radius = radius_ref[core]
    scale = 1.0 / math.sqrt(DH)

    def place(block):
        slot = lax.rem(block // 16 - z + NZ, NZ)
        side = lax.rem(block // 8 + core, 2)
        return slot, side, pl.multiple_of(lax.rem(block, 8) * BLK, BLK)

    column = lax.broadcasted_iota(jnp.int32, (BLK, 8 * BLK), 1) // BLK
    nt = (((1,), (1,)), ((), ()))

    def one_block(side, j):
        block = z * 16 + lax.rem(core + side, 2) * 8 + j
        base = side * 48 + (j * 2 + core) * 3
        ids = [jnp.maximum(block - 1, 0), block, jnp.minimum(block + 1, 127)]
        ids += [rand_ref[base + r] for r in range(3)] + [glob_ref[g] for g in range(2)]
        places = [place(i) for i in ids]
        keys = jnp.concatenate([kv_buf[slot, owner, 0, pl.ds(row, BLK)] for slot, owner, row in places], axis=0)
        values = jnp.concatenate([kv_buf[slot, owner, 1, pl.ds(row, BLK)] for slot, owner, row in places], axis=0)
        mine = pl.ds(j * BLK, BLK)
        scores = lax.dot_general(q_buf[side, mine], keys, nt, preferred_element_type=jnp.float32) * scale
        low_off = jnp.where((radius >= 1) & (block > 0), -1, 0)
        high_off = jnp.where((radius >= 1) & (block < 127), -1, 2)
        scores = jnp.where((column == low_off) | (column == high_off), NEG, scores)
        top = jnp.max(scores, axis=1, keepdims=True)
        probs = jnp.exp(scores - top)
        total = jnp.sum(probs, axis=1, keepdims=True)
        acc = jnp.dot(probs.astype(jnp.bfloat16), values, preferred_element_type=jnp.float32)
        o_buf[side, mine] = (acc / total).astype(jnp.bfloat16)

    def eight_blocks(side, carry):
        for j in range(8):
            one_block(side, j)
        return carry

    lax.fori_loop(0, 2, eight_blocks, 0)

    glob, owned, rows_of = owned_globals(glob_ref)

    @pl.when(owned[0] | owned[1])
    def _():
        query = jnp.concatenate([q_buf[side, pl.ds(row, BLK)] for side, row in rows_of], axis=0)
        state = (dense_ref[0], dense_ref[1], dense_ref[2])
        _, total, acc = dense_step(query, kv_buf.at[4], state)
        result = (acc / total).astype(jnp.bfloat16)
        for k, (side, row) in enumerate(rows_of):

            @pl.when(owned[k])
            def _(k=k, side=side, row=row):
                o_buf[side, pl.ds(row, BLK)] = result[k * BLK : (k + 1) * BLK]

    copies = [pltpu.make_async_copy(o_buf.at[side], o_refs[side], sem.at[side]) for side in range(2)]
    for copy in copies:
        copy.start()
    for copy in copies:
        copy.wait()


def owned_globals(glob_ref):
    z = lax.axis_index("z")
    core = lax.axis_index("core")
    glob = [glob_ref[g] for g in range(2)]
    rows_of = [(lax.rem(g // 8 + core, 2), pl.multiple_of(lax.rem(g, 8) * BLK, BLK)) for g in glob]
    return glob, [g // 16 == z for g in glob], rows_of


def dense_step(query, kv_ref, state):
    top, total, acc = state
    keys = jnp.concatenate([kv_ref[0, 0], kv_ref[1, 0]], axis=0)
    values = jnp.concatenate([kv_ref[0, 1], kv_ref[1, 1]], axis=0)
    scores = lax.dot_general(query, keys, (((1,), (1,)), ((), ())), preferred_element_type=jnp.float32)
    scores = scores * (1.0 / math.sqrt(DH))
    new = jnp.maximum(top, jnp.max(scores, axis=1, keepdims=True))
    factor = jnp.exp(top - new)
    probs = jnp.exp(scores - new[:, :1])
    total = total * factor + jnp.sum(probs, axis=1, keepdims=True)
    acc = acc * factor + jnp.dot(probs.astype(jnp.bfloat16), values, preferred_element_type=jnp.float32)
    return new, total, acc


def dense_kernel(n, has_state, *refs):
    glob_ref, mine_ref, theirs_ref = refs[:3]
    rings = refs[3 : 3 + n], refs[3 + n : 3 + 2 * n]
    state_ref = refs[3 + 2 * n]
    o_ref, kv_buf, q_buf, sem = refs[-4:]
    _, owned, rows_of = owned_globals(glob_ref)

    @pl.when(owned[0] | owned[1])
    def _():
        copies = [(mine_ref, q_buf.at[0]), (theirs_ref.at[pl.ds(0, 512)], q_buf.at[1])]
        for side, arrays in enumerate(rings):
            copies += [(array, kv_buf.at[i, side]) for i, array in enumerate(arrays)]
        copies = [pltpu.make_async_copy(src, dst, sem.at[i]) for i, (src, dst) in enumerate(copies)]
        for copy in copies:
            copy.start()
        for copy in copies:
            copy.wait()
        query = jnp.concatenate([q_buf[side, pl.ds(row, BLK)] for side, row in rows_of], axis=0)
        if has_state:
            init = (state_ref[0], state_ref[1], state_ref[2])
        else:
            zeros = jnp.zeros((2 * BLK, DH), jnp.float32)
            init = (zeros + NEG, zeros, zeros)
        state = lax.fori_loop(0, n, lambda i, state: dense_step(query, kv_buf.at[i], state), init)
        for i, value in enumerate(state):
            o_ref[i] = value


def dense(glob, mine, theirs, own, other, state=None):
    bf16 = jnp.bfloat16
    n = len(own)
    has_state = state is not None
    return pl.pallas_call(
        lambda *refs: dense_kernel(n, has_state, *refs),
        out_shape=jax.ShapeDtypeStruct((3, 2 * BLK, DH), jnp.float32),
        in_specs=[SMEM] + [HBM] * 2 + [VMEM] * (2 * n + has_state),
        out_specs=VMEM,
        scratch_shapes=[
            pltpu.VMEM((n, 2, 2, 512, DH), bf16),
            pltpu.VMEM((2, 512, DH), bf16),
            pltpu.SemaphoreType.DMA((2 + 2 * n,)),
        ],
        compiler_params=PARAMS,
        name="dense",
    )(glob, mine, theirs, *map(in_vmem, [*own, *other]), *([state] if has_state else []))


def attend(rand, glob, radius, mine, theirs, own, other, started):
    bf16 = jnp.bfloat16
    return pl.pallas_call(
        attend_kernel,
        out_shape=(jax.ShapeDtypeStruct((512, DH), bf16),) * 2,
        in_specs=[SMEM] * 3 + [HBM] * 2 + [VMEM] * 17,
        out_specs=(HBM, HBM),
        scratch_shapes=[
            pltpu.VMEM((NZ, 2, 2, 512, DH), bf16),
            pltpu.VMEM((2, 512, DH), bf16),
            pltpu.VMEM((2, 512, DH), bf16),
            pltpu.SemaphoreType.DMA((18,)),
        ],
        compiler_params=PARAMS,
        cost_estimate=pl.CostEstimate(flops=14000000000, transcendentals=0, bytes_accessed=28000000),
        name="attend",
    )(rand, glob, radius, mine, theirs, *map(in_vmem, [*own, *other]), started)


def swap(a):
    return lax.ppermute(a, "core", [(0, 1), (1, 0)])


def body(tokens, w_qkv, w_out, rand_blocks, glob_blocks, window_radius):
    bf16 = jnp.bfloat16
    rand = rand_blocks.reshape(-1)
    ids = jnp.pad(rand.astype(bf16)[None], ((0, 15), (0, DH - 48)))
    heads = jax.ShapeDtypeStruct((2, 512, DH), bf16)
    shapes = (jax.ShapeDtypeStruct((512, DH), bf16), heads, jax.ShapeDtypeStruct((528, DH), bf16), heads)
    (mine, own, send_q, send_kv), (ordered, rand) = plane_matmul(
        tokens, w_qkv.transpose(1, 0, 2), split_heads, shapes, "project", (ids,), (order(w_out), rand), False
    )
    own = z_ring(own)
    other = swap(send_kv)
    ordered, _ = lax.optimization_barrier((ordered, other))
    w_cols = lax.all_to_all(ordered, ("y", "x"), 0, 0, tiled=True)
    other = z_ring(other)
    theirs = swap(send_q)
    ids, _ = lax.optimization_barrier((theirs[512:], own[1:3]))
    rand = jnp.concatenate([rand, ids[0, :48].astype(jnp.int32)])
    started = dense(glob_blocks, mine, theirs, own[:5], other[:5])
    own[5], other[6], started, rand = lax.optimization_barrier((own[5], other[6], started, rand))
    started = dense(glob_blocks, mine, theirs, own[5:], other[5:], started)
    own.append(shift(own[5], "z", 1))
    other.append(shift(other[6], "z", -1))
    att = attend(rand, glob_blocks, window_radius, mine, theirs, own, other, started)
    att, w_cols = lax.optimization_barrier((att, w_cols))
    attended = jnp.concatenate([att[0], swap(att[1])], axis=1)
    out = jax.ShapeDtypeStruct((512, 256), bf16)
    return plane_matmul(attended, w_cols[None], round_out, out, "output")[0]


def solution(mesh):
    grid = Mesh(mesh.devices.reshape(NZ, 2, NXY, NXY), ("z", "core", "y", "x"))
    seq, tp = ("z", "core"), ("y", "x")
    return jax.shard_map(
        body,
        mesh=grid,
        in_specs=(P(seq, tp), P(None, None, tp), P(tp, None), P(seq, tp, None), P(), P(tp)),
        out_specs=P(seq, tp),
        check_vma=False,
    )
```

```python
import math

import jax
import jax.numpy as jnp
from jax import lax
from jax.experimental import pallas as pl
from jax.experimental.pallas import tpu as pltpu
from jax.sharding import Mesh, PartitionSpec as P

DH = 128
BLK = 64
NZ = 8
NXY = 4
NEG = -1e30
OFFS = (0, -1, 1, 2)


def shift(a, axis, step):
    n = lax.axis_size(axis)
    return lax.ppermute(a, axis, [(i, (i + step) % n) for i in range(n)])


def around4(a, axis):
    return [shift(a, axis, 1), shift(a, axis, -1), shift(a, axis, 2)]


def plane_matmul(a, w, finish, out_shape, name, more=(), extra=(), halves=True):
    n = a.shape[0] // 2
    w = in_vmem(w)
    others = around4(a[n:], "y")
    by_x = lax.all_to_all(jnp.broadcast_to(a[:n], (NXY, n, 256)).reshape(NXY * n, 256), "x", 0, 0, tiled=True)
    by_x, others = lax.optimization_barrier((by_x, others))
    near = [by_x, jnp.concatenate([a[n:], *others], axis=0)]
    far = [(shift(stack, second, 1), shift(stack, second, -1)) for stack, second in zip(near, "yx")]

    def blocks(v):
        return v.reshape(-1, n, 256)

    sums = partial_matmul((0,), [[blocks(v)] for v in near], w, None, name)
    lows, highs = zip(*far)
    lows, sums, extra = lax.optimization_barrier((lows, sums, extra))
    last = []
    for low, high, second in zip(lows, highs, "yx"):
        if halves:
            last.append((shift(low[: 2 * n], second, 1), shift(high[2 * n :], second, -1)))
        else:
            last.append((shift(low, second, 1),))
    far = list(zip(lows, highs))
    sums = partial_matmul((1, 2), [[blocks(v) for v in f] for f in far], w, sums, name)
    out = partial_matmul((3,), [[blocks(v) for v in f] for f in last], w, sums, name, finish, out_shape, more)
    return out, extra


def partial_kernel(steps, counts, n, groups, has_sums, n_more, finish, *refs):
    n_x = sum(len(c) for c in counts)
    x_refs, w_ref = refs[:n_x], refs[n_x]
    sums_ref = refs[n_x + 1] if has_sums else None
    acc = refs[-1]
    more = refs[n_x + 1 + has_sums : n_x + 1 + has_sums + n_more]
    outs = refs[n_x + 1 + has_sums + n_more : -1]
    y = lax.axis_index("y")
    x = lax.axis_index("x")
    n_steps = len(steps)
    arrays = [[], []]
    i = 0
    for half in range(2):
        for count in counts[half]:
            arrays[half] += [(x_refs[i], j) for j in range(count)]
            i += 1
    acc = acc if finish is not None else outs[0]
    for half in range(2):
        for k, step in enumerate(steps):
            blocks = arrays[half][NXY * k : NXY * (k + 1)]
            rows = jnp.concatenate([ref[j] for ref, j in blocks], axis=1)
            starts = []
            for j in range(NXY):
                if half == 0:
                    owner = lax.rem(y + OFFS[step] + NXY, NXY) * NXY + j
                else:
                    owner = lax.rem(y + OFFS[j] + NXY, NXY) * NXY + lax.rem(x + OFFS[step] + NXY, NXY)
                starts.append(pl.multiple_of(owner * 256, 256))
            span = slice(half * n, (half + 1) * n)

            def column(g, carry, rows=rows, starts=starts, span=span, first=k == 0):
                weights = jnp.concatenate([w_ref[g, pl.ds(start, 256)] for start in starts], axis=0)
                value = jnp.dot(rows, weights, preferred_element_type=jnp.float32)
                if not first:
                    value = acc[g, span] + value
                elif has_sums:
                    value = sums_ref[g, span] + value
                acc[g, span] = value
                return carry

            lax.fori_loop(0, groups, column, 0)
    if finish is not None:
        finish(acc, *more, *outs)


HBM = pl.BlockSpec(memory_space=pltpu.HBM)
VMEM = pl.BlockSpec(memory_space=pltpu.VMEM)
SMEM = pl.BlockSpec(memory_space=pltpu.SMEM)
PARAMS = pltpu.CompilerParams(vmem_limit_bytes=8 * 1024 * 1024)


def in_vmem(a):
    return pltpu.with_memory_space_constraint(a, pltpu.VMEM)


def partial_matmul(steps, halves, w, sums, name, finish=None, out_shape=None, more=()):
    counts = [[v.shape[0] for v in half] for half in halves]
    xs = [v for half in halves for v in half]
    n, groups = xs[0].shape[1], w.shape[0]
    total = jax.ShapeDtypeStruct((groups, 2 * n, 256), jnp.float32)
    has_sums = sums is not None
    operands = [*(xs if finish is None else map(in_vmem, xs)), w] + ([in_vmem(sums)] if has_sums else [])
    return pl.pallas_call(
        lambda *refs: partial_kernel(steps, counts, n, groups, has_sums, len(more), finish, *refs),
        out_shape=total if finish is None else out_shape,
        in_specs=[VMEM] * (len(operands) + len(more)),
        out_specs=VMEM if finish is None else jax.tree.map(lambda _: VMEM, out_shape),
        scratch_shapes=[
            pltpu.VMEM((groups, 2 * n, 256), jnp.float32),
        ],
        compiler_params=PARAMS,
        name=name + str(steps[0]),
    )(*operands, *more)


def split_heads(acc, ids_ref, q_ref, kv_ref, send_q_ref, send_kv_ref):
    first = lax.axis_index("core") == 0
    for g in range(3):
        h0 = acc[g, :, :DH].astype(jnp.bfloat16)
        h1 = acc[g, :, DH:].astype(jnp.bfloat16)
        mine = jnp.where(first, h0, h1)
        other = jnp.where(first, h1, h0)
        if g == 0:
            q_ref[...] = mine
            send_q_ref[:512] = other
        else:
            kv_ref[g - 1] = mine
            send_kv_ref[g - 1] = other
    send_q_ref[512:] = ids_ref[...]


def round_out(acc, o_ref):
    o_ref[...] = acc[0].astype(jnp.bfloat16)


def order_kernel(w_ref, o_ref, sem):
    core = lax.axis_index("core")
    copies = []
    for h in range(2):
        row = pl.multiple_of(lax.rem(core + h, 2) * DH, DH)
        for t in range(16):
            src = w_ref.at[pl.ds(row, DH), pl.ds(t * 256, 256)]
            copies.append(pltpu.make_async_copy(src, o_ref.at[t, pl.ds(h * DH, DH)], sem.at[h, t]))
    for copy in copies:
        copy.start()
    for copy in copies:
        copy.wait()


def order(w_out):
    return pl.pallas_call(
        order_kernel,
        out_shape=jax.ShapeDtypeStruct((16, 256, 256), jnp.bfloat16),
        in_specs=[VMEM],
        out_specs=HBM,
        scratch_shapes=[pltpu.SemaphoreType.DMA((2, 16))],
        compiler_params=PARAMS,
        name="order",
    )(w_out).reshape(4096, 256)


def z_ring(a):
    f1, b1 = shift(a, "z", 1), shift(a, "z", -1)
    f2, b2 = shift(f1, "z", 1), shift(b1, "z", -1)
    return [a, f1, b1, f2, b2, shift(f2, "z", 1), shift(b2, "z", -1)]


SLOTS = (0, 7, 1, 6, 2, 5, 3, 4)


def attend_kernel(*refs):
    rand_ref, glob_ref, radius_ref, mine_ref, theirs_ref = refs[:5]
    rings, dense_ref = (refs[5:13], refs[13:21]), refs[21]
    o_refs = refs[22:24]
    kv_buf, q_buf, o_buf, sem = refs[24:]
    copies = [(mine_ref, q_buf.at[0]), (theirs_ref.at[pl.ds(0, 512)], q_buf.at[1])]
    for side, arrays in enumerate(rings):
        copies += [(array, kv_buf.at[slot, side]) for array, slot in zip(arrays, SLOTS)]
    copies = [pltpu.make_async_copy(src, dst, sem.at[i]) for i, (src, dst) in enumerate(copies)]
    for copy in copies:
        copy.start()
    for copy in copies:
        copy.wait()

    z = lax.axis_index("z")
    core = lax.axis_index("core")
    radius = radius_ref[core]
    scale = 1.0 / math.sqrt(DH)

    def place(block):
        slot = lax.rem(block // 16 - z + NZ, NZ)
        side = lax.rem(block // 8 + core, 2)
        return slot, side, pl.multiple_of(lax.rem(block, 8) * BLK, BLK)

    column = lax.broadcasted_iota(jnp.int32, (BLK, 8 * BLK), 1) // BLK
    nt = (((1,), (1,)), ((), ()))

    def one_block(side, j):
        block = z * 16 + lax.rem(core + side, 2) * 8 + j
        base = side * 48 + (j * 2 + core) * 3
        ids = [jnp.maximum(block - 1, 0), block, jnp.minimum(block + 1, 127)]
        ids += [rand_ref[base + r] for r in range(3)] + [glob_ref[g] for g in range(2)]
        places = [place(i) for i in ids]
        keys = jnp.concatenate([kv_buf[slot, owner, 0, pl.ds(row, BLK)] for slot, owner, row in places], axis=0)
        values = jnp.concatenate([kv_buf[slot, owner, 1, pl.ds(row, BLK)] for slot, owner, row in places], axis=0)
        mine = pl.ds(j * BLK, BLK)
        scores = lax.dot_general(q_buf[side, mine], keys, nt, preferred_element_type=jnp.float32) * scale
        low_off = jnp.where((radius >= 1) & (block > 0), -1, 0)
        high_off = jnp.where((radius >= 1) & (block < 127), -1, 2)
        scores = jnp.where((column == low_off) | (column == high_off), NEG, scores)
        top = jnp.max(scores, axis=1, keepdims=True)
        probs = jnp.exp(scores - top)
        total = jnp.sum(probs, axis=1, keepdims=True)
        acc = jnp.dot(probs.astype(jnp.bfloat16), values, preferred_element_type=jnp.float32)
        o_buf[side, mine] = (acc / total).astype(jnp.bfloat16)

    def eight_blocks(side, carry):
        for j in range(8):
            one_block(side, j)
        return carry

    lax.fori_loop(0, 2, eight_blocks, 0)

    glob, owned, rows_of = owned_globals(glob_ref)

    @pl.when(owned[0] | owned[1])
    def _():
        query = jnp.concatenate([q_buf[side, pl.ds(row, BLK)] for side, row in rows_of], axis=0)
        state = (dense_ref[0], dense_ref[1], dense_ref[2])
        _, total, acc = dense_step(query, kv_buf.at[4], state)
        result = (acc / total).astype(jnp.bfloat16)
        for k, (side, row) in enumerate(rows_of):

            @pl.when(owned[k])
            def _(k=k, side=side, row=row):
                o_buf[side, pl.ds(row, BLK)] = result[k * BLK : (k + 1) * BLK]

    copies = [pltpu.make_async_copy(o_buf.at[side], o_refs[side], sem.at[side]) for side in range(2)]
    for copy in copies:
        copy.start()
    for copy in copies:
        copy.wait()


def owned_globals(glob_ref):
    z = lax.axis_index("z")
    core = lax.axis_index("core")
    glob = [glob_ref[g] for g in range(2)]
    rows_of = [(lax.rem(g // 8 + core, 2), pl.multiple_of(lax.rem(g, 8) * BLK, BLK)) for g in glob]
    return glob, [g // 16 == z for g in glob], rows_of


def dense_step(query, kv_ref, state):
    top, total, acc = state
    keys = jnp.concatenate([kv_ref[0, 0], kv_ref[1, 0]], axis=0)
    values = jnp.concatenate([kv_ref[0, 1], kv_ref[1, 1]], axis=0)
    scores = lax.dot_general(query, keys, (((1,), (1,)), ((), ())), preferred_element_type=jnp.float32)
    scores = scores * (1.0 / math.sqrt(DH))
    new = jnp.maximum(top, jnp.max(scores, axis=1, keepdims=True))
    factor = jnp.exp(top - new)
    probs = jnp.exp(scores - new[:, :1])
    total = total * factor + jnp.sum(probs, axis=1, keepdims=True)
    acc = acc * factor + jnp.dot(probs.astype(jnp.bfloat16), values, preferred_element_type=jnp.float32)
    return new, total, acc


def dense_kernel(n, has_state, *refs):
    glob_ref, mine_ref, theirs_ref = refs[:3]
    rings = refs[3 : 3 + n], refs[3 + n : 3 + 2 * n]
    state_ref = refs[3 + 2 * n]
    o_ref, kv_buf, q_buf, sem = refs[-4:]
    _, owned, rows_of = owned_globals(glob_ref)

    @pl.when(owned[0] | owned[1])
    def _():
        copies = [(mine_ref, q_buf.at[0]), (theirs_ref.at[pl.ds(0, 512)], q_buf.at[1])]
        for side, arrays in enumerate(rings):
            copies += [(array, kv_buf.at[i, side]) for i, array in enumerate(arrays)]
        copies = [pltpu.make_async_copy(src, dst, sem.at[i]) for i, (src, dst) in enumerate(copies)]
        for copy in copies:
            copy.start()
        for copy in copies:
            copy.wait()
        query = jnp.concatenate([q_buf[side, pl.ds(row, BLK)] for side, row in rows_of], axis=0)
        if has_state:
            init = (state_ref[0], state_ref[1], state_ref[2])
        else:
            zeros = jnp.zeros((2 * BLK, DH), jnp.float32)
            init = (zeros + NEG, zeros, zeros)
        state = lax.fori_loop(0, n, lambda i, state: dense_step(query, kv_buf.at[i], state), init)
        for i, value in enumerate(state):
            o_ref[i] = value


def dense(glob, mine, theirs, own, other, state=None):
    bf16 = jnp.bfloat16
    n = len(own)
    has_state = state is not None
    return pl.pallas_call(
        lambda *refs: dense_kernel(n, has_state, *refs),
        out_shape=jax.ShapeDtypeStruct((3, 2 * BLK, DH), jnp.float32),
        in_specs=[SMEM] + [HBM] * 2 + [VMEM] * (2 * n + has_state),
        out_specs=VMEM,
        scratch_shapes=[
            pltpu.VMEM((n, 2, 2, 512, DH), bf16),
            pltpu.VMEM((2, 512, DH), bf16),
            pltpu.SemaphoreType.DMA((2 + 2 * n,)),
        ],
        compiler_params=PARAMS,
        name="dense",
    )(glob, mine, theirs, *map(in_vmem, [*own, *other]), *([state] if has_state else []))


def attend(rand, glob, radius, mine, theirs, own, other, started):
    bf16 = jnp.bfloat16
    return pl.pallas_call(
        attend_kernel,
        out_shape=(jax.ShapeDtypeStruct((512, DH), bf16),) * 2,
        in_specs=[SMEM] * 3 + [HBM] * 2 + [VMEM] * 17,
        out_specs=(HBM, HBM),
        scratch_shapes=[
            pltpu.VMEM((NZ, 2, 2, 512, DH), bf16),
            pltpu.VMEM((2, 512, DH), bf16),
            pltpu.VMEM((2, 512, DH), bf16),
            pltpu.SemaphoreType.DMA((18,)),
        ],
        compiler_params=PARAMS,
        cost_estimate=pl.CostEstimate(flops=14000000000, transcendentals=0, bytes_accessed=28000000),
        name="attend",
    )(rand, glob, radius, mine, theirs, *map(in_vmem, [*own, *other]), started)


def swap(a):
    return lax.ppermute(a, "core", [(0, 1), (1, 0)])


def body(tokens, w_qkv, w_out, rand_blocks, glob_blocks, window_radius):
    bf16 = jnp.bfloat16
    rand = rand_blocks.reshape(-1)
    ids = jnp.pad(rand.astype(bf16)[None], ((0, 15), (0, DH - 48)))
    heads = jax.ShapeDtypeStruct((2, 512, DH), bf16)
    shapes = (jax.ShapeDtypeStruct((512, DH), bf16), heads, jax.ShapeDtypeStruct((528, DH), bf16), heads)
    (mine, own, send_q, send_kv), (ordered, rand) = plane_matmul(
        tokens, w_qkv.transpose(1, 0, 2), split_heads, shapes, "project", (ids,), (order(w_out), rand), False
    )
    own = z_ring(own)
    other = swap(send_kv)
    ordered, _ = lax.optimization_barrier((ordered, other))
    w_cols = lax.all_to_all(ordered, ("y", "x"), 0, 0, tiled=True)
    other = z_ring(other)
    theirs = swap(send_q)
    ids, _ = lax.optimization_barrier((theirs[512:], own[1:3]))
    rand = jnp.concatenate([rand, ids[0, :48].astype(jnp.int32)])
    started = dense(glob_blocks, mine, theirs, own[:5], other[:5])
    own[5], other[6], started, rand = lax.optimization_barrier((own[5], other[6], started, rand))
    started = dense(glob_blocks, mine, theirs, own[5:], other[5:], started)
    own.append(shift(own[5], "z", 1))
    other.append(shift(other[6], "z", -1))
    att = attend(rand, glob_blocks, window_radius, mine, theirs, own, other, started)
    att, w_cols = lax.optimization_barrier((att, w_cols))
    attended = jnp.concatenate([att[0], swap(att[1])], axis=1)
    out = jax.ShapeDtypeStruct((512, 256), bf16)
    return plane_matmul(attended, w_cols[None], round_out, out, "output")[0]


def solution(mesh):
    grid = Mesh(mesh.devices.reshape(NZ, 2, NXY, NXY), ("z", "core", "y", "x"))
    seq, tp = ("z", "core"), ("y", "x")
    return jax.shard_map(
        body,
        mesh=grid,
        in_specs=(P(seq, tp), P(None, None, tp), P(tp, None), P(seq, tp, None), P(), P(tp)),
        out_specs=P(seq, tp),
        check_vma=False,
    )
```

```python
import math

import jax
import jax.numpy as jnp
from jax import lax
from jax.experimental import pallas as pl
from jax.experimental.pallas import tpu as pltpu
from jax.sharding import Mesh, PartitionSpec as P

DH = 128
BLK = 64
NZ = 8
NXY = 4
NEG = -1e30
OFFS = (0, -1, 1, 2)


def shift(a, axis, step):
    n = lax.axis_size(axis)
    return lax.ppermute(a, axis, [(i, (i + step) % n) for i in range(n)])


def around4(a, axis):
    return [shift(a, axis, 1), shift(a, axis, -1), shift(a, axis, 2)]


def plane_matmul(a, w, finish, out_shape, name, more=(), extra=(), halves=True):
    n = a.shape[0] // 2
    w = in_vmem(w)
    others = around4(a[n:], "y")
    by_x = lax.all_to_all(jnp.broadcast_to(a[:n], (NXY, n, 256)).reshape(NXY * n, 256), "x", 0, 0, tiled=True)
    by_x, others = lax.optimization_barrier((by_x, others))
    near = [by_x, jnp.concatenate([a[n:], *others], axis=0)]
    far = [(shift(stack, second, 1), shift(stack, second, -1)) for stack, second in zip(near, "yx")]

    def blocks(v):
        return v.reshape(-1, n, 256)

    sums = partial_matmul((0,), [[blocks(v)] for v in near], w, None, name)
    lows, highs = zip(*far)
    lows, sums, extra = lax.optimization_barrier((lows, sums, extra))
    last = []
    for low, high, second in zip(lows, highs, "yx"):
        if halves:
            last.append((shift(low[: 2 * n], second, 1), shift(high[2 * n :], second, -1)))
        else:
            last.append((shift(low, second, 1),))
    far = list(zip(lows, highs))
    sums = partial_matmul((1, 2), [[blocks(v) for v in f] for f in far], w, sums, name)
    out = partial_matmul((3,), [[blocks(v) for v in f] for f in last], w, sums, name, finish, out_shape, more)
    return out, extra


def partial_kernel(steps, counts, n, groups, has_sums, n_more, finish, *refs):
    n_x = sum(len(c) for c in counts)
    x_refs, w_ref = refs[:n_x], refs[n_x]
    sums_ref = refs[n_x + 1] if has_sums else None
    acc = refs[-1]
    more = refs[n_x + 1 + has_sums : n_x + 1 + has_sums + n_more]
    outs = refs[n_x + 1 + has_sums + n_more : -1]
    y = lax.axis_index("y")
    x = lax.axis_index("x")
    n_steps = len(steps)
    arrays = [[], []]
    i = 0
    for half in range(2):
        for count in counts[half]:
            arrays[half] += [(x_refs[i], j) for j in range(count)]
            i += 1
    acc = acc if finish is not None else outs[0]
    for half in range(2):
        for k, step in enumerate(steps):
            blocks = arrays[half][NXY * k : NXY * (k + 1)]
            rows = jnp.concatenate([ref[j] for ref, j in blocks], axis=1)
            starts = []
            for j in range(NXY):
                if half == 0:
                    owner = lax.rem(y + OFFS[step] + NXY, NXY) * NXY + j
                else:
                    owner = lax.rem(y + OFFS[j] + NXY, NXY) * NXY + lax.rem(x + OFFS[step] + NXY, NXY)
                starts.append(pl.multiple_of(owner * 256, 256))
            span = slice(half * n, (half + 1) * n)

            def column(g, carry, rows=rows, starts=starts, span=span, first=k == 0):
                weights = jnp.concatenate([w_ref[g, pl.ds(start, 256)] for start in starts], axis=0)
                value = jnp.dot(rows, weights, preferred_element_type=jnp.float32)
                if not first:
                    value = acc[g, span] + value
                elif has_sums:
                    value = sums_ref[g, span] + value
                acc[g, span] = value
                return carry

            lax.fori_loop(0, groups, column, 0)
    if finish is not None:
        finish(acc, *more, *outs)


HBM = pl.BlockSpec(memory_space=pltpu.HBM)
VMEM = pl.BlockSpec(memory_space=pltpu.VMEM)
SMEM = pl.BlockSpec(memory_space=pltpu.SMEM)
PARAMS = pltpu.CompilerParams(vmem_limit_bytes=8 * 1024 * 1024)


def in_vmem(a):
    return pltpu.with_memory_space_constraint(a, pltpu.VMEM)


def partial_matmul(steps, halves, w, sums, name, finish=None, out_shape=None, more=()):
    counts = [[v.shape[0] for v in half] for half in halves]
    xs = [v for half in halves for v in half]
    n, groups = xs[0].shape[1], w.shape[0]
    total = jax.ShapeDtypeStruct((groups, 2 * n, 256), jnp.float32)
    has_sums = sums is not None
    operands = [*(xs if finish is None else map(in_vmem, xs)), w] + ([in_vmem(sums)] if has_sums else [])
    return pl.pallas_call(
        lambda *refs: partial_kernel(steps, counts, n, groups, has_sums, len(more), finish, *refs),
        out_shape=total if finish is None else out_shape,
        in_specs=[VMEM] * (len(operands) + len(more)),
        out_specs=VMEM if finish is None else jax.tree.map(lambda _: VMEM, out_shape),
        scratch_shapes=[
            pltpu.VMEM((groups, 2 * n, 256), jnp.float32),
        ],
        compiler_params=PARAMS,
        name=name + str(steps[0]),
    )(*operands, *more)


def split_heads(acc, ids_ref, q_ref, kv_ref, send_q_ref, send_kv_ref):
    first = lax.axis_index("core") == 0
    for g in range(3):
        h0 = acc[g, :, :DH].astype(jnp.bfloat16)
        h1 = acc[g, :, DH:].astype(jnp.bfloat16)
        mine = jnp.where(first, h0, h1)
        other = jnp.where(first, h1, h0)
        if g == 0:
            q_ref[...] = mine
            send_q_ref[:512] = other
        else:
            kv_ref[g - 1] = mine
            send_kv_ref[g - 1] = other
    send_q_ref[512:] = ids_ref[...]


def round_out(acc, o_ref):
    o_ref[...] = acc[0].astype(jnp.bfloat16)


def order_kernel(w_ref, o_ref, sem):
    core = lax.axis_index("core")
    copies = []
    for h in range(2):
        row = pl.multiple_of(lax.rem(core + h, 2) * DH, DH)
        for t in range(16):
            src = w_ref.at[pl.ds(row, DH), pl.ds(t * 256, 256)]
            copies.append(pltpu.make_async_copy(src, o_ref.at[t, pl.ds(h * DH, DH)], sem.at[h, t]))
    for copy in copies:
        copy.start()
    for copy in copies:
        copy.wait()


def order(w_out):
    return pl.pallas_call(
        order_kernel,
        out_shape=jax.ShapeDtypeStruct((16, 256, 256), jnp.bfloat16),
        in_specs=[VMEM],
        out_specs=HBM,
        scratch_shapes=[pltpu.SemaphoreType.DMA((2, 16))],
        compiler_params=PARAMS,
        name="order",
    )(w_out).reshape(4096, 256)


def z_ring(a):
    f1, b1 = shift(a, "z", 1), shift(a, "z", -1)
    f2, b2 = shift(f1, "z", 1), shift(b1, "z", -1)
    return [a, f1, b1, f2, b2, shift(f2, "z", 1), shift(b2, "z", -1)]


SLOTS = (0, 7, 1, 6, 2, 5, 3, 4)


def attend_kernel(*refs):
    rand_ref, glob_ref, radius_ref, mine_ref, theirs_ref = refs[:5]
    rings, dense_ref = (refs[5:13], refs[13:21]), refs[21]
    o_refs = refs[22:24]
    kv_buf, q_buf, o_buf, sem = refs[24:]
    copies = [(mine_ref, q_buf.at[0]), (theirs_ref.at[pl.ds(0, 512)], q_buf.at[1])]
    for side, arrays in enumerate(rings):
        copies += [(array, kv_buf.at[slot, side]) for array, slot in zip(arrays, SLOTS)]
    copies = [pltpu.make_async_copy(src, dst, sem.at[i]) for i, (src, dst) in enumerate(copies)]
    for copy in copies:
        copy.start()
    for copy in copies:
        copy.wait()

    z = lax.axis_index("z")
    core = lax.axis_index("core")
    radius = radius_ref[core]
    scale = 1.0 / math.sqrt(DH)

    def place(block):
        slot = lax.rem(block // 16 - z + NZ, NZ)
        side = lax.rem(block // 8 + core, 2)
        return slot, side, pl.multiple_of(lax.rem(block, 8) * BLK, BLK)

    column = lax.broadcasted_iota(jnp.int32, (BLK, 8 * BLK), 1) // BLK
    nt = (((1,), (1,)), ((), ()))

    def one_block(side, j):
        block = z * 16 + lax.rem(core + side, 2) * 8 + j
        base = side * 48 + (j * 2 + core) * 3
        ids = [jnp.maximum(block - 1, 0), block, jnp.minimum(block + 1, 127)]
        ids += [rand_ref[base + r] for r in range(3)] + [glob_ref[g] for g in range(2)]
        places = [place(i) for i in ids]
        keys = jnp.concatenate([kv_buf[slot, owner, 0, pl.ds(row, BLK)] for slot, owner, row in places], axis=0)
        values = jnp.concatenate([kv_buf[slot, owner, 1, pl.ds(row, BLK)] for slot, owner, row in places], axis=0)
        mine = pl.ds(j * BLK, BLK)
        scores = lax.dot_general(q_buf[side, mine], keys, nt, preferred_element_type=jnp.float32) * scale
        low_off = jnp.where((radius >= 1) & (block > 0), -1, 0)
        high_off = jnp.where((radius >= 1) & (block < 127), -1, 2)
        scores = jnp.where((column == low_off) | (column == high_off), NEG, scores)
        top = jnp.max(scores, axis=1, keepdims=True)
        probs = jnp.exp(scores - top)
        total = jnp.sum(probs, axis=1, keepdims=True)
        acc = jnp.dot(probs.astype(jnp.bfloat16), values, preferred_element_type=jnp.float32)
        o_buf[side, mine] = (acc / total).astype(jnp.bfloat16)

    def eight_blocks(side, carry):
        for j in range(8):
            one_block(side, j)
        return carry

    lax.fori_loop(0, 2, eight_blocks, 0)

    glob, owned, rows_of = owned_globals(glob_ref)

    @pl.when(owned[0] | owned[1])
    def _():
        query = jnp.concatenate([q_buf[side, pl.ds(row, BLK)] for side, row in rows_of], axis=0)
        state = (dense_ref[0], dense_ref[1], dense_ref[2])
        _, total, acc = dense_step(query, kv_buf.at[4], state)
        result = (acc / total).astype(jnp.bfloat16)
        for k, (side, row) in enumerate(rows_of):

            @pl.when(owned[k])
            def _(k=k, side=side, row=row):
                o_buf[side, pl.ds(row, BLK)] = result[k * BLK : (k + 1) * BLK]

    copies = [pltpu.make_async_copy(o_buf.at[side], o_refs[side], sem.at[side]) for side in range(2)]
    for copy in copies:
        copy.start()
    for copy in copies:
        copy.wait()


def owned_globals(glob_ref):
    z = lax.axis_index("z")
    core = lax.axis_index("core")
    glob = [glob_ref[g] for g in range(2)]
    rows_of = [(lax.rem(g // 8 + core, 2), pl.multiple_of(lax.rem(g, 8) * BLK, BLK)) for g in glob]
    return glob, [g // 16 == z for g in glob], rows_of


def dense_step(query, kv_ref, state):
    top, total, acc = state
    keys = jnp.concatenate([kv_ref[0, 0], kv_ref[1, 0]], axis=0)
    values = jnp.concatenate([kv_ref[0, 1], kv_ref[1, 1]], axis=0)
    scores = lax.dot_general(query, keys, (((1,), (1,)), ((), ())), preferred_element_type=jnp.float32)
    scores = scores * (1.0 / math.sqrt(DH))
    new = jnp.maximum(top, jnp.max(scores, axis=1, keepdims=True))
    factor = jnp.exp(top - new)
    probs = jnp.exp(scores - new[:, :1])
    total = total * factor + jnp.sum(probs, axis=1, keepdims=True)
    acc = acc * factor + jnp.dot(probs.astype(jnp.bfloat16), values, preferred_element_type=jnp.float32)
    return new, total, acc


def dense_kernel(n, has_state, *refs):
    glob_ref, mine_ref, theirs_ref = refs[:3]
    rings = refs[3 : 3 + n], refs[3 + n : 3 + 2 * n]
    state_ref = refs[3 + 2 * n]
    o_ref, kv_buf, q_buf, sem = refs[-4:]
    _, owned, rows_of = owned_globals(glob_ref)

    @pl.when(owned[0] | owned[1])
    def _():
        copies = [(mine_ref, q_buf.at[0]), (theirs_ref.at[pl.ds(0, 512)], q_buf.at[1])]
        for side, arrays in enumerate(rings):
            copies += [(array, kv_buf.at[i, side]) for i, array in enumerate(arrays)]
        copies = [pltpu.make_async_copy(src, dst, sem.at[i]) for i, (src, dst) in enumerate(copies)]
        for copy in copies:
            copy.start()
        for copy in copies:
            copy.wait()
        query = jnp.concatenate([q_buf[side, pl.ds(row, BLK)] for side, row in rows_of], axis=0)
        if has_state:
            init = (state_ref[0], state_ref[1], state_ref[2])
        else:
            zeros = jnp.zeros((2 * BLK, DH), jnp.float32)
            init = (zeros + NEG, zeros, zeros)
        state = lax.fori_loop(0, n, lambda i, state: dense_step(query, kv_buf.at[i], state), init)
        for i, value in enumerate(state):
            o_ref[i] = value


def dense(glob, mine, theirs, own, other, state=None):
    bf16 = jnp.bfloat16
    n = len(own)
    has_state = state is not None
    return pl.pallas_call(
        lambda *refs: dense_kernel(n, has_state, *refs),
        out_shape=jax.ShapeDtypeStruct((3, 2 * BLK, DH), jnp.float32),
        in_specs=[SMEM] + [HBM] * 2 + [VMEM] * (2 * n + has_state),
        out_specs=VMEM,
        scratch_shapes=[
            pltpu.VMEM((n, 2, 2, 512, DH), bf16),
            pltpu.VMEM((2, 512, DH), bf16),
            pltpu.SemaphoreType.DMA((2 + 2 * n,)),
        ],
        compiler_params=PARAMS,
        name="dense",
    )(glob, mine, theirs, *map(in_vmem, [*own, *other]), *([state] if has_state else []))


def attend(rand, glob, radius, mine, theirs, own, other, started):
    bf16 = jnp.bfloat16
    return pl.pallas_call(
        attend_kernel,
        out_shape=(jax.ShapeDtypeStruct((512, DH), bf16),) * 2,
        in_specs=[SMEM] * 3 + [HBM] * 2 + [VMEM] * 17,
        out_specs=(HBM, HBM),
        scratch_shapes=[
            pltpu.VMEM((NZ, 2, 2, 512, DH), bf16),
            pltpu.VMEM((2, 512, DH), bf16),
            pltpu.VMEM((2, 512, DH), bf16),
            pltpu.SemaphoreType.DMA((18,)),
        ],
        compiler_params=PARAMS,
        cost_estimate=pl.CostEstimate(flops=14000000000, transcendentals=0, bytes_accessed=28000000),
        name="attend",
    )(rand, glob, radius, mine, theirs, *map(in_vmem, [*own, *other]), started)


def swap(a):
    return lax.ppermute(a, "core", [(0, 1), (1, 0)])


def body(tokens, w_qkv, w_out, rand_blocks, glob_blocks, window_radius):
    bf16 = jnp.bfloat16
    rand = rand_blocks.reshape(-1)
    ids = jnp.pad(rand.astype(bf16)[None], ((0, 15), (0, DH - 48)))
    heads = jax.ShapeDtypeStruct((2, 512, DH), bf16)
    shapes = (jax.ShapeDtypeStruct((512, DH), bf16), heads, jax.ShapeDtypeStruct((528, DH), bf16), heads)
    (mine, own, send_q, send_kv), (ordered, rand) = plane_matmul(
        tokens, w_qkv.transpose(1, 0, 2), split_heads, shapes, "project", (ids,), (order(w_out), rand), False
    )
    own = z_ring(own)
    other = swap(send_kv)
    other = z_ring(other)
    ordered, _ = lax.optimization_barrier((ordered, own[3:5]))
    w_cols = lax.all_to_all(ordered, ("y", "x"), 0, 0, tiled=True)
    theirs = swap(send_q)
    ids, _ = lax.optimization_barrier((theirs[512:], own[1:3]))
    rand = jnp.concatenate([rand, ids[0, :48].astype(jnp.int32)])
    started = dense(glob_blocks, mine, theirs, own[:5], other[:5])
    own[5], other[6], started, rand = lax.optimization_barrier((own[5], other[6], started, rand))
    started = dense(glob_blocks, mine, theirs, own[5:], other[5:], started)
    own.append(shift(own[5], "z", 1))
    other.append(shift(other[6], "z", -1))
    att = attend(rand, glob_blocks, window_radius, mine, theirs, own, other, started)
    att, w_cols = lax.optimization_barrier((att, w_cols))
    attended = jnp.concatenate([att[0], swap(att[1])], axis=1)
    out = jax.ShapeDtypeStruct((512, 256), bf16)
    return plane_matmul(attended, w_cols[None], round_out, out, "output")[0]


def solution(mesh):
    grid = Mesh(mesh.devices.reshape(NZ, 2, NXY, NXY), ("z", "core", "y", "x"))
    seq, tp = ("z", "core"), ("y", "x")
    return jax.shard_map(
        body,
        mesh=grid,
        in_specs=(P(seq, tp), P(None, None, tp), P(tp, None), P(seq, tp, None), P(), P(tp)),
        out_specs=P(seq, tp),
        check_vma=False,
    )
```

```python
import math

import jax
import jax.numpy as jnp
from jax import lax
from jax.experimental import pallas as pl
from jax.experimental.pallas import tpu as pltpu
from jax.sharding import Mesh, PartitionSpec as P

DH = 128
BLK = 64
NZ = 8
NXY = 4
NEG = -1e30
OFFS = (0, -1, 1, 2)


def shift(a, axis, step):
    n = lax.axis_size(axis)
    return lax.ppermute(a, axis, [(i, (i + step) % n) for i in range(n)])


def around4(a, axis):
    return [shift(a, axis, 1), shift(a, axis, -1), shift(a, axis, 2)]


def plane_matmul(a, w, finish, out_shape, name, more=(), extra=(), halves=True):
    n = a.shape[0] // 2
    w = in_vmem(w)
    others = around4(a[n:], "y")
    by_x = lax.all_to_all(jnp.broadcast_to(a[:n], (NXY, n, 256)).reshape(NXY * n, 256), "x", 0, 0, tiled=True)
    by_x, others = lax.optimization_barrier((by_x, others))
    near = [by_x, jnp.concatenate([a[n:], *others], axis=0)]
    far = [(shift(stack, second, 1), shift(stack, second, -1)) for stack, second in zip(near, "yx")]

    def blocks(v):
        return v.reshape(-1, n, 256)

    sums = partial_matmul((0,), [[blocks(v)] for v in near], w, None, name)
    lows, highs = zip(*far)
    lows, sums, extra = lax.optimization_barrier((lows, sums, extra))
    last = []
    for low, high, second in zip(lows, highs, "yx"):
        if halves:
            last.append((shift(low[: 2 * n], second, 1), shift(high[2 * n :], second, -1)))
        else:
            last.append((shift(low, second, 1),))
    far = list(zip(lows, highs))
    sums = partial_matmul((1, 2), [[blocks(v) for v in f] for f in far], w, sums, name)
    out = partial_matmul((3,), [[blocks(v) for v in f] for f in last], w, sums, name, finish, out_shape, more)
    return out, extra


def partial_kernel(steps, counts, n, groups, has_sums, n_more, finish, *refs):
    n_x = sum(len(c) for c in counts)
    x_refs, w_ref = refs[:n_x], refs[n_x]
    sums_ref = refs[n_x + 1] if has_sums else None
    acc = refs[-1]
    more = refs[n_x + 1 + has_sums : n_x + 1 + has_sums + n_more]
    outs = refs[n_x + 1 + has_sums + n_more : -1]
    y = lax.axis_index("y")
    x = lax.axis_index("x")
    n_steps = len(steps)
    arrays = [[], []]
    i = 0
    for half in range(2):
        for count in counts[half]:
            arrays[half] += [(x_refs[i], j) for j in range(count)]
            i += 1
    acc = acc if finish is not None else outs[0]
    for half in range(2):
        for k, step in enumerate(steps):
            blocks = arrays[half][NXY * k : NXY * (k + 1)]
            rows = jnp.concatenate([ref[j] for ref, j in blocks], axis=1)
            starts = []
            for j in range(NXY):
                if half == 0:
                    owner = lax.rem(y + OFFS[step] + NXY, NXY) * NXY + j
                else:
                    owner = lax.rem(y + OFFS[j] + NXY, NXY) * NXY + lax.rem(x + OFFS[step] + NXY, NXY)
                starts.append(pl.multiple_of(owner * 256, 256))
            span = slice(half * n, (half + 1) * n)

            def column(g, carry, rows=rows, starts=starts, span=span, first=k == 0):
                weights = jnp.concatenate([w_ref[g, pl.ds(start, 256)] for start in starts], axis=0)
                value = jnp.dot(rows, weights, preferred_element_type=jnp.float32)
                if not first:
                    value = acc[g, span] + value
                elif has_sums:
                    value = sums_ref[g, span] + value
                acc[g, span] = value
                return carry

            lax.fori_loop(0, groups, column, 0)
    if finish is not None:
        finish(acc, *more, *outs)


HBM = pl.BlockSpec(memory_space=pltpu.HBM)
VMEM = pl.BlockSpec(memory_space=pltpu.VMEM)
SMEM = pl.BlockSpec(memory_space=pltpu.SMEM)
PARAMS = pltpu.CompilerParams(vmem_limit_bytes=8 * 1024 * 1024)


def in_vmem(a):
    return pltpu.with_memory_space_constraint(a, pltpu.VMEM)


def partial_matmul(steps, halves, w, sums, name, finish=None, out_shape=None, more=()):
    counts = [[v.shape[0] for v in half] for half in halves]
    xs = [v for half in halves for v in half]
    n, groups = xs[0].shape[1], w.shape[0]
    total = jax.ShapeDtypeStruct((groups, 2 * n, 256), jnp.float32)
    has_sums = sums is not None
    operands = [*(xs if finish is None else map(in_vmem, xs)), w] + ([in_vmem(sums)] if has_sums else [])
    return pl.pallas_call(
        lambda *refs: partial_kernel(steps, counts, n, groups, has_sums, len(more), finish, *refs),
        out_shape=total if finish is None else out_shape,
        in_specs=[VMEM] * (len(operands) + len(more)),
        out_specs=VMEM if finish is None else jax.tree.map(lambda _: VMEM, out_shape),
        scratch_shapes=[
            pltpu.VMEM((groups, 2 * n, 256), jnp.float32),
        ],
        compiler_params=PARAMS,
        name=name + str(steps[0]),
    )(*operands, *more)


def split_heads(acc, ids_ref, q_ref, kv_ref, send_q_ref, send_kv_ref):
    first = lax.axis_index("core") == 0
    for g in range(3):
        h0 = acc[g, :, :DH].astype(jnp.bfloat16)
        h1 = acc[g, :, DH:].astype(jnp.bfloat16)
        mine = jnp.where(first, h0, h1)
        other = jnp.where(first, h1, h0)
        if g == 0:
            q_ref[...] = mine
            send_q_ref[:512] = other
        else:
            kv_ref[g - 1] = mine
            send_kv_ref[g - 1] = other
    send_q_ref[512:] = ids_ref[...]


def round_out(acc, o_ref):
    o_ref[...] = acc[0].astype(jnp.bfloat16)


def order_kernel(w_ref, o_ref, sem):
    core = lax.axis_index("core")
    copies = []
    for h in range(2):
        row = pl.multiple_of(lax.rem(core + h, 2) * DH, DH)
        for t in range(16):
            src = w_ref.at[pl.ds(row, DH), pl.ds(t * 256, 256)]
            copies.append(pltpu.make_async_copy(src, o_ref.at[t, pl.ds(h * DH, DH)], sem.at[h, t]))
    for copy in copies:
        copy.start()
    for copy in copies:
        copy.wait()


def order(w_out):
    return pl.pallas_call(
        order_kernel,
        out_shape=jax.ShapeDtypeStruct((16, 256, 256), jnp.bfloat16),
        in_specs=[VMEM],
        out_specs=HBM,
        scratch_shapes=[pltpu.SemaphoreType.DMA((2, 16))],
        compiler_params=PARAMS,
        name="order",
    )(w_out).reshape(4096, 256)


def z_ring(a):
    f1, b1 = shift(a, "z", 1), shift(a, "z", -1)
    f2, b2 = shift(f1, "z", 1), shift(b1, "z", -1)
    return [a, f1, b1, f2, b2, shift(f2, "z", 1), shift(b2, "z", -1)]


SLOTS = (0, 7, 1, 6, 2, 5, 3, 4)


def attend_kernel(*refs):
    rand_ref, glob_ref, radius_ref, mine_ref, theirs_ref = refs[:5]
    rings, dense_ref = (refs[5:13], refs[13:21]), refs[21]
    o_refs = refs[22:24]
    kv_buf, q_buf, o_buf, sem = refs[24:]
    copies = [(mine_ref, q_buf.at[0]), (theirs_ref.at[pl.ds(0, 512)], q_buf.at[1])]
    for side, arrays in enumerate(rings):
        copies += [(array, kv_buf.at[slot, side]) for array, slot in zip(arrays, SLOTS)]
    copies = [pltpu.make_async_copy(src, dst, sem.at[i]) for i, (src, dst) in enumerate(copies)]
    for copy in copies:
        copy.start()
    for copy in copies:
        copy.wait()

    z = lax.axis_index("z")
    core = lax.axis_index("core")
    radius = radius_ref[core]
    scale = 1.0 / math.sqrt(DH)

    def place(block):
        slot = lax.rem(block // 16 - z + NZ, NZ)
        side = lax.rem(block // 8 + core, 2)
        return slot, side, pl.multiple_of(lax.rem(block, 8) * BLK, BLK)

    column = lax.broadcasted_iota(jnp.int32, (BLK, 8 * BLK), 1) // BLK
    nt = (((1,), (1,)), ((), ()))

    def one_block(side, j):
        block = z * 16 + lax.rem(core + side, 2) * 8 + j
        base = side * 48 + (j * 2 + core) * 3
        ids = [jnp.maximum(block - 1, 0), block, jnp.minimum(block + 1, 127)]
        ids += [rand_ref[base + r] for r in range(3)] + [glob_ref[g] for g in range(2)]
        places = [place(i) for i in ids]
        keys = jnp.concatenate([kv_buf[slot, owner, 0, pl.ds(row, BLK)] for slot, owner, row in places], axis=0)
        values = jnp.concatenate([kv_buf[slot, owner, 1, pl.ds(row, BLK)] for slot, owner, row in places], axis=0)
        mine = pl.ds(j * BLK, BLK)
        scores = lax.dot_general(q_buf[side, mine], keys, nt, preferred_element_type=jnp.float32) * scale
        low_off = jnp.where((radius >= 1) & (block > 0), -1, 0)
        high_off = jnp.where((radius >= 1) & (block < 127), -1, 2)
        scores = jnp.where((column == low_off) | (column == high_off), NEG, scores)
        top = jnp.max(scores, axis=1, keepdims=True)
        probs = jnp.exp(scores - top)
        total = jnp.sum(probs, axis=1, keepdims=True)
        acc = jnp.dot(probs.astype(jnp.bfloat16), values, preferred_element_type=jnp.float32)
        o_buf[side, mine] = (acc / total).astype(jnp.bfloat16)

    def eight_blocks(side, carry):
        for j in range(8):
            one_block(side, j)
        return carry

    lax.fori_loop(0, 2, eight_blocks, 0)

    glob, owned, rows_of = owned_globals(glob_ref)

    @pl.when(owned[0] | owned[1])
    def _():
        query = jnp.concatenate([q_buf[side, pl.ds(row, BLK)] for side, row in rows_of], axis=0)
        state = (dense_ref[0], dense_ref[1], dense_ref[2])
        _, total, acc = dense_step(query, kv_buf.at[4], state)
        result = (acc / total).astype(jnp.bfloat16)
        for k, (side, row) in enumerate(rows_of):

            @pl.when(owned[k])
            def _(k=k, side=side, row=row):
                o_buf[side, pl.ds(row, BLK)] = result[k * BLK : (k + 1) * BLK]

    copies = [pltpu.make_async_copy(o_buf.at[side], o_refs[side], sem.at[side]) for side in range(2)]
    for copy in copies:
        copy.start()
    for copy in copies:
        copy.wait()


def owned_globals(glob_ref):
    z = lax.axis_index("z")
    core = lax.axis_index("core")
    glob = [glob_ref[g] for g in range(2)]
    rows_of = [(lax.rem(g // 8 + core, 2), pl.multiple_of(lax.rem(g, 8) * BLK, BLK)) for g in glob]
    return glob, [g // 16 == z for g in glob], rows_of


def dense_step(query, kv_ref, state):
    top, total, acc = state
    keys = jnp.concatenate([kv_ref[0, 0], kv_ref[1, 0]], axis=0)
    values = jnp.concatenate([kv_ref[0, 1], kv_ref[1, 1]], axis=0)
    scores = lax.dot_general(query, keys, (((1,), (1,)), ((), ())), preferred_element_type=jnp.float32)
    scores = scores * (1.0 / math.sqrt(DH))
    new = jnp.maximum(top, jnp.max(scores, axis=1, keepdims=True))
    factor = jnp.exp(top - new)
    probs = jnp.exp(scores - new[:, :1])
    total = total * factor + jnp.sum(probs, axis=1, keepdims=True)
    acc = acc * factor + jnp.dot(probs.astype(jnp.bfloat16), values, preferred_element_type=jnp.float32)
    return new, total, acc


def dense_kernel(n, has_state, *refs):
    glob_ref, mine_ref, theirs_ref = refs[:3]
    rings = refs[3 : 3 + n], refs[3 + n : 3 + 2 * n]
    state_ref = refs[3 + 2 * n]
    o_ref, kv_buf, q_buf, sem = refs[-4:]
    _, owned, rows_of = owned_globals(glob_ref)

    @pl.when(owned[0] | owned[1])
    def _():
        copies = [(mine_ref, q_buf.at[0]), (theirs_ref.at[pl.ds(0, 512)], q_buf.at[1])]
        for side, arrays in enumerate(rings):
            copies += [(array, kv_buf.at[i, side]) for i, array in enumerate(arrays)]
        copies = [pltpu.make_async_copy(src, dst, sem.at[i]) for i, (src, dst) in enumerate(copies)]
        for copy in copies:
            copy.start()
        for copy in copies:
            copy.wait()
        query = jnp.concatenate([q_buf[side, pl.ds(row, BLK)] for side, row in rows_of], axis=0)
        if has_state:
            init = (state_ref[0], state_ref[1], state_ref[2])
        else:
            zeros = jnp.zeros((2 * BLK, DH), jnp.float32)
            init = (zeros + NEG, zeros, zeros)
        state = lax.fori_loop(0, n, lambda i, state: dense_step(query, kv_buf.at[i], state), init)
        for i, value in enumerate(state):
            o_ref[i] = value


def dense(glob, mine, theirs, own, other, state=None):
    bf16 = jnp.bfloat16
    n = len(own)
    has_state = state is not None
    return pl.pallas_call(
        lambda *refs: dense_kernel(n, has_state, *refs),
        out_shape=jax.ShapeDtypeStruct((3, 2 * BLK, DH), jnp.float32),
        in_specs=[SMEM] + [HBM] * 2 + [VMEM] * (2 * n + has_state),
        out_specs=VMEM,
        scratch_shapes=[
            pltpu.VMEM((n, 2, 2, 512, DH), bf16),
            pltpu.VMEM((2, 512, DH), bf16),
            pltpu.SemaphoreType.DMA((2 + 2 * n,)),
        ],
        compiler_params=PARAMS,
        name="dense",
    )(glob, mine, theirs, *map(in_vmem, [*own, *other]), *([state] if has_state else []))


def attend(rand, glob, radius, mine, theirs, own, other, started):
    bf16 = jnp.bfloat16
    return pl.pallas_call(
        attend_kernel,
        out_shape=(jax.ShapeDtypeStruct((512, DH), bf16),) * 2,
        in_specs=[SMEM] * 3 + [HBM] * 2 + [VMEM] * 17,
        out_specs=(HBM, HBM),
        scratch_shapes=[
            pltpu.VMEM((NZ, 2, 2, 512, DH), bf16),
            pltpu.VMEM((2, 512, DH), bf16),
            pltpu.VMEM((2, 512, DH), bf16),
            pltpu.SemaphoreType.DMA((18,)),
        ],
        compiler_params=PARAMS,
        cost_estimate=pl.CostEstimate(flops=14000000000, transcendentals=0, bytes_accessed=28000000),
        name="attend",
    )(rand, glob, radius, mine, theirs, *map(in_vmem, [*own, *other]), started)


def swap(a):
    return lax.ppermute(a, "core", [(0, 1), (1, 0)])


def body(tokens, w_qkv, w_out, rand_blocks, glob_blocks, window_radius):
    bf16 = jnp.bfloat16
    rand = rand_blocks.reshape(-1)
    ids = jnp.pad(rand.astype(bf16)[None], ((0, 15), (0, DH - 48)))
    heads = jax.ShapeDtypeStruct((2, 512, DH), bf16)
    shapes = (jax.ShapeDtypeStruct((512, DH), bf16), heads, jax.ShapeDtypeStruct((528, DH), bf16), heads)
    (mine, own, send_q, send_kv), (ordered, rand) = plane_matmul(
        tokens, w_qkv.transpose(1, 0, 2), split_heads, shapes, "project", (ids,), (order(w_out), rand), False
    )
    own = z_ring(own)
    other = swap(send_kv)
    other = z_ring(other)
    ordered, _ = lax.optimization_barrier((ordered, other[1:3]))
    w_cols = lax.all_to_all(ordered, ("y", "x"), 0, 0, tiled=True)
    theirs = swap(send_q)
    ids, _ = lax.optimization_barrier((theirs[512:], own[1:3]))
    rand = jnp.concatenate([rand, ids[0, :48].astype(jnp.int32)])
    started = dense(glob_blocks, mine, theirs, own[:5], other[:5])
    own[5], other[6], started, rand = lax.optimization_barrier((own[5], other[6], started, rand))
    started = dense(glob_blocks, mine, theirs, own[5:], other[5:], started)
    own.append(shift(own[5], "z", 1))
    other.append(shift(other[6], "z", -1))
    att = attend(rand, glob_blocks, window_radius, mine, theirs, own, other, started)
    att, w_cols = lax.optimization_barrier((att, w_cols))
    attended = jnp.concatenate([att[0], swap(att[1])], axis=1)
    out = jax.ShapeDtypeStruct((512, 256), bf16)
    return plane_matmul(attended, w_cols[None], round_out, out, "output")[0]


def solution(mesh):
    grid = Mesh(mesh.devices.reshape(NZ, 2, NXY, NXY), ("z", "core", "y", "x"))
    seq, tp = ("z", "core"), ("y", "x")
    return jax.shard_map(
        body,
        mesh=grid,
        in_specs=(P(seq, tp), P(None, None, tp), P(tp, None), P(seq, tp, None), P(), P(tp)),
        out_specs=P(seq, tp),
        check_vma=False,
    )
```
